32 devices in a mesh: dp: 16 (over z, y, core), tensor: 2 (over x).
Axes of the slice: x: 2, y: 2, z: 4, core: 2. Of those that a mesh axis runs over, the one named last changes fastest.
Arguments:
- inputs: bfloat16 [16, 1024, 768], P('dp', 'tensor'), may hold values from -6 to 6
- prev_logits: float32 [16, 1024, 12], P('dp', 'tensor'), may hold values from -6 to 6
- routes: int32 [16, 1024, 2], P('dp'), may hold values from 0 to 11, all different within a row; in each aligned block of 1024 rows (0 to 1023, 1024 to 2047, ..., all dimensions but the last counted through in order) at most 256 rows name the same one
- lengths: int32 [16], P('dp'), may hold values from 256 to 1024, as said below
- cotangent: bfloat16 [16, 1024, 768], P('dp', 'tensor'), may hold values from -6 to 6
- attn_gain: float32 [768], replicated, may hold values from 0.25 to 1.75
- w_qkv: float32 [768, 3, 768], P('dp', None, 'tensor'), may hold values from -0.21875 to 0.21875
- w_out: float32 [768, 768], P('dp', 'tensor'), may hold values from -1.75 to 1.75
- moe_gain: float32 [768], replicated, may hold values from 0.25 to 1.75
- w_router: float32 [768, 12], replicated, may hold values from -0.21875 to 0.21875
- w_resid: float32 [12, 12], replicated, may hold values from -1.75 to 1.75
- const_mix: float32 [2, 2, 768], replicated, may hold values from -0.21875 to 0.21875
- const_vec: float32 [2, 768], replicated, may hold values from -6 to 6
- w_experts: float32 [768, 8, 3, 2048], P('dp', None, None, 'tensor'), may hold values from -0.21875 to 0.21875
Outputs:
- block_out: bfloat16 [16, 1024, 768], P('dp', 'tensor')
- grad_inputs: bfloat16 [16, 1024, 768], P('dp', 'tensor')
- grad_prev: float32 [16, 1024, 12], P('dp', 'tensor')
- grad_attn_gain: float32 [768], replicated
- grad_qkv: float32 [768, 3, 768], P('dp', None, 'tensor')
- grad_out: float32 [768, 768], P('dp', 'tensor')
- grad_moe_gain: float32 [768], replicated
- grad_router: float32 [768, 12], replicated
- grad_resid: float32 [12, 12], replicated
- grad_const_mix: float32 [2, 2, 768], replicated
- grad_const_vec: float32 [2, 768], replicated
- grad_experts: float32 [768, 8, 3, 2048], P('dp', None, None, 'tensor')
The draws below stay inside these ranges and needn't reach their ends.
Inputs may be any that keep to these rules, and one draw needn't show every extreme that they name: `routes`: within one slot no expert is named by more than 256 positions, and the two experts of a position differ. `lengths`: positions at or beyond a slot's length are padding.
All inputs are finite; a program needn't handle non-finite values.
Results may differ from the reference program's by a relative error of at most 0.017.
The reference program's roundings to bfloat16 on the way count: a program that leaves them out, or rounds other values in their place, can miss the bound.
Values may be sent and summed in bfloat16 or wider, within the bound.
No kernel may reach another device: no remote copies, remote signals or barrier semaphores. Data moves between devices by JAX's collectives and lax.ppermute only.
A program may use at most 384 MiB of HBM per device.

```python
import math
import jax
import jax.numpy as jnp
import numpy as np
from jax import lax

D = 768
HEAD_DIM = 64
HEADS = 12
FF = 2048
FFN_EXPERTS = 8
EXPERTS = 12
LEN = 1024
CAP = 256
SLOTS = 16


def draw_lengths(key, part):
    key_one, key_two = jax.random.split(jax.random.fold_in(key, 17))
    length_draw = jax.random.randint(key_one, (SLOTS,), LEN // 4, LEN + 1)
    chosen_slot = jax.random.randint(key_two, (), 0, SLOTS)
    return length_draw.at[chosen_slot].set(LEN).astype(jnp.int32)


def block_levels(rng, extent, pieces, low, high):
    factor_of, own = 1.0, jax.random.fold_in(rng, 6)
    for position, blocks in pieces:
        heights = jnp.exp(jax.random.uniform(jax.random.fold_in(own, position), (blocks,), jnp.float32, low / len(pieces), high / len(pieces)))
        factor_of = factor_of * jnp.repeat(heights, extent[position] // blocks).reshape([-1 if axis == position else 1 for axis in range(len(extent))])
    return factor_of


def routed_block(own_key, own, number, rows, count, top, most, slope):
    ranking = jax.random.permutation(own_key, count)
    crowded, common = portions_of(count, rows * top, most, slope, True), portions_of(count, rows * top, most, slope, False)
    places = jnp.arange(count)

    def named(sizes, turn):
        used = int((sizes > 0).sum())
        fixed = max(1, used // 4)
        passed = fixed + (places - fixed + turn * (used - fixed)) % max(1, count - fixed)
        return jnp.zeros((count,), jnp.int32).at[ranking[jnp.where(places < fixed, places, passed)]].set(jnp.asarray(sizes, jnp.int32))

    sizes = jnp.where(number % 4 == 0, named(crowded, number // 4), named(common, number - number // 4 - 1))
    mixed = jax.random.permutation(jax.random.fold_in(own, 3), count)
    giver, sink = mixed[0:count // 2 * 2:2], mixed[1:count // 2 * 2:2]
    room = jnp.minimum(sizes[giver] - 1, most - sizes[sink]) // 2
    room = jnp.where((giver == ranking[0]) | (sink == ranking[0]) | (sizes[sink] == 0), 0, jnp.maximum(room, 0))
    passed = jax.random.randint(jax.random.fold_in(own, 4), (count // 2,), 0, 1 << 20) % (room + 1)
    sizes = sizes.at[giver].add(-passed).at[sink].add(passed)
    items = jnp.searchsorted(jnp.cumsum(sizes), jnp.arange(rows * top), side="right").astype(jnp.int32)
    listing = items.reshape(top, rows).T
    listing = listing[jax.random.permutation(jax.random.fold_in(own, 1), rows)]
    turn = jax.random.randint(jax.random.fold_in(own, 2), (rows, 1), 0, top)
    return jnp.take_along_axis(listing, (jnp.arange(top)[None, :] + turn) % top, axis=1)


def portions_of(amount, total, bound, slope, full):
    loads = [(1 << 20) // math.isqrt(grade ** slope) + 1 for grade in range(1, amount + 1)]
    largest = bound if full else min(bound, max(-(-total // amount), total * loads[0] // sum(loads)))
    least = 1 if total - largest >= amount - 1 else 0
    given, spare = [largest] + [least] * (amount - 1), total - largest - least * (amount - 1)
    while spare > 0:
        candidates = [i for i in range(1, amount) if given[i] < largest] or [i for i in range(1, amount) if given[i] < bound]
        pool, budget = sum([loads[i] for i in candidates]), spare
        for i in candidates:
            more = min(bound - given[i], max(1, budget * loads[i] // pool), spare)
            given[i] = given[i] + more
            spare = spare - more
    return np.array(given)


def gaussian(rng, dims, spread, most, cuts=(), held_as=jnp.bfloat16):
    values = jax.random.normal(rng, dims, jnp.float32) * spread
    if len(cuts) > 0:
        values = block_levels(rng, dims, cuts, -0.22, 0.18) * values
    return jnp.clip(values, min=-most, max=most).astype(held_as)


def setup_inputs(seed: int = 0) -> dict:
    splits = jax.random.split(jax.random.key(seed), 15)
    inputs = gaussian(splits[0], (SLOTS, LEN, D), 1.0, 6.0, ((0, 16), (1, 2)))
    prev_logits = gaussian(splits[1], (SLOTS, LEN, EXPERTS), 1.0, 6.0, ((0, 16), (1, 2)), jnp.float32)
    routes_keys = jax.random.split(jax.random.fold_in(splits[2], 1), SLOTS * LEN // LEN)
    routes_turns = jax.random.permutation(jax.random.fold_in(splits[2], 3), SLOTS * LEN // LEN)
    routes = jax.vmap(lambda own, number: routed_block(jax.random.fold_in(splits[2], 2), own, number, LEN, EXPERTS, 2, CAP, 1))(routes_keys, routes_turns).reshape((SLOTS, LEN, 2))
    lengths = draw_lengths(jax.random.fold_in(splits[14], 71), 0)
    cotangent = gaussian(splits[4], (SLOTS, LEN, D), 1.0, 6.0, ((0, 16), (1, 2)))
    attn_gain = jnp.clip(1.0 + 0.15 * jax.random.normal(splits[5], (D,), jnp.float32), 0.25, 1.75)
    w_qkv = gaussian(splits[6], (D, 3, D), D ** -0.5, 0.21875, ((0, 16), (2, 2)), jnp.float32)
    w_out = gaussian(splits[7], (D, D), (D // 64) ** -0.5, 1.75, ((0, 16), (1, 2)), jnp.float32)
    moe_gain = jnp.clip(1.0 + 0.15 * jax.random.normal(splits[8], (D,), jnp.float32), 0.25, 1.75)
    w_router = gaussian(splits[9], (D, EXPERTS), D ** -0.5, 0.21875, (), jnp.float32)
    w_resid = gaussian(splits[10], (EXPERTS, EXPERTS), EXPERTS ** -0.5, 1.75, (), jnp.float32)
    const_mix = gaussian(splits[11], (2, 2, D), D ** -0.5, 0.21875, (), jnp.float32)
    const_vec = gaussian(splits[12], (2, D), 1.0, 6.0, (), jnp.float32)
    w_experts = gaussian(splits[13], (D, FFN_EXPERTS, 3, FF), D ** -0.5, 0.21875, ((0, 16), (3, 2)), jnp.float32)
    return {"inputs": inputs, "prev_logits": prev_logits, "routes": routes, "lengths": lengths, "cotangent": cotangent, "attn_gain": attn_gain, "w_qkv": w_qkv, "w_out": w_out, "moe_gain": moe_gain, "w_router": w_router, "w_resid": w_resid, "const_mix": const_mix, "const_vec": const_vec, "w_experts": w_experts}


EPS = 1e-05
THETA = 10000.0
HIGHEST = lax.Precision.HIGHEST

@jax.custom_vjp
def low(v):
    return lax.optimization_barrier(v.astype(jnp.bfloat16)).astype(jnp.float32)

@jax.custom_vjp
def low_back(v):
    return v

def low_keep(v):
    return (low(v), None)

def low_pass(kept, grad):
    return (grad,)

def back_keep(v):
    return (v, None)

def back_low(kept, grad):
    return (low(grad),)
low.defvjp(low_keep, low_pass)
low_back.defvjp(back_keep, back_low)

def rms_norm(values, gain):
    return values * lax.rsqrt(lax.optimization_barrier(jnp.mean(values * values, axis=-1, keepdims=True)) + EPS) * gain

def rotate(values):
    length, head_count, head_width = values.shape
    half_width = head_width // 2
    inv_freq = THETA ** (-jnp.arange(half_width, dtype=jnp.float32) / half_width)
    angles = jnp.arange(length, dtype=jnp.float32)[:, None] * inv_freq[None, :]
    cosine = jnp.cos(angles)[:, None, :]
    sine_val = jnp.sin(angles)[:, None, :]
    lower_half = values[..., :half_width]
    upper_half = values[..., half_width:]
    return jnp.concatenate([lower_half * cosine - upper_half * sine_val, upper_half * cosine + lower_half * sine_val], axis=-1)

def normalize(scores):
    row_max = lax.optimization_barrier(jnp.max(scores, axis=-1, keepdims=True))
    exp_rows = jnp.exp(scores - row_max)
    return exp_rows / lax.optimization_barrier(jnp.sum(exp_rows, axis=-1, keepdims=True))

def dispatch(route_rows, expert_count, capacity):
    flat_routes = route_rows.reshape(-1).astype(jnp.int32)
    pair_count = flat_routes.shape[0]
    sort_keys = flat_routes * pair_count + jnp.arange(pair_count, dtype=jnp.int32)
    sort_order = jnp.argsort(sort_keys).astype(jnp.int32)
    labels = jnp.arange(expert_count, dtype=jnp.int32)
    counts = lax.optimization_barrier(jnp.sum((flat_routes[None, :] == labels[:, None]).astype(jnp.int32), axis=1))
    starts = jnp.cumsum(counts) - counts
    places = jnp.arange(capacity, dtype=jnp.int32)
    slot_valid = places[None, :] < counts[:, None]
    slot_pos = jnp.minimum(starts[:, None] + places[None, :], pair_count - 1)
    slot_index = jnp.where(slot_valid, sort_order[slot_pos], 0).astype(jnp.int32)
    return (slot_index, slot_valid)

def slot_forward(slot_in, slot_prev, slot_routes, slot_length, gain_one, qkv_w, out_w, gain_two, router_w, resid_w, mix_w, vec_w, expert_w):
    length, model_width = slot_in.shape
    scale = HEAD_DIM ** (-0.5)
    attn_in = low(rms_norm(slot_in, gain_one))
    projected = low_back(jnp.einsum('td,dkh->tkh', attn_in, qkv_w, precision=HIGHEST))
    head_shape = (length, HEADS, HEAD_DIM)
    query_rows = low(rotate(projected[:, 0].reshape(head_shape)))
    key_rows = low(rotate(projected[:, 1].reshape(head_shape)))
    value_rows = low(projected[:, 2].reshape(head_shape))
    scores = low_back(jnp.einsum('qhd,khd->hqk', query_rows, key_rows, precision=HIGHEST) * scale)
    places = jnp.arange(length, dtype=jnp.int32)
    allowed = (places[None, :] <= places[:, None]) & (places[None, :] < slot_length)
    scores = jnp.where(allowed[None], scores, -jnp.inf)
    prob_rows = low(normalize(scores))
    attended = jnp.einsum('hqk,khd->qhd', prob_rows, value_rows, precision=HIGHEST).reshape(length, model_width)
    attended = low(low_back(attended))
    attn_mixed = low_back(jnp.dot(attended, out_w.T, precision=HIGHEST))
    resid_mid = slot_in + attn_mixed
    normed = rms_norm(resid_mid, gain_two)
    moe_in = low(normed)
    slot_index, slot_valid = dispatch(slot_routes, FFN_EXPERTS, CAP)
    token_of = slot_index // 2
    buffered = moe_in[token_of]
    gate_up = low_back(jnp.einsum('ecd,dekf->eckf', buffered, expert_w[:, :, :2], precision=HIGHEST))
    gate_pre = gate_up[:, :, 0]
    up_pre = gate_up[:, :, 1]
    activated = low(gate_pre * jax.nn.sigmoid(gate_pre) * up_pre)
    result = low_back(jnp.einsum('ecf,def->ecd', activated, expert_w[:, :, 2], precision=HIGHEST))
    result = result * slot_valid[..., None].astype(jnp.float32)
    routed = jnp.zeros((2 * length, model_width), jnp.float32).at[slot_index.reshape(-1)].add(result.reshape(-1, model_width))
    routed = routed.reshape(length, 2, model_width)
    logits = jnp.dot(normed, router_w, precision=HIGHEST) + jnp.dot(slot_prev, resid_w, precision=HIGHEST)
    labels = jnp.arange(EXPERTS, dtype=jnp.int32)
    route_onehot = (slot_routes[:, :, None] == labels[None, None, :]).astype(jnp.float32)
    chosen = lax.optimization_barrier(jnp.sum(route_onehot * logits[:, None, :], axis=-1))
    gate_weight = normalize(chosen)
    mix_weight = normalize(jnp.einsum('td,jid->tji', normed, mix_w, precision=HIGHEST))
    constant = mix_weight[:, :, 0:1] * normed[:, None, :] + mix_weight[:, :, 1:2] * vec_w[None]
    is_copy = route_onehot[:, :, FFN_EXPERTS + 1][..., None]
    is_first = route_onehot[:, :, FFN_EXPERTS + 2][..., None]
    is_second = route_onehot[:, :, FFN_EXPERTS + 3][..., None]
    expert_out = routed + is_copy * normed[:, None, :] + is_first * constant[:, None, 0] + is_second * constant[:, None, 1]
    moe_sum = lax.optimization_barrier(jnp.sum(gate_weight[..., None] * expert_out, axis=1))
    return resid_mid + moe_sum

def reference(inputs, prev_logits, routes, lengths, cotangent, attn_gain, w_qkv, w_out, moe_gain, w_router, w_resid, const_mix, const_vec, w_experts):

    def forward(resid_in, prev_in, gain_one, qkv_w, out_w, gain_two, router_w, resid_w, mix_w, vec_w, expert_w):
        qkv_low = low(qkv_w)
        out_low = low(out_w)
        expert_low = low(expert_w)

        def one_slot(carry, slot_item):
            slot_in, slot_prev, slot_routes, slot_length = slot_item
            return (carry, slot_forward(slot_in, slot_prev, slot_routes, slot_length, gain_one, qkv_low, out_low, gain_two, router_w, resid_w, mix_w, vec_w, expert_low))
        carry_out, outputs = lax.scan(jax.checkpoint(one_slot), jnp.zeros((), jnp.float32), (resid_in, prev_in, routes, lengths))
        return outputs
    primals = (inputs.astype(jnp.float32), prev_logits, attn_gain, w_qkv, w_out, moe_gain, w_router, w_resid, const_mix, const_vec, w_experts)
    block_out, pullback = jax.vjp(forward, *primals)
    places = jnp.arange(inputs.shape[1], dtype=jnp.int32)
    live_mask = (places[None, :] < lengths[:, None]).astype(jnp.float32)
    grads = pullback(cotangent.astype(jnp.float32) * live_mask[..., None])
    return (block_out.astype(jnp.bfloat16), grads[0].astype(jnp.bfloat16), grads[1], grads[2], grads[3], grads[4], grads[5], grads[6], grads[7], grads[8], grads[9], grads[10])
```

```python
import functools

import jax
import jax.numpy as jnp
from jax import lax
from jax.experimental import pallas as pl
from jax.experimental.pallas import tpu as pltpu
from jax.sharding import PartitionSpec as P

HEAD_DIM = 64
FFN_EXPERTS = 8
EXPERTS = 12
CAP = 256
EPS = 1e-05
THETA = 10000.0
HIGHEST = lax.Precision.HIGHEST
BF = jnp.bfloat16
F32 = jnp.float32
NEG = float("-inf")
MIB = 1 << 20
SPLIT = FFN_EXPERTS // 2
EXTRA = 128


def params(mib):
    return pltpu.CompilerParams(vmem_limit_bytes=mib * MIB)


def mm(a, b):
    return jnp.dot(a, b, preferred_element_type=F32)


def mm_nt(a, b):
    return lax.dot_general(a, b, (((1,), (1,)), ((), ())), preferred_element_type=F32)


def mm_tn(a, b):
    return lax.dot_general(a, b, (((0,), (0,)), ((), ())), preferred_element_type=F32)


def full_spec(shape):
    zeros = (0,) * len(shape)
    return pl.BlockSpec(shape, lambda *ids: zeros)


def swap_x(value):
    return lax.ppermute(value, "tensor", [(0, 1), (1, 0)])


def swap_dp(value, count, bit):
    return lax.ppermute(value, "dp", [(i, i ^ bit) for i in range(count)])


def pick(blocks, index):
    return lax.dynamic_index_in_dim(blocks, index, 0, keepdims=False)


def add_low(*terms):
    total = terms[0].astype(F32)
    for term in terms[1:]:
        total = total + term.astype(F32)
    return total


def scatter_line(blocks, count, stride, place):
    length = blocks.shape[0]
    while length > 4:
        half = length // 2
        top = place // half
        pair = blocks.reshape((2, half) + blocks.shape[1:])
        got = swap_dp(pick(pair, 1 - top), count, half * stride)
        blocks = add_low(pick(pair, top), got).astype(BF)
        place = place % half
        length = half
    if length == 1:
        return blocks[0].astype(F32)
    member = [(i // stride) % length for i in range(count)]
    upward = downward = None
    for step in range(length - 1):
        high = jnp.minimum(length - 1 - step + place, length - 1)
        low = jnp.maximum(step - (length - 1) + place, 0)
        send_up, send_down = pick(blocks, high), pick(blocks, low)
        if step > 0:
            send_up = add_low(send_up, upward).astype(BF)
            send_down = add_low(send_down, downward).astype(BF)
        upward = lax.ppermute(
            send_up, "dp", [(i, i + stride) for i in range(count) if member[i] <= step and member[i] < length - 1]
        )
        downward = lax.ppermute(
            send_down, "dp", [(i, i - stride) for i in range(count) if member[i] >= length - 1 - step and member[i] > 0]
        )
    return add_low(pick(blocks, place), upward, downward)


def sum_all(value, count):
    value = value + swap_x(value)
    bit = 1
    while bit < count:
        value = value + swap_dp(value, count, bit)
        bit *= 2
    return value


def turn(values, cosine, sine):
    lane = lax.broadcasted_iota(jnp.int32, values.shape, 1)
    other = jnp.where(lane % HEAD_DIM < HEAD_DIM // 2, pltpu.roll(values, 96, 1), pltpu.roll(values, 32, 1))
    return values * cosine + other * sine


def qkv_kernel(x_ref, gain_ref, w_ref, cos_ref, sin_ref, attn_ref, q_ref, k_ref, v_ref):
    values = x_ref[...].astype(F32)
    inverse = lax.rsqrt(jnp.mean(values * values, axis=-1, keepdims=True) + EPS)
    attn = (values * inverse * gain_ref[...]).astype(BF)
    attn_ref[...] = attn
    width = q_ref.shape[1]
    for part, out in enumerate((q_ref, k_ref, v_ref)):
        weight = w_ref[:, part].reshape(values.shape[1], width)
        rows = mm(attn, weight)
        if part == 2:
            out[...] = rows.astype(BF)
            continue
        for start in range(0, width, 128):
            turned = turn(rows[:, start : start + 128], cos_ref[...], sin_ref[...]).astype(BF)
            if part == 0:
                turned = turned * BF(HEAD_DIM ** -0.5)
            out[:, start : start + 128] = turned


def project(rows, gain, weight, cosine, sine):
    length, width = rows.shape
    heads = weight.shape[-1]
    block = 256
    row_spec = lambda n: pl.BlockSpec((block, n), lambda i: (i, 0))
    return pl.pallas_call(
        qkv_kernel,
        grid=(length // block,),
        in_specs=[
            row_spec(width),
            full_spec((1, width)),
            full_spec(weight.shape),
            row_spec(128),
            row_spec(128),
        ],
        out_specs=[row_spec(width), row_spec(heads), row_spec(heads), row_spec(heads)],
        out_shape=[jax.ShapeDtypeStruct((length, width), BF)] + [jax.ShapeDtypeStruct((length, heads), BF)] * 3,
        compiler_params=params(40),
        name="project",
    )(rows, gain, weight, cosine, sine)


BLOCK = 256


def head_scores(query, k_ref, bias_ref, index):
    row = lax.broadcasted_iota(jnp.int32, (BLOCK, BLOCK), 0)
    column = lax.broadcasted_iota(jnp.int32, (BLOCK, BLOCK), 1)
    parts = []
    for block in range(index + 1):
        span = pl.ds(block * BLOCK, BLOCK)
        scores = mm_nt(query, k_ref[span, :]) + bias_ref[:, span]
        if block == index:
            scores = jnp.where(column <= row, scores, NEG)
        parts.append(scores)
    return parts


def attend_kernel(q_ref, k_ref, v_ref, bias_ref, o_ref, lse_ref):
    length = q_ref.shape[0]
    lane = lax.broadcasted_iota(jnp.int32, (BLOCK, 128), 1)
    for index in range(length // BLOCK):
        rows = pl.ds(index * BLOCK, BLOCK)
        outs, totals = [], []
        for head in range(2):
            mine = (lane < HEAD_DIM) if head == 0 else (lane >= HEAD_DIM)
            query = jnp.where(mine, q_ref[rows, :], BF(0))
            parts = head_scores(query, k_ref, bias_ref, index)
            top = functools.reduce(jnp.maximum, [jnp.max(p, axis=1, keepdims=True) for p in parts])
            parts = [jnp.exp(p - top) for p in parts]
            total = functools.reduce(jnp.add, [jnp.sum(p, axis=1, keepdims=True) for p in parts])
            inverse = 1.0 / total
            out = jnp.zeros((BLOCK, 128), F32)
            for block, part in enumerate(parts):
                out = out + mm((part * inverse).astype(BF), v_ref[pl.ds(block * BLOCK, BLOCK), :])
            outs.append(out)
            totals.append(top + jnp.log(total))
        o_ref[rows, :] = jnp.where(lane < HEAD_DIM, outs[0], outs[1]).astype(BF)
        lse_ref[rows, :] = jnp.where(lane < HEAD_DIM, totals[0], totals[1])


def attend(query, key, value, bias):
    length, width = query.shape
    pair = pl.BlockSpec((length, 128), lambda p: (0, p))
    return pl.pallas_call(
        attend_kernel,
        grid=(width // 128,),
        in_specs=[pair, pair, pair, full_spec((1, length))],
        out_specs=[pair, pair],
        out_shape=[jax.ShapeDtypeStruct((length, width), BF), jax.ShapeDtypeStruct((length, width), F32)],
        compiler_params=params(40),
        name="attend",
    )(query, key, value, bias)


def attend_back_kernel(q_ref, k_ref, v_ref, g_ref, lse_ref, bias_ref, cos_ref, sin_ref, out_ref, dk_ref, dv_ref):
    length = q_ref.shape[0]
    lane = lax.broadcasted_iota(jnp.int32, (BLOCK, 128), 1)
    dk_ref[...] = jnp.zeros_like(dk_ref)
    dv_ref[...] = jnp.zeros_like(dv_ref)
    for index in range(length // BLOCK):
        rows = pl.ds(index * BLOCK, BLOCK)
        grad_query = jnp.zeros((BLOCK, 128), F32)
        for head in range(2):
            mine = (lane < HEAD_DIM) if head == 0 else (lane >= HEAD_DIM)
            query = jnp.where(mine, q_ref[rows, :], BF(0))
            grad = jnp.where(mine, g_ref[rows, :], BF(0))
            lse = lse_ref[rows, head * HEAD_DIM : head * HEAD_DIM + 1]
            probs = [jnp.exp(p - lse) for p in head_scores(query, k_ref, bias_ref, index)]
            grads = [mm_nt(grad, v_ref[pl.ds(b * BLOCK, BLOCK), :]) for b in range(index + 1)]
            delta = functools.reduce(
                jnp.add, [jnp.sum(p * g, axis=1, keepdims=True) for p, g in zip(probs, grads)]
            )
            for block in range(index + 1):
                span = pl.ds(block * BLOCK, BLOCK)
                scored = (probs[block] * (grads[block] - delta)).astype(BF)
                key = k_ref[span, :]
                grad_query = grad_query + jnp.where(mine, mm(scored, key), 0.0)
                dk_ref[span, :] += mm_tn(scored, query)
                dv_ref[span, :] += mm_tn(probs[block].astype(BF), grad)
        grad_query = grad_query * HEAD_DIM ** -0.5
        out_ref[0, rows, :] = turn(grad_query, cos_ref[rows, :], -sin_ref[rows, :]).astype(BF)
    out_ref[1] = turn(dk_ref[...], cos_ref[...], -sin_ref[...]).astype(BF)
    out_ref[2] = dv_ref[...].astype(BF)


def attend_back(query, key, value, grad, lse, bias, cosine, sine):
    length, width = query.shape
    pair = pl.BlockSpec((length, 128), lambda p: (0, p))
    return pl.pallas_call(
        attend_back_kernel,
        grid=(width // 128,),
        in_specs=[pair, pair, pair, pair, pair, full_spec((1, length)), full_spec((length, 128)), full_spec((length, 128))],
        out_specs=pl.BlockSpec((3, length, 128), lambda p: (0, 0, p)),
        out_shape=jax.ShapeDtypeStruct((3, length, width), BF),
        scratch_shapes=[pltpu.VMEM((length, 128), F32)] * 2,
        compiler_params=params(48),
        name="attend_back",
    )(query, key, value, grad, lse, bias, cosine, sine)


def slot_ids(routes):
    length = routes.shape[0]
    labels = jnp.arange(FFN_EXPERTS, dtype=jnp.int32)
    chosen = (routes[:, :, None] == labels).astype(BF)
    member = chosen[:, 0] + chosen[:, 1]
    order = jnp.arange(length, dtype=jnp.int32)
    before = (order[None, :] < order[:, None]).astype(BF)
    place = mm(before, member).astype(jnp.int32)
    ids = jnp.sum(
        jnp.where(routes[:, :, None] == labels, place[:, None, :] + labels * CAP, 0), axis=-1
    )
    return jnp.where(routes < FFN_EXPERTS, ids, -1)


def hits(ids_ref, slot, first):
    row = lax.broadcasted_iota(jnp.int32, (CAP, ids_ref.shape[2]), 0) + first
    return row == ids_ref[slot, 0:1, :], row == ids_ref[slot, 1:2, :]


def dispatch_kernel(info_ref, ids_ref, a0_ref, b0_ref, a1_ref, b1_ref, out_ref):
    first = (info_ref[0] * SPLIT + pl.program_id(0)) * CAP
    half = a0_ref.shape[0]
    for slot, (a_ref, b_ref) in enumerate(((a0_ref, b0_ref), (a1_ref, b1_ref))):
        one, two = hits(ids_ref, slot, first)
        select = jnp.where(one | two, 1.0, 0.0).astype(BF)
        rows = mm(select[:, :half], a_ref[...]) + mm(select[:, half:], b_ref[...])
        out_ref[0, slot] = rows.astype(BF)


def dispatch(info, ids, halves):
    half, width = halves[0].shape
    whole = full_spec((half, width))
    return pl.pallas_call(
        dispatch_kernel,
        grid_spec=pltpu.PrefetchScalarGridSpec(
            num_scalar_prefetch=1,
            grid=(SPLIT,),
            in_specs=[full_spec(ids.shape)] + [whole] * 4,
            out_specs=pl.BlockSpec((1, 2, CAP, width), lambda e, info: (e, 0, 0, 0)),
        ),
        out_shape=jax.ShapeDtypeStruct((SPLIT, 2, CAP, width), BF),
        compiler_params=params(40),
        name="dispatch",
    )(info, ids, *halves)


def split_low(value):
    high = value.astype(BF)
    rest = value - high.astype(F32)
    middle = rest.astype(BF)
    return high, middle, (rest - middle.astype(F32)).astype(BF)


def expert_kernel(
    chunk, groups,
    info_ref, ids_ref, gates_ref, x_ref, c_ref, w_ref,
    send_ref, keep_ref, own_ref, other_ref,
    xt_ref, dt_ref, grad_ref, gate_ref, sign_ref, y_ref, db_ref,
):
    step = pl.program_id(0)
    width = x_ref.shape[-1]
    rows = 2 * CAP
    x = x_ref[...].reshape(rows, width)

    @pl.when(step == 0)
    def _():
        first = (info_ref[0] * SPLIT + chunk) * CAP
        for slot in range(2):
            one, two = hits(ids_ref, slot, first)
            weight = jnp.where(one, gates_ref[slot, 0:1, :], 0.0) + jnp.where(two, gates_ref[slot, 1:2, :], 0.0)
            sign = jnp.where(one, 1.0, 0.0) - jnp.where(two, 1.0, 0.0)
            span = pl.ds(slot * CAP, CAP)
            gate_ref[span, :] = jnp.broadcast_to(jnp.sum(weight, axis=1, keepdims=True), (CAP, 128))
            sign_ref[span, :] = jnp.broadcast_to(jnp.sum(sign, axis=1, keepdims=True), (CAP, 128))
        grad = (c_ref[...].reshape(rows, width).astype(F32) * gate_ref[:, 0:1]).astype(BF)
        grad_ref[...] = grad
        xt_ref[...] = x.T.reshape(xt_ref.shape)
        dt_ref[...] = grad.T.reshape(dt_ref.shape)
        y_ref[...] = jnp.zeros_like(y_ref)
        db_ref[...] = jnp.zeros_like(db_ref)

    columns = w_ref.shape[-1]
    w_gate, w_up, w_down = [w_ref[:, 0, part].reshape(width, columns) for part in range(3)]
    grad = grad_ref[...]
    gate = mm(x, w_gate)
    up = mm(x, w_up)
    sigmoid = 1.0 / (1.0 + jnp.exp(-gate))
    silu = gate * sigmoid
    act = (silu * up).astype(BF)
    d_act = mm(grad, w_down)
    d_gate = (d_act * up * sigmoid * (1.0 + gate * (1.0 - sigmoid))).astype(BF)
    d_up = (d_act * silu).astype(BF)
    y_ref[...] += mm_nt(act, w_down)
    db_ref[...] += mm_nt(d_gate, w_gate) + mm_nt(d_up, w_up)
    for out_ref, flip in ((send_ref, 1), (keep_ref, 0)):
        if out_ref is None:
            continue
        side = jnp.bitwise_xor(info_ref[1], flip) if groups > 1 else 0
        shape = (xt_ref.shape[0], xt_ref.shape[2], columns)
        xt = xt_ref[:, side].reshape(-1, rows)
        dt = dt_ref[:, side].reshape(-1, rows)
        out_ref[:, 0] = mm(xt, d_gate).astype(BF).reshape(shape)
        out_ref[:, 1] = mm(xt, d_up).astype(BF).reshape(shape)
        out_ref[:, 2] = mm(dt, act).astype(BF).reshape(shape)

    @pl.when(step == pl.num_programs(0) - 1)
    def _():
        y = y_ref[...]
        share = jnp.sum(c_ref[...].reshape(rows, width).astype(F32) * y, axis=1, keepdims=True) * sign_ref[:, 0:1]
        lane = lax.broadcasted_iota(jnp.int32, (rows, EXTRA), 1)
        high, middle, low = [part.astype(F32) for part in split_low(share)]
        extra = jnp.where(lane == 0, high, jnp.where(lane == 1, middle, jnp.where(lane == 2, low, 0.0)))
        weighted = (y * gate_ref[:, 0:1]).astype(BF)
        back = db_ref[...].astype(BF)
        extra = extra.astype(BF)
        for slot, out_ref in enumerate((own_ref, other_ref)):
            span = slice(slot * CAP, (slot + 1) * CAP)
            out_ref[:, :width] = weighted[span]
            out_ref[:, width : 2 * width] = back[span]
            out_ref[:, 2 * width :] = extra[span]


def experts(info, ids, gates, rows, cotangents, weights, chunk, line):
    width = rows.shape[-1]
    ranks, _, _, depth, hidden = weights.shape
    tile = 256
    groups = 2 if line else 1
    lead = line if line else 1
    piece = width // (groups * lead)
    grads = (lead, 3, piece, hidden)
    grad_spec = pl.BlockSpec((lead, 3, piece, tile), lambda f, info: (0, 0, 0, f))
    row_spec = pl.BlockSpec((1, 2, CAP, width), lambda f, info: (chunk, 0, 0, 0))
    out_width = 2 * width + EXTRA
    out_spec = pl.BlockSpec((CAP, out_width), lambda f, info: (0, 0))
    grad_shape = jax.ShapeDtypeStruct(grads, BF)
    row_shape = jax.ShapeDtypeStruct((CAP, out_width), BF)
    body = functools.partial(expert_kernel, chunk, groups)
    if groups == 1:
        inner = body
        body = lambda *refs: inner(*refs[:6], None, *refs[6:])
    return pl.pallas_call(
        body,
        grid_spec=pltpu.PrefetchScalarGridSpec(
            num_scalar_prefetch=1,
            grid=(hidden // tile,),
            in_specs=[
                full_spec(ids.shape),
                full_spec(gates.shape),
                row_spec,
                row_spec,
                pl.BlockSpec((ranks, 1, 3, depth, tile), lambda f, info: (0, info[0], 0, 0, f)),
            ],
            out_specs=[grad_spec] * groups + [out_spec] * 2,
            scratch_shapes=[
                pltpu.VMEM((lead, groups, piece, 2 * CAP), BF),
                pltpu.VMEM((lead, groups, piece, 2 * CAP), BF),
                pltpu.VMEM((2 * CAP, width), BF),
                pltpu.VMEM((2 * CAP, 128), F32),
                pltpu.VMEM((2 * CAP, 128), F32),
                pltpu.VMEM((2 * CAP, width), F32),
                pltpu.VMEM((2 * CAP, width), F32),
            ],
        ),
        out_shape=[grad_shape] * groups + [row_shape] * 2,
        compiler_params=params(48),
        cost_estimate=pl.CostEstimate(flops=9 * 10**9, bytes_accessed=14 * 10**6, transcendentals=10**6),
        name="experts",
    )(info, ids, gates, rows, cotangents, weights)


def combine_kernel(info_ref, ids_ref, *refs):
    row_refs, (y_ref, d_ref, share_ref) = refs[:-3], refs[-3:]
    width = y_ref.shape[1]
    block = ids_ref.shape[0]
    column = lax.broadcasted_iota(jnp.int32, (block, CAP), 1)
    one = jnp.broadcast_to(ids_ref[:, 0:1], (block, CAP)) - column
    two = jnp.broadcast_to(ids_ref[:, 1:2], (block, CAP)) - column
    total = jnp.zeros((block, 2 * width + EXTRA), F32)
    for index, rows in enumerate(row_refs):
        core, chunk = index // SPLIT, index % SPLIT
        expert = jnp.bitwise_xor(info_ref[0], core) * SPLIT + chunk
        select = jnp.where((one == expert * CAP) | (two == expert * CAP), 1.0, 0.0).astype(BF)
        total = total + mm(select, rows[...])
    y_ref[...] = total[:, :width].astype(y_ref.dtype)
    d_ref[...] = total[:, width : 2 * width].astype(d_ref.dtype)
    share_ref[...] = total[:, 2 * width :]


def combine(info, ids, rows, width):
    length = ids.shape[0]
    block = 256
    return pl.pallas_call(
        combine_kernel,
        grid_spec=pltpu.PrefetchScalarGridSpec(
            num_scalar_prefetch=1,
            grid=(length // block,),
            in_specs=[pl.BlockSpec((block, 2), lambda i, info: (i, 0))] + [full_spec(r.shape) for r in rows],
            out_specs=[
                pl.BlockSpec((block, width), lambda i, info: (i, 0)),
                pl.BlockSpec((block, width), lambda i, info: (i, 0)),
                pl.BlockSpec((block, EXTRA), lambda i, info: (i, 0)),
            ],
        ),
        out_shape=[
            jax.ShapeDtypeStruct((length, width), F32),
            jax.ShapeDtypeStruct((length, width), F32),
            jax.ShapeDtypeStruct((length, EXTRA), F32),
        ],
        compiler_params=params(48),
        name="combine",
    )(info, ids, *rows)


def per_device(
    count,
    inputs,
    prev_logits,
    routes,
    lengths,
    cotangent,
    attn_gain,
    w_qkv,
    w_out,
    moe_gain,
    w_router,
    w_resid,
    const_mix,
    const_vec,
    w_experts,
):
    half, width = inputs.shape[1:]
    length = routes.shape[1]
    depth = w_experts.shape[0]
    hidden = w_experts.shape[3]
    heads = w_out.shape[1]
    chips = count // 2
    t_rank = lax.axis_index("tensor")
    d_rank = lax.axis_index("dp")
    core, chip = d_rank % 2, d_rank // 2
    place = chip // 2
    fast = (width // chips) % 16 == 0 and depth % 16 == 0
    info = jnp.stack([core, chip % 2]).astype(jnp.int32)
    first_row = t_rank * half
    length_here = lengths[0]

    def in_order(own, other):
        return jnp.where(t_rank == 0, jnp.concatenate([own, other]), jnp.concatenate([other, own]))

    attn_shard = jnp.concatenate([w_qkv.transpose(1, 0, 2), w_out[None]]).astype(BF)
    attn_full = lax.all_gather(attn_shard, "dp", axis=0, tiled=False)
    expert_low = w_experts.astype(BF).transpose(1, 2, 0, 3).reshape(2, SPLIT, 3, depth, hidden)
    expert_full = [lax.all_gather(expert_low[:, c], "dp", axis=0, tiled=False) for c in range(SPLIT)]
    if not fast:
        attn_full = attn_full.transpose(1, 0, 2, 3).reshape(1, 4, width, heads)
        expert_full = [
            w.transpose(1, 2, 0, 3, 4).reshape(1, 2, 3, width, hidden) for w in expert_full
        ]
    out_own = attn_full[:, 3].reshape(width, heads)

    own_in = inputs[0]
    all_in = in_order(own_in, swap_x(own_in))
    row_place = first_row + jnp.arange(half, dtype=jnp.int32)
    live = (row_place < length_here)[:, None]
    cot_own = jnp.where(live, cotangent[0], BF(0))
    cot_other = swap_x(cot_own)
    cot_pair = [swap_dp(cot_own, count, 1), swap_dp(cot_other, count, 1)]
    out_other = swap_x(out_own)
    routes_here = routes[0]
    turned = jnp.concatenate([routes_here[half:], routes_here[:half]])
    routes_rel = jnp.where(t_rank == 0, routes_here, turned)
    ids_own = slot_ids(routes_rel)
    ids_rows = jnp.stack([ids_own.T, swap_dp(ids_own.T, count, 1)])
    cot_rows = dispatch(info, ids_rows, [cot_own, cot_other] + cot_pair)
    inv_freq = THETA ** (-jnp.arange(HEAD_DIM // 2, dtype=F32) / (HEAD_DIM // 2))
    angles = jnp.arange(length, dtype=F32)[:, None] * inv_freq[None, :]
    cosine = jnp.tile(jnp.cos(angles), (1, 4))
    sine = jnp.sin(angles)
    sine = jnp.tile(jnp.concatenate([-sine, sine], axis=1), (1, 2))
    bias = jnp.where(jnp.arange(length, dtype=jnp.int32) < length_here, 0.0, NEG)[None, :].astype(F32)

    attn, query, key, value = project(all_in, attn_gain[None], attn_full, cosine, sine)
    attended, lse = attend(query, key, value, bias)
    att_own = lax.dynamic_slice_in_dim(attended, first_row, half, 0)
    att_other = swap_x(lax.dynamic_slice_in_dim(attended, half - first_row, half, 0))
    resid_in = own_in.astype(F32)
    resid_mid = resid_in + mm_nt(att_own, out_own) + mm_nt(att_other, out_other)

    inv_two = lax.rsqrt(jnp.mean(resid_mid * resid_mid, axis=-1, keepdims=True) + EPS)
    normed = resid_mid * inv_two * moe_gain
    moe_own = normed.astype(BF)
    moe_other = swap_x(moe_own)
    moe_pair = [swap_dp(moe_own, count, 1), swap_dp(moe_other, count, 1)]
    prev_rows = prev_logits[0]
    small_w = jnp.concatenate([w_router, const_mix.reshape(4, width).T], axis=1)
    small = jnp.dot(normed, small_w, precision=HIGHEST)
    logits = small[:, :EXPERTS] + jnp.dot(prev_rows, w_resid, precision=HIGHEST)
    route_own = routes_rel[:half]
    labels = jnp.arange(EXPERTS, dtype=jnp.int32)
    onehot = (route_own[:, :, None] == labels).astype(F32)
    chosen = jnp.sum(onehot * logits[:, None, :], axis=-1)
    top = jnp.max(chosen, axis=-1, keepdims=True)
    gate_weight = jnp.exp(chosen - top)
    gate_weight = gate_weight / jnp.sum(gate_weight, axis=-1, keepdims=True)
    mix = small[:, EXPERTS:].reshape(half, 2, 2)
    mix = jnp.exp(mix - jnp.max(mix, axis=-1, keepdims=True))
    mix = mix / jnp.sum(mix, axis=-1, keepdims=True)
    gate_t = gate_weight.T
    gates_own = jnp.concatenate([gate_t, swap_x(gate_t)], axis=1)
    gates = jnp.stack([gates_own, swap_dp(gates_own, count, 1)])

    moe_rows = dispatch(info, ids_rows, [moe_own, moe_other] + moe_pair)
    own_rows, pair_rows, grads = [], [], []
    for chunk in range(SPLIT):
        line = chips // 2 if fast else 0
        results = experts(info, ids_rows, gates, moe_rows, cot_rows, expert_full[chunk], chunk, line)
        own_rows.append(results[-2])
        pair_rows.append(swap_dp(results[-1], count, 1))
        if fast:
            send, keep = results[0], results[1]
        else:
            parts = results[0].reshape(3, chips // 2, 2, width // chips, hidden)
            send = lax.dynamic_index_in_dim(parts, 1 - chip % 2, 2, keepdims=False).transpose(1, 0, 2, 3)
            keep = lax.dynamic_index_in_dim(parts, chip % 2, 2, keepdims=False).transpose(1, 0, 2, 3)
        got = swap_dp(send, count, 2)
        summed = scatter_line(add_low(keep, got).astype(BF), count, 4, place)
        summed = summed.reshape(3, 2, depth, hidden)
        mine = lax.dynamic_index_in_dim(summed, core, 1, keepdims=False)
        theirs = swap_dp(lax.dynamic_index_in_dim(summed, 1 - core, 1, keepdims=False), count, 1)
        grads.append((mine, theirs))
    mine = jnp.stack([g[0] for g in grads])
    theirs = jnp.stack([g[1] for g in grads])
    grad_experts = jnp.where(core == 0, jnp.concatenate([mine, theirs]), jnp.concatenate([theirs, mine]))
    grad_experts = grad_experts.transpose(2, 0, 1, 3)

    y_all, d_all, share_all = combine(info, ids_own, own_rows + pair_rows, width)
    share_all = jnp.sum(share_all[:, :3], axis=1)
    d_tokens = d_all[:half] + swap_x(d_all[half:].astype(BF)).astype(F32)
    share = share_all[:half] + swap_x(share_all[half:])
    moe_sum = y_all[:half] + swap_x(y_all[half:].astype(BF)).astype(F32)

    is_copy = onehot[:, :, FFN_EXPERTS + 1]
    is_const = onehot[:, :, FFN_EXPERTS + 2 :]
    w_copy = jnp.sum(gate_weight * is_copy, axis=1, keepdims=True)
    w_const = jnp.sum(gate_weight[:, :, None] * is_const, axis=1)
    on_normed = w_copy + jnp.sum(w_const * mix[:, :, 0], axis=1, keepdims=True)
    on_vec = w_const * mix[:, :, 1]
    block_out = resid_mid + moe_sum + on_normed * normed
    block_out = block_out + on_vec[:, 0:1] * const_vec[0] + on_vec[:, 1:2] * const_vec[1]
    block_out = block_out.astype(BF)
    grad_top = cot_own.astype(F32)
    dot_normed = jnp.sum(grad_top * normed, axis=1, keepdims=True)
    dot_vec = jnp.stack([jnp.sum(grad_top * const_vec[j], axis=1) for j in range(2)], axis=1)
    const_gate = mix[:, :, 0] * dot_normed + mix[:, :, 1] * dot_vec
    special = is_copy * dot_normed + jnp.sum(is_const * const_gate[:, None, :], axis=-1)
    delta = share + special[:, 0] - special[:, 1]
    d_first = gate_weight[:, 0] * gate_weight[:, 1] * delta
    d_logits = d_first[:, None] * (onehot[:, 0] - onehot[:, 1])
    d_mix = jnp.stack([w_const * dot_normed, w_const * dot_vec], axis=-1)
    d_mix = mix * (d_mix - jnp.sum(mix * d_mix, axis=-1, keepdims=True))
    grad_prev = jnp.dot(d_logits, w_resid.T, precision=HIGHEST)
    grad_resid = jnp.dot(prev_rows.T, d_logits, precision=HIGHEST)
    d_small = jnp.concatenate([d_logits, d_mix.reshape(half, 4)], axis=1)
    grad_small = jnp.dot(d_small.T, normed, precision=HIGHEST)
    grad_const_vec = jnp.dot(on_vec.T, grad_top, precision=HIGHEST)
    d_normed = jnp.dot(d_small, small_w.T, precision=HIGHEST) + on_normed * grad_top + d_tokens
    grad_moe_gain = jnp.sum(d_normed * resid_mid * inv_two, axis=0)
    scaled = moe_gain * d_normed
    d_resid = (
        grad_top
        + inv_two * scaled
        - resid_mid * (inv_two * inv_two * inv_two) * jnp.mean(scaled * resid_mid, axis=-1, keepdims=True)
    )

    d_mixed = d_resid.astype(BF)
    d_att_own = mm(d_mixed, out_own).astype(BF)
    d_att_other = swap_x(mm(d_mixed, out_other).astype(BF))
    d_attended = in_order(d_att_own, d_att_other)
    d_mixed_all = in_order(d_mixed, swap_x(d_mixed))
    grad_out = mm_tn(d_mixed_all, attended)
    d_qkv = attend_back(query, key, value, d_attended, lse, bias, cosine, sine)
    grad_qkv = jnp.stack([mm_tn(attn, d_qkv[k]) for k in range(3)] + [grad_out])
    d_attn = sum(mm_nt(d_qkv[k], attn_full[:, k].reshape(width, heads)) for k in range(3))
    d_attn_own = lax.dynamic_slice_in_dim(d_attn, first_row, half, 0)
    d_attn_other = lax.dynamic_slice_in_dim(d_attn, half - first_row, half, 0).astype(BF)
    d_attn_own = d_attn_own + swap_x(d_attn_other).astype(F32)
    inv_one = lax.rsqrt(jnp.mean(resid_in * resid_in, axis=-1, keepdims=True) + EPS)
    scaled = attn_gain * d_attn_own
    grad_attn_gain = jnp.sum(d_attn_own * resid_in * inv_one, axis=0)
    grad_inputs = (
        d_resid
        + inv_one * scaled
        - resid_in * (inv_one * inv_one * inv_one) * jnp.mean(scaled * resid_in, axis=-1, keepdims=True)
    )

    blocks = grad_qkv.astype(BF).reshape(4, chips, 2, depth, heads).transpose(2, 1, 0, 3, 4)
    blocks = add_low(pick(blocks, core), swap_dp(pick(blocks, 1 - core), count, 1)).astype(BF)
    blocks = blocks.reshape((chips // 2, 2) + blocks.shape[1:])
    side = chip % 2
    got = swap_dp(lax.dynamic_index_in_dim(blocks, 1 - side, 1, keepdims=False), count, 2)
    blocks = add_low(lax.dynamic_index_in_dim(blocks, side, 1, keepdims=False), got).astype(BF)
    grad_attn = scatter_line(blocks, count, 4, place)

    early = jnp.concatenate(
        [grad_small.reshape(-1), grad_const_vec.reshape(-1), grad_moe_gain, jnp.pad(grad_resid.reshape(-1), (0, 112))]
    )
    early = sum_all(early.reshape(-1, 128), count).reshape(-1)
    grad_attn_gain = sum_all(grad_attn_gain.reshape(-1, 128), count).reshape(-1)
    sizes = [EXPERTS * width, 4 * width, 2 * width, width]
    cuts = [sum(sizes[: i + 1]) for i in range(4)]
    grad_router = early[: cuts[0]].reshape(EXPERTS, width).T
    grad_const_mix = early[cuts[0] : cuts[1]].reshape(2, 2, width)
    grad_const_vec = early[cuts[1] : cuts[2]].reshape(2, width)
    grad_moe_gain = early[cuts[2] : cuts[3]]
    grad_resid = early[cuts[3] : cuts[3] + EXPERTS * EXPERTS].reshape(EXPERTS, EXPERTS)
    return (
        block_out[None],
        grad_inputs.astype(BF)[None],
        grad_prev[None],
        grad_attn_gain,
        grad_attn[:3].transpose(1, 0, 2),
        grad_attn[3],
        grad_moe_gain,
        grad_router,
        grad_resid,
        grad_const_mix,
        grad_const_vec,
        grad_experts,
    )


def solution(mesh):
    placed = (
        P("dp", "tensor", None),
        P("dp", "tensor", None),
        P("dp", None, None),
        P("dp"),
        P("dp", "tensor", None),
        P(),
        P("dp", None, "tensor"),
        P("dp", "tensor"),
        P(),
        P(),
        P(),
        P(),
        P(),
        P("dp", None, None, "tensor"),
    )
    return jax.shard_map(
        functools.partial(per_device, mesh.shape["dp"]),
        mesh=mesh,
        in_specs=placed,
        out_specs=(
            P("dp", "tensor", None),
            P("dp", "tensor", None),
            P("dp", "tensor", None),
            P(),
            P("dp", None, "tensor"),
            P("dp", "tensor"),
            P(),
            P(),
            P(),
            P(),
            P(),
            P("dp", None, None, "tensor"),
        ),
        check_vma=False,
    )
```

```python
import functools

import jax
import jax.numpy as jnp
from jax import lax
from jax.experimental import pallas as pl
from jax.experimental.pallas import tpu as pltpu
from jax.sharding import PartitionSpec as P

HEAD_DIM = 64
FFN_EXPERTS = 8
EXPERTS = 12
CAP = 256
EPS = 1e-05
THETA = 10000.0
HIGHEST = lax.Precision.HIGHEST
BF = jnp.bfloat16
F32 = jnp.float32
NEG = float("-inf")
MIB = 1 << 20
GROUP = 4
SPLIT = FFN_EXPERTS // GROUP
EXTRA = 128


def params(mib):
    return pltpu.CompilerParams(vmem_limit_bytes=mib * MIB)


def mm(a, b):
    return jnp.dot(a, b, preferred_element_type=F32)


def mm_nt(a, b):
    return lax.dot_general(a, b, (((1,), (1,)), ((), ())), preferred_element_type=F32)


def mm_tn(a, b):
    return lax.dot_general(a, b, (((0,), (0,)), ((), ())), preferred_element_type=F32)


def full_spec(shape):
    zeros = (0,) * len(shape)
    return pl.BlockSpec(shape, lambda *ids: zeros)


def swap_x(value):
    return lax.ppermute(value, "tensor", [(0, 1), (1, 0)])


def swap_dp(value, count, mask):
    return lax.ppermute(value, "dp", [(i, i ^ mask) for i in range(count)])


def after(value, *earlier):
    return lax.optimization_barrier((value, earlier))[0]


def pick(blocks, index):
    return lax.dynamic_index_in_dim(blocks, index, 0, keepdims=False)


def add_low(*terms):
    total = terms[0].astype(F32)
    for term in terms[1:]:
        total = total + term.astype(F32)
    return total


def halve(blocks, bits, bit, rank, count):
    place = bits.index(bit)
    high, low = 2**place, 2 ** (len(bits) - place - 1)
    pair = blocks.reshape((high, 2, low) + blocks.shape[1:])
    side = (rank >> bit) & 1
    send = lax.dynamic_index_in_dim(pair, 1 - side, 1, keepdims=False)
    keep = lax.dynamic_index_in_dim(pair, side, 1, keepdims=False)
    total = add_low(keep, swap_dp(send, count, 1 << bit)).astype(BF)
    return total.reshape((high * low,) + blocks.shape[1:])


def scatter_bits(blocks, order, rank, count):
    bits = list(range(count.bit_length() - 1))[::-1]
    for bit in order:
        blocks = halve(blocks, bits, bit, rank, count)
        bits.remove(bit)
    return blocks


def sum_all(value, count):
    bit = 1
    while bit < count:
        value = value + swap_dp(value, count, bit)
        bit *= 2
    return value + swap_x(value)


def group_mask(member):
    return (member & 1) | ((member >> 1) << 2)


def share_group(own, count):
    other = swap_x(own)
    far_own = swap_dp(own, count, 4)
    far_other = swap_dp(other, count, 4)
    near = [swap_dp(v, count, 1) for v in (own, other, far_own, far_other)]
    return [own, other, near[0], near[1], far_own, far_other, near[2], near[3]]


def share_far(pair, far, count):
    got = swap_dp(far, count, 4)
    return [swap_dp(pair, count, 1), got[:1], swap_dp(got[1:], count, 1)]


def share_rows(own, count):
    pair = jnp.stack([own, swap_dp(own, count, 1)])
    return jnp.concatenate([pair, swap_dp(pair, count, 4)])


def turn(values, cosine, sine):
    lane = lax.broadcasted_iota(jnp.int32, values.shape, 1)
    other = jnp.where(lane % HEAD_DIM < HEAD_DIM // 2, pltpu.roll(values, 96, 1), pltpu.roll(values, 32, 1))
    return values * cosine + other * sine


def qkv_kernel(x_ref, gain_ref, w_ref, cos_ref, sin_ref, attn_ref, q_ref, k_ref, v_ref, out_ref):
    @pl.when(pl.program_id(0) == 0)
    def _():
        out_ref[...] = w_ref[:, 3].reshape(out_ref.shape)

    values = x_ref[...].astype(F32)
    inverse = lax.rsqrt(jnp.mean(values * values, axis=-1, keepdims=True) + EPS)
    attn = (values * inverse * gain_ref[...]).astype(BF)
    attn_ref[...] = attn
    width = q_ref.shape[1]
    for part, out in enumerate((q_ref, k_ref, v_ref)):
        weight = w_ref[:, part].reshape(values.shape[1], width)
        rows = mm(attn, weight)
        if part == 2:
            out[...] = rows.astype(BF)
            continue
        for start in range(0, width, 128):
            turned = turn(rows[:, start : start + 128], cos_ref[...], sin_ref[...]).astype(BF)
            if part == 0:
                turned = turned * BF(HEAD_DIM ** -0.5)
            out[:, start : start + 128] = turned


def project(rows, gain, weight, cosine, sine):
    length, width = rows.shape
    heads = weight.shape[-1]
    block = 256
    row_spec = lambda n: pl.BlockSpec((block, n), lambda i: (i, 0))
    return pl.pallas_call(
        qkv_kernel,
        grid=(length // block,),
        in_specs=[
            row_spec(width),
            full_spec((1, width)),
            full_spec(weight.shape),
            row_spec(128),
            row_spec(128),
        ],
        out_specs=[row_spec(width), row_spec(heads), row_spec(heads), row_spec(heads), full_spec((width, heads))],
        out_shape=[jax.ShapeDtypeStruct((length, width), BF)]
        + [jax.ShapeDtypeStruct((length, heads), BF)] * 3
        + [jax.ShapeDtypeStruct((width, heads), BF)],
        compiler_params=params(40),
        name="project",
    )(rows, gain, weight, cosine, sine)


BLOCK = 256


def head_scores(query, k_ref, bias_ref, index):
    row = lax.broadcasted_iota(jnp.int32, (BLOCK, BLOCK), 0)
    column = lax.broadcasted_iota(jnp.int32, (BLOCK, BLOCK), 1)
    parts = []
    for block in range(index + 1):
        span = pl.ds(block * BLOCK, BLOCK)
        scores = mm_nt(query, k_ref[span, :]) + bias_ref[:, span]
        if block == index:
            scores = jnp.where(column <= row, scores, NEG)
        parts.append(scores)
    return parts


def attend_kernel(q_ref, k_ref, v_ref, bias_ref, o_ref, lse_ref):
    length = q_ref.shape[0]
    lane = lax.broadcasted_iota(jnp.int32, (BLOCK, 128), 1)
    for index in range(length // BLOCK):
        rows = pl.ds(index * BLOCK, BLOCK)
        outs, totals = [], []
        for head in range(2):
            mine = (lane < HEAD_DIM) if head == 0 else (lane >= HEAD_DIM)
            query = jnp.where(mine, q_ref[rows, :], BF(0))
            parts = head_scores(query, k_ref, bias_ref, index)
            top = functools.reduce(jnp.maximum, [jnp.max(p, axis=1, keepdims=True) for p in parts])
            parts = [jnp.exp(p - top) for p in parts]
            total = functools.reduce(jnp.add, [jnp.sum(p, axis=1, keepdims=True) for p in parts])
            inverse = 1.0 / total
            out = jnp.zeros((BLOCK, 128), F32)
            for block, part in enumerate(parts):
                out = out + mm((part * inverse).astype(BF), v_ref[pl.ds(block * BLOCK, BLOCK), :])
            outs.append(out)
            totals.append(top + jnp.log(total))
        o_ref[rows, :] = jnp.where(lane < HEAD_DIM, outs[0], outs[1]).astype(BF)
        lse_ref[rows, :] = jnp.where(lane < HEAD_DIM, totals[0], totals[1])


def attend(query, key, value, bias):
    length, width = query.shape
    pair = pl.BlockSpec((length, 128), lambda p: (0, p))
    return pl.pallas_call(
        attend_kernel,
        grid=(width // 128,),
        in_specs=[pair, pair, pair, full_spec((1, length))],
        out_specs=[pair, pair],
        out_shape=[jax.ShapeDtypeStruct((length, width), BF), jax.ShapeDtypeStruct((length, width), F32)],
        compiler_params=params(40),
        name="attend",
    )(query, key, value, bias)


def attend_back_kernel(q_ref, k_ref, v_ref, g_ref, lse_ref, bias_ref, cos_ref, sin_ref, out_ref, dk_ref, dv_ref):
    length = q_ref.shape[0]
    lane = lax.broadcasted_iota(jnp.int32, (BLOCK, 128), 1)
    dk_ref[...] = jnp.zeros_like(dk_ref)
    dv_ref[...] = jnp.zeros_like(dv_ref)
    for index in range(length // BLOCK):
        rows = pl.ds(index * BLOCK, BLOCK)
        grad_query = jnp.zeros((BLOCK, 128), F32)
        for head in range(2):
            mine = (lane < HEAD_DIM) if head == 0 else (lane >= HEAD_DIM)
            query = jnp.where(mine, q_ref[rows, :], BF(0))
            grad = jnp.where(mine, g_ref[rows, :], BF(0))
            lse = lse_ref[rows, head * HEAD_DIM : head * HEAD_DIM + 1]
            probs = [jnp.exp(p - lse) for p in head_scores(query, k_ref, bias_ref, index)]
            grads = [mm_nt(grad, v_ref[pl.ds(b * BLOCK, BLOCK), :]) for b in range(index + 1)]
            delta = functools.reduce(
                jnp.add, [jnp.sum(p * g, axis=1, keepdims=True) for p, g in zip(probs, grads)]
            )
            for block in range(index + 1):
                span = pl.ds(block * BLOCK, BLOCK)
                scored = (probs[block] * (grads[block] - delta)).astype(BF)
                key = k_ref[span, :]
                grad_query = grad_query + jnp.where(mine, mm(scored, key), 0.0)
                dk_ref[span, :] += mm_tn(scored, query)
                dv_ref[span, :] += mm_tn(probs[block].astype(BF), grad)
        grad_query = grad_query * HEAD_DIM ** -0.5
        out_ref[0, rows, :] = turn(grad_query, cos_ref[rows, :], -sin_ref[rows, :]).astype(BF)
    out_ref[1] = turn(dk_ref[...], cos_ref[...], -sin_ref[...]).astype(BF)
    out_ref[2] = dv_ref[...].astype(BF)


def attend_back(query, key, value, grad, lse, bias, cosine, sine):
    length, width = query.shape
    pair = pl.BlockSpec((length, 128), lambda p: (0, p))
    return pl.pallas_call(
        attend_back_kernel,
        grid=(width // 128,),
        in_specs=[pair, pair, pair, pair, pair, full_spec((1, length)), full_spec((length, 128)), full_spec((length, 128))],
        out_specs=pl.BlockSpec((3, length, 128), lambda p: (0, 0, p)),
        out_shape=jax.ShapeDtypeStruct((3, length, width), BF),
        scratch_shapes=[pltpu.VMEM((length, 128), F32)] * 2,
        compiler_params=params(48),
        name="attend_back",
    )(query, key, value, grad, lse, bias, cosine, sine)


def slot_ids(routes):
    length = routes.shape[0]
    labels = jnp.arange(FFN_EXPERTS, dtype=jnp.int32)
    chosen = (routes[:, :, None] == labels).astype(BF)
    member = chosen[:, 0] + chosen[:, 1]
    order = jnp.arange(length, dtype=jnp.int32)
    before = (order[None, :] < order[:, None]).astype(BF)
    place = mm(before, member).astype(jnp.int32)
    ids = jnp.sum(
        jnp.where(routes[:, :, None] == labels, place[:, None, :] + labels * CAP, 0), axis=-1
    )
    return jnp.where(routes < FFN_EXPERTS, ids, -1)


def unpack_kernel(info_ref, w_ref, *out_refs):
    for index, out_ref in enumerate(out_refs):
        chunk, first = index // 3, index % 3
        for place in range(out_ref.shape[0]):
            expert = jnp.bitwise_xor(info_ref[0], first + place) * SPLIT + chunk
            for part in range(3):
                rows = pl.ds(part * FFN_EXPERTS + expert, out_ref.shape[3], stride=3 * FFN_EXPERTS)
                out_ref[place, 0, part] = w_ref[rows, :].astype(BF)


def unpack(info, weights, halves):
    depth, _, _, hidden = weights.shape
    flat = weights.transpose(0, 2, 1, 3).reshape(depth * 3 * FFN_EXPERTS, hidden)
    tile = 128
    each = hidden // halves // tile
    counts = [1, 1, 2] * SPLIT
    return pl.pallas_call(
        unpack_kernel,
        grid_spec=pltpu.PrefetchScalarGridSpec(
            num_scalar_prefetch=1,
            grid=(hidden // tile,),
            in_specs=[pl.BlockSpec((flat.shape[0], tile), lambda c, info: (0, c))],
            out_specs=[
                pl.BlockSpec((n, 1, 3, depth, tile), lambda c, info: (0, c // each, 0, 0, c % each)) for n in counts
            ],
        ),
        out_shape=[jax.ShapeDtypeStruct((n, halves, 3, depth, hidden // halves), BF) for n in counts],
        compiler_params=params(40),
        name="unpack",
    )(info, flat)


def pack_kernel(info_ref, *refs):
    out_ref = refs[-1]
    depth = refs[0].shape[3]
    for index, ref in enumerate(refs[:-1]):
        chunk, member = index // GROUP, index % GROUP
        expert = jnp.bitwise_xor(info_ref[0], member) * SPLIT + chunk
        for part in range(3):
            rows = pl.ds(part * FFN_EXPERTS + expert, depth, stride=3 * FFN_EXPERTS)
            out_ref[rows, :] = ref[0, 0, part].astype(F32)


def pack(info, pieces):
    _, halves, _, depth, part = pieces[0].shape
    hidden = halves * part
    tile = 128
    each = part // tile
    flat = pl.pallas_call(
        pack_kernel,
        grid_spec=pltpu.PrefetchScalarGridSpec(
            num_scalar_prefetch=1,
            grid=(hidden // tile,),
            in_specs=[pl.BlockSpec((1, 1, 3, depth, tile), lambda c, info: (0, c // each, 0, 0, c % each))] * len(pieces),
            out_specs=pl.BlockSpec((depth * 3 * FFN_EXPERTS, tile), lambda c, info: (0, c)),
        ),
        out_shape=jax.ShapeDtypeStruct((depth * 3 * FFN_EXPERTS, hidden), F32),
        compiler_params=params(40),
        name="pack",
    )(info, *pieces)
    return flat.reshape(depth, 3, FFN_EXPERTS, hidden).transpose(0, 2, 1, 3)


def dispatch_kernel(with_gates, info_ref, ids_ref, *refs):
    first = (info_ref[0] * SPLIT + pl.program_id(0)) * CAP
    half_refs, outs = refs[-9:-1] if not with_gates else refs[1:9], refs[-2:] if with_gates else refs[-1:]
    half = half_refs[0].shape[0]
    for slot in range(GROUP):
        row = lax.broadcasted_iota(jnp.int32, (CAP, 2 * half), 0) + first
        one, two = row == ids_ref[slot, 0:1, :], row == ids_ref[slot, 1:2, :]
        select = jnp.where(one | two, 1.0, 0.0).astype(BF)
        rows = mm(select[:, :half], half_refs[2 * slot][...]) + mm(select[:, half:], half_refs[2 * slot + 1][...])
        outs[0][0, slot] = rows.astype(BF)
        if not with_gates:
            continue
        gates_ref = refs[0]
        weight = jnp.where(one, gates_ref[slot, 0:1, :], 0.0) + jnp.where(two, gates_ref[slot, 1:2, :], 0.0)
        sign = jnp.where(one, 1.0, 0.0) - jnp.where(two, 1.0, 0.0)
        lane = lax.broadcasted_iota(jnp.int32, (CAP, 128), 1)
        outs[1][0, slot] = jnp.where(
            lane < 64, jnp.sum(weight, axis=1, keepdims=True), jnp.sum(sign, axis=1, keepdims=True)
        )


def dispatch(info, ids, halves, gates=None):
    half, width = halves[0].shape
    whole = full_spec((half, width))
    extra = [] if gates is None else [gates]
    block = lambda n: pl.BlockSpec((1, GROUP, CAP, n), lambda e, info: (e, 0, 0, 0))
    outs = [(width, BF)] + ([] if gates is None else [(128, F32)])
    return pl.pallas_call(
        functools.partial(dispatch_kernel, gates is not None),
        grid_spec=pltpu.PrefetchScalarGridSpec(
            num_scalar_prefetch=1,
            grid=(SPLIT,),
            in_specs=[full_spec(ids.shape)] + [full_spec(g.shape) for g in extra] + [whole] * (2 * GROUP),
            out_specs=[block(n) for n, _ in outs],
        ),
        out_shape=[jax.ShapeDtypeStruct((SPLIT, GROUP, CAP, n), t) for n, t in outs],
        compiler_params=params(48),
        name="dispatch",
    )(info, ids, *extra, *halves)


def split_low(value):
    high = value.astype(BF)
    rest = value - high.astype(F32)
    middle = rest.astype(BF)
    return high, middle, (rest - middle.astype(F32)).astype(BF)


def expert_kernel(pieces, groups, last, joined, info_ref, x_ref, c_ref, meta_ref, *refs):
    refs = list(refs)
    take = lambda n: [refs.pop(0) for _ in range(n)]
    piece_refs = take(len(pieces))
    if last:
        y_in, db_in = take(2)
    grad_refs = take(groups)
    if last:
        d_refs = take(3)
        y_refs = d_refs if joined else take(3)
    else:
        y_ref, db_ref = take(2)
    xt_ref, dt_ref, grad_ref, w_ref = take(4)
    if last:
        y_ref, db_ref = take(2)
    step = pl.program_id(0)
    width = x_ref.shape[-1]
    rows = GROUP * CAP
    x = x_ref[...].reshape(rows, width)

    @pl.when(step == 0)
    def _():
        grad = (c_ref[...].reshape(rows, width).astype(F32) * meta_ref[...].reshape(rows, 128)[:, 0:1]).astype(BF)
        grad_ref[...] = grad
        xt_ref[...] = x.T.reshape(xt_ref.shape)
        dt_ref[...] = grad.T.reshape(dt_ref.shape)
        if last:
            y_ref[...] = y_in[...]
            db_ref[...] = db_in[...]
        else:
            y_ref[...] = jnp.zeros_like(y_ref)
            db_ref[...] = jnp.zeros_like(db_ref)

    columns = w_ref.shape[-1]
    for ref, mask in zip(piece_refs, pieces):
        for member in range(ref.shape[0]):
            source = jnp.bitwise_xor(info_ref[2], mask | group_mask(member)) if ref.shape[0] > 1 else 0
            w_ref[source] = ref[member, 0]
    w_gate, w_up, w_down = [w_ref[:, part].reshape(width, columns) for part in range(3)]
    grad = grad_ref[...]
    gate = mm(x, w_gate)
    up = mm(x, w_up)
    sigmoid = 1.0 / (1.0 + jnp.exp(-gate))
    silu = gate * sigmoid
    act = (silu * up).astype(BF)
    d_act = mm(grad, w_down)
    d_gate = (d_act * up * sigmoid * (1.0 + gate * (1.0 - sigmoid))).astype(BF)
    d_up = (d_act * silu).astype(BF)
    y_ref[...] += mm_nt(act, w_down)
    db_ref[...] += mm_nt(d_gate, w_gate) + mm_nt(d_up, w_up)
    for flip, out_ref in zip((1, 0), grad_refs if groups > 1 else [None] + grad_refs):
        if out_ref is None:
            continue
        side = jnp.bitwise_xor(info_ref[1], flip) if groups > 1 else 0
        shape = (xt_ref.shape[0], xt_ref.shape[2], columns)
        xt = xt_ref[:, side].reshape(-1, rows)
        dt = dt_ref[:, side].reshape(-1, rows)
        out_ref[:, 0] = mm(xt, d_gate).astype(BF).reshape(shape)
        out_ref[:, 1] = mm(xt, d_up).astype(BF).reshape(shape)
        out_ref[:, 2] = mm(dt, act).astype(BF).reshape(shape)

    if last:

        @pl.when(step == pl.num_programs(0) - 1)
        def _():
            meta = meta_ref[...].reshape(rows, 128)
            y = y_ref[...]
            share = jnp.sum(c_ref[...].reshape(rows, width).astype(F32) * y, axis=1, keepdims=True) * meta[:, 64:65]
            lane = lax.broadcasted_iota(jnp.int32, (rows, EXTRA), 1)
            high, middle, low = [part.astype(F32) for part in split_low(share)]
            extra = jnp.where(lane == 0, high, jnp.where(lane == 1, middle, jnp.where(lane == 2, low, 0.0)))
            weighted = (y * meta[:, 0:1]).astype(BF)
            back = db_ref[...].astype(BF)
            extra = extra.astype(BF)
            for slot in range(GROUP):
                span = slice(slot * CAP, (slot + 1) * CAP)
                to, place = min(slot, 2), max(slot - 2, 0)
                d_refs[to][place, :, :width] = back[span]
                d_refs[to][place, :, width : width + EXTRA] = extra[span]
                if joined:
                    y_refs[to][place, :, width + EXTRA :] = weighted[span]
                else:
                    y_refs[to][place] = weighted[span]


def experts(info, rows, cotangents, meta, pieces, masks, chunk, half, line, sums, joined):
    width = rows.shape[-1]
    hidden = pieces[0].shape[4]
    tile = 256
    groups = 2 if line else 1
    lead = line if line else 1
    piece = width // (groups * lead)
    count = GROUP * CAP
    once = pl.Buffered(1)
    grad_spec = pl.BlockSpec((lead, 3, piece, tile), lambda f, info: (0, 0, 0, f))
    row_spec = lambda n: pl.BlockSpec((1, GROUP, CAP, n), lambda f, info: (chunk, 0, 0, 0), pipeline_mode=once)
    whole = lambda n, m: pl.BlockSpec((n, m), lambda f, info: (0, 0))
    single = lambda n, m: pl.BlockSpec((n, m), lambda f, info: (0, 0), pipeline_mode=once)
    sum_shape = jax.ShapeDtypeStruct((count, width), F32)
    if sums:
        widths = [2 * width + EXTRA] if joined else [width + EXTRA, width]
        shapes = [(n, CAP, m) for m in widths for n in (1, 1, 2)]
        out_specs = [pl.BlockSpec(shape, lambda f, info: (0, 0, 0)) for shape in shapes]
        out_shape = [jax.ShapeDtypeStruct(shape, BF) for shape in shapes]
    else:
        out_specs = [whole(count, width)] * 2
        out_shape = [sum_shape] * 2
    w_shape = (width // pieces[0].shape[3], 3, pieces[0].shape[3], tile)
    return pl.pallas_call(
        functools.partial(expert_kernel, masks, groups, bool(sums), joined),
        grid_spec=pltpu.PrefetchScalarGridSpec(
            num_scalar_prefetch=1,
            grid=(hidden // tile,),
            in_specs=[row_spec(width), row_spec(width), row_spec(128)]
            + [pl.BlockSpec((p.shape[0], 1) + p.shape[2:4] + (tile,), lambda f, info: (0, half, 0, 0, f)) for p in pieces]
            + [single(count, width)] * len(sums),
            out_specs=[grad_spec] * groups + out_specs,
            scratch_shapes=[
                pltpu.VMEM((lead, groups, piece, count), BF),
                pltpu.VMEM((lead, groups, piece, count), BF),
                pltpu.VMEM((count, width), BF),
                pltpu.VMEM(w_shape, BF),
            ]
            + [pltpu.VMEM((count, width), F32)] * len(sums),
        ),
        out_shape=[jax.ShapeDtypeStruct((lead, 3, piece, hidden), BF)] * groups + out_shape,
        compiler_params=params(60),
        name="experts",
    )(info, rows, cotangents, meta, *pieces, *sums)


def combine_kernel(starts, info_ref, ids_ref, *refs):
    row_refs, out_ref = refs[:-1], refs[-1]
    block = ids_ref.shape[0]
    column = lax.broadcasted_iota(jnp.int32, (block, CAP), 1)
    one = jnp.broadcast_to(ids_ref[:, 0:1], (block, CAP)) - column
    two = jnp.broadcast_to(ids_ref[:, 1:2], (block, CAP)) - column
    total = jnp.zeros(out_ref.shape, F32)
    for index, rows in enumerate(row_refs):
        member, chunk = index // SPLIT, index % SPLIT
        expert = jnp.bitwise_xor(info_ref[0], member) * SPLIT + chunk
        select = jnp.where((one == expert * CAP) | (two == expert * CAP), 1.0, 0.0).astype(BF)
        total = total + mm(select, rows[0, :, starts[chunk] : starts[chunk] + total.shape[1]])
    out_ref[...] = total


def combine(info, ids, rows, width, starts):
    length = ids.shape[0]
    block = 256
    return pl.pallas_call(
        functools.partial(combine_kernel, starts),
        grid_spec=pltpu.PrefetchScalarGridSpec(
            num_scalar_prefetch=1,
            grid=(length // block,),
            in_specs=[pl.BlockSpec((block, 2), lambda i, info: (i, 0))] + [full_spec(r.shape) for r in rows],
            out_specs=pl.BlockSpec((block, width), lambda i, info: (i, 0)),
        ),
        out_shape=jax.ShapeDtypeStruct((length, width), F32),
        compiler_params=params(48),
        name="combine",
    )(info, ids, *rows)


def per_device(
    count,
    inputs,
    prev_logits,
    routes,
    lengths,
    cotangent,
    attn_gain,
    w_qkv,
    w_out,
    moe_gain,
    w_router,
    w_resid,
    const_mix,
    const_vec,
    w_experts,
):
    half, width = inputs.shape[1:]
    length = routes.shape[1]
    depth = w_experts.shape[0]
    hidden = w_experts.shape[3]
    heads = w_out.shape[1]
    t_rank = lax.axis_index("tensor")
    d_rank = lax.axis_index("dp")
    bit = lambda n: (d_rank >> n) & 1
    group = bit(2) * 2 + bit(0)
    fast = count == 16 and depth % 16 == 0
    info = jnp.stack([group, bit(1), d_rank]).astype(jnp.int32)
    first_row = t_rank * half
    length_here = lengths[0]

    def in_order(own, other):
        return jnp.where(t_rank == 0, jnp.concatenate([own, other]), jnp.concatenate([other, own]))

    attn_shard = jnp.concatenate([w_qkv.transpose(1, 0, 2), w_out[None]]).astype(BF)
    attn_full = lax.all_gather(attn_shard, "dp", axis=0, tiled=False)
    halves = 2
    part = hidden // halves
    chunks = [(e, h) for e in range(SPLIT) for h in range(halves)]
    if fast:
        mine = unpack(info, after(w_experts, attn_shard), halves)
        quads = []
        for e in range(SPLIT):
            near_mine, near_pair, far_mine = mine[3 * e : 3 * e + 3]
            quads.append(jnp.concatenate([near_mine] + share_far(near_pair, far_mine, count)))
        masks = [0, 8, 2, 10]
        quads, attn_full = lax.optimization_barrier((quads, attn_full))
        far = [swap_dp(quads[0], count, 8)]
        near = [swap_dp(quads[0], count, 2)]
    else:
        attn_full = attn_full.transpose(1, 0, 2, 3).reshape(1, 4, width, heads)
        expert_low = w_experts.astype(BF).reshape(depth, GROUP, SPLIT, 3, halves, part)
        expert_low = expert_low.transpose(1, 2, 4, 3, 0, 5)
        gathered = lax.all_gather(expert_low, "dp", axis=4, tiled=True)
        gathered = pick(gathered, group)
        masks = [0]
        weights = [[gathered[e][None]] for e in range(SPLIT)]

    own_in = inputs[0]
    other_in = swap_x(own_in)
    all_in = in_order(own_in, other_in)
    row_place = first_row + jnp.arange(half, dtype=jnp.int32)
    live = (row_place < length_here)[:, None]
    cot_own = jnp.where(live, cotangent[0], BF(0))
    def slot_order(rows):
        turned = jnp.concatenate([rows[:, half:], rows[:, :half]], axis=1)
        return jnp.where(t_rank == 0, rows, turned)

    far_routes = jnp.concatenate([routes, swap_dp(routes, count, 4)])
    near_routes = swap_dp(far_routes, count, 1)
    all_routes = jnp.stack([far_routes[0], near_routes[0], far_routes[1], near_routes[1]])
    all_routes = slot_order(all_routes)
    routes_rel = all_routes[0]
    ids_own = slot_ids(routes_rel)
    ids_rows = jnp.stack([ids_own.T] + [slot_ids(all_routes[m]).T for m in range(1, GROUP)])
    cot_other = swap_x(after(cot_own, other_in))
    far_cot = [swap_dp(after(cot_own, mine) if fast else cot_own, count, 4)]
    far_cot.append(swap_dp(after(cot_other, far_cot[0]), count, 4))
    inv_freq = THETA ** (-jnp.arange(HEAD_DIM // 2, dtype=F32) / (HEAD_DIM // 2))
    angles = jnp.arange(length, dtype=F32)[:, None] * inv_freq[None, :]
    cosine = jnp.tile(jnp.cos(angles), (1, 4))
    sine = jnp.sin(angles)
    sine = jnp.tile(jnp.concatenate([-sine, sine], axis=1), (1, 2))
    bias = jnp.where(jnp.arange(length, dtype=jnp.int32) < length_here, 0.0, NEG)[None, :].astype(F32)

    all_in = after(all_in, ids_rows, cot_other, far_cot[0])
    if fast:
        all_in = after(all_in, quads)
    attn, query, key, value, out_own = project(all_in, attn_gain[None], attn_full, cosine, sine)
    out_other = swap_x(out_own)
    attended, lse = attend(query, key, value, bias)
    att_own = lax.dynamic_slice_in_dim(attended, first_row, half, 0)
    att_other = swap_x(lax.dynamic_slice_in_dim(attended, half - first_row, half, 0))
    if fast:
        near.append(swap_dp(after(quads[1], near[0], attended), count, 2))
    near_cot = [swap_dp(v, count, 1) for v in [cot_own, cot_other] + far_cot]
    att_other = after(att_other, far_cot[1], near_cot)
    if fast:
        att_other = after(att_other, far[0], near[0])
    resid_in = own_in.astype(F32)
    resid_mid = resid_in + mm_nt(att_own, out_own) + mm_nt(att_other, out_other)

    inv_two = lax.rsqrt(jnp.mean(resid_mid * resid_mid, axis=-1, keepdims=True) + EPS)
    normed = resid_mid * inv_two * moe_gain
    moe_own = normed.astype(BF)
    moe_halves = share_group(moe_own, count)
    prev_rows = prev_logits[0]
    (cot_rows,) = dispatch(
        info, ids_rows, after([cot_own, cot_other] + near_cot[:2] + far_cot + near_cot[2:], moe_own)
    )
    if fast:
        far.append(swap_dp(after(quads[1], far[0], attended), count, 8))
        weights = [[quads[0], far[0], near[0], swap_dp(far[0], count, 2)]]
        weights += [[quads[1], far[1], near[1], swap_dp(far[1], count, 2)]]
    small_w = jnp.concatenate([w_router, const_mix.reshape(4, width).T], axis=1)
    small = jnp.dot(normed, small_w, precision=HIGHEST)
    logits = small[:, :EXPERTS] + jnp.dot(prev_rows, w_resid, precision=HIGHEST)
    route_own = routes_rel[:half]
    labels = jnp.arange(EXPERTS, dtype=jnp.int32)
    onehot = (route_own[:, :, None] == labels).astype(F32)
    chosen = jnp.sum(onehot * logits[:, None, :], axis=-1)
    top = jnp.max(chosen, axis=-1, keepdims=True)
    gate_weight = jnp.exp(chosen - top)
    gate_weight = gate_weight / jnp.sum(gate_weight, axis=-1, keepdims=True)
    mix = small[:, EXPERTS:].reshape(half, 2, 2)
    mix = jnp.exp(mix - jnp.max(mix, axis=-1, keepdims=True))
    mix = mix / jnp.sum(mix, axis=-1, keepdims=True)
    gate_t = gate_weight.T
    gates = jnp.stack([gate_t, swap_dp(gate_t, count, 4)])
    gates = jnp.concatenate([gates, swap_x(gates)], axis=2)
    gates = jnp.stack([gates, swap_dp(gates, count, 1)], axis=1).reshape(GROUP, 2, length)

    moe_rows, meta = dispatch(info, ids_rows, moe_halves, gates)
    d_rows, y_rows, grads = [], [], []
    sent, kept, ready = [], [], []

    def own_side(index):
        total = add_low(kept[index], sent[index]).astype(BF)
        pair = total.reshape((2, 2) + total.shape[1:])
        ready.append((swap_dp(pick(pair, 1 - bit(3)), count, 8), pick(pair, bit(3))))
        return pair

    def far_side(index):
        total = add_low(*ready[index])
        return total.reshape(2, 3, 2, depth, part).transpose(0, 2, 1, 3, 4)

    rows_in = moe_rows
    if fast:
        rows_in = after(rows_in, far[1], near[1], cot_rows)
    for index, (e, h) in enumerate(chunks):
        if h == 0:
            sums = []
        if fast and index == 3:
            far_rows = share_far(joint[1], joint[2], count)
            rows_in = after(rows_in, own_side(0), far_rows[:2])
        line = 4 if fast else 0
        results = experts(info, rows_in, cot_rows, meta, weights[e], masks, e, h, line, sums, e == 0)
        if h == 0:
            sums = list(results[-2:])
        elif e == 0:
            joint = results[-3:]
        else:
            d_last, y_last = results[-6:-3], results[-3:]
        if fast:
            kept.append(results[1])
            sent.append(results[0])
            if index < 3:
                sent[index] = swap_dp(results[0], count, 2)
        else:
            blocks = results[0].reshape(3, count, depth, part).transpose(1, 0, 2, 3)
            order = [1] + list(range(3, count.bit_length() - 1))
            blocks = scatter_bits(blocks, order, d_rank, count)
            grads.append(add_low(blocks.reshape(2, 2, 3, depth, part)))
    if not fast:
        far_rows = share_far(joint[1], joint[2], count)
    first_rows = [joint[0]] + far_rows
    near_last = swap_dp(d_last[1], count, 1)
    far_last = swap_dp(after(d_last[2], first_rows[3]), count, 4)
    if fast:
        kept[1] = after(kept[1], far_last)
        sent[3] = swap_dp(after(sent[3], far_last), count, 2)
    last_rows = [d_last[0], near_last, far_last[:1], swap_dp(far_last[1:], count, 1)]
    d_rows = [r for pair in zip(first_rows, last_rows) for r in pair]
    d_starts = (0, 0)
    d_other = combine(info, ids_own[half:], d_rows, width + EXTRA, d_starts)
    d_got = swap_x(d_other[:, :width].astype(BF))
    share_got = swap_x(jnp.sum(d_other[:, width : width + 3], axis=1))
    if fast:
        d_rows[0] = after(d_rows[0], own_side(1), d_other)
    d_own = combine(info, ids_own[:half], d_rows, width + EXTRA, d_starts)
    if fast:
        d_own = after(d_own, own_side(2))
    y_near = swap_dp(after(y_last[1], d_own), count, 1)
    y_far = swap_dp(after(y_last[2], d_own), count, 4)
    d_tokens = d_own[:, :width] + d_got.astype(F32)
    share = jnp.sum(d_own[:, width : width + 3], axis=1) + share_got

    is_copy = onehot[:, :, FFN_EXPERTS + 1]
    is_const = onehot[:, :, FFN_EXPERTS + 2 :]
    w_copy = jnp.sum(gate_weight * is_copy, axis=1, keepdims=True)
    w_const = jnp.sum(gate_weight[:, :, None] * is_const, axis=1)
    on_normed = w_copy + jnp.sum(w_const * mix[:, :, 0], axis=1, keepdims=True)
    on_vec = w_const * mix[:, :, 1]
    grad_top = cot_own.astype(F32)
    dot_normed = jnp.sum(grad_top * normed, axis=1, keepdims=True)
    dot_vec = jnp.stack([jnp.sum(grad_top * const_vec[j], axis=1) for j in range(2)], axis=1)
    const_gate = mix[:, :, 0] * dot_normed + mix[:, :, 1] * dot_vec
    special = is_copy * dot_normed + jnp.sum(is_const * const_gate[:, None, :], axis=-1)
    delta = share + special[:, 0] - special[:, 1]
    d_first = gate_weight[:, 0] * gate_weight[:, 1] * delta
    d_logits = d_first[:, None] * (onehot[:, 0] - onehot[:, 1])
    d_mix = jnp.stack([w_const * dot_normed, w_const * dot_vec], axis=-1)
    d_mix = mix * (d_mix - jnp.sum(mix * d_mix, axis=-1, keepdims=True))
    grad_prev = jnp.dot(d_logits, w_resid.T, precision=HIGHEST)
    grad_resid = jnp.dot(prev_rows.T, d_logits, precision=HIGHEST)
    d_small = jnp.concatenate([d_logits, d_mix.reshape(half, 4)], axis=1)
    grad_small = jnp.dot(d_small.T, normed, precision=HIGHEST)
    grad_const_vec = jnp.dot(on_vec.T, grad_top, precision=HIGHEST)
    d_normed = jnp.dot(d_small, small_w.T, precision=HIGHEST) + on_normed * grad_top + d_tokens
    grad_moe_gain = jnp.sum(d_normed * resid_mid * inv_two, axis=0)
    scaled = moe_gain * d_normed
    d_resid = (
        grad_top
        + inv_two * scaled
        - resid_mid * (inv_two * inv_two * inv_two) * jnp.mean(scaled * resid_mid, axis=-1, keepdims=True)
    )

    d_mixed = d_resid.astype(BF)
    d_att_own = mm(d_mixed, out_own).astype(BF)
    d_att_other = swap_x(mm(d_mixed, out_other).astype(BF))
    if fast:
        d_att_other = after(d_att_other, own_side(3), y_near, y_far)
    d_attended = in_order(d_att_own, d_att_other)
    d_mixed_all = in_order(d_mixed, swap_x(d_mixed))
    grad_out = mm_tn(d_mixed_all, attended)
    d_qkv = attend_back(query, key, value, d_attended, lse, bias, cosine, sine)
    grad_qkv = jnp.stack([mm_tn(attn, d_qkv[k]) for k in range(3)] + [grad_out])
    d_attn = sum(mm_nt(d_qkv[k], attn_full[:, k].reshape(width, heads)) for k in range(3))
    values = all_in.astype(F32)
    inv_all = lax.rsqrt(jnp.mean(values * values, axis=-1, keepdims=True) + EPS)
    grad_attn_gain = jnp.sum(d_attn * values * inv_all, axis=0)
    d_attn_own = lax.dynamic_slice_in_dim(d_attn, first_row, half, 0)
    d_attn_other = lax.dynamic_slice_in_dim(d_attn, half - first_row, half, 0).astype(BF)
    d_attn_own = d_attn_own + swap_x(d_attn_other).astype(F32)
    inv_one = lax.rsqrt(jnp.mean(resid_in * resid_in, axis=-1, keepdims=True) + EPS)
    scaled = attn_gain * d_attn_own
    grad_inputs = (
        d_resid
        + inv_one * scaled
        - resid_in * (inv_one * inv_one * inv_one) * jnp.mean(scaled * resid_in, axis=-1, keepdims=True)
    )

    y_all_rows = [y_last[0], y_near, y_far[:1], swap_dp(y_far[1:], count, 1)]
    y_all_rows = [r for pair in zip(first_rows, y_all_rows) for r in pair]
    y_all = combine(info, ids_own, after(y_all_rows, d_qkv), width, (width + EXTRA, 0))
    moe_sum = y_all[:half] + swap_x(y_all[half:].astype(BF)).astype(F32)
    block_out = resid_mid + moe_sum + on_normed * normed
    block_out = block_out + on_vec[:, 0:1] * const_vec[0] + on_vec[:, 1:2] * const_vec[1]
    block_out = block_out.astype(BF)

    if fast:
        grads = [far_side(index) for index in range(len(chunks))]
    pieces = []
    for e in range(SPLIT):
        blocks = jnp.stack(grads[e * halves : (e + 1) * halves], axis=2)

        def block_of(m):
            side = pick(blocks, jnp.bitwise_xor(bit(2), m >> 1))
            return pick(side, jnp.bitwise_xor(bit(0), m & 1))[None]

        far_blocks = jnp.concatenate([block_of(2), block_of(3)]).astype(BF)
        pieces += [block_of(0)] + share_far(block_of(1).astype(BF), far_blocks, count)
    if fast:
        grad_experts = pack(info, pieces)
    else:
        table = jnp.stack([p.astype(F32) for p in pieces]).reshape(SPLIT, GROUP, halves, 3, depth, part)
        table = jnp.take(table, jnp.bitwise_xor(jnp.arange(GROUP), group), axis=1)
        grad_experts = table.transpose(4, 1, 0, 3, 2, 5).reshape(depth, FFN_EXPERTS, 3, hidden)
    blocks = grad_qkv.astype(BF).reshape(4, count, depth, heads).transpose(1, 0, 2, 3)
    order = [0, 1] + list(range(3, count.bit_length() - 1)) + [2]
    grad_attn = scatter_bits(blocks, order, d_rank, count)[0].astype(F32)

    early = jnp.concatenate(
        [
            grad_small.reshape(-1),
            grad_const_vec.reshape(-1),
            grad_moe_gain,
            jnp.pad(grad_resid.reshape(-1), (0, 112)),
            grad_attn_gain,
        ]
    )
    early = sum_all(early.reshape(-1, 128), count).reshape(-1)
    grad_attn_gain = early[-width:]
    sizes = [EXPERTS * width, 4 * width, 2 * width, width]
    cuts = [sum(sizes[: i + 1]) for i in range(4)]
    grad_router = early[: cuts[0]].reshape(EXPERTS, width).T
    grad_const_mix = early[cuts[0] : cuts[1]].reshape(2, 2, width)
    grad_const_vec = early[cuts[1] : cuts[2]].reshape(2, width)
    grad_moe_gain = early[cuts[2] : cuts[3]]
    grad_resid = early[cuts[3] : cuts[3] + EXPERTS * EXPERTS].reshape(EXPERTS, EXPERTS)
    return (
        block_out[None],
        grad_inputs.astype(BF)[None],
        grad_prev[None],
        grad_attn_gain,
        grad_attn[:3].transpose(1, 0, 2),
        grad_attn[3],
        grad_moe_gain,
        grad_router,
        grad_resid,
        grad_const_mix,
        grad_const_vec,
        grad_experts,
    )


def solution(mesh):
    placed = (
        P("dp", "tensor", None),
        P("dp", "tensor", None),
        P("dp", None, None),
        P("dp"),
        P("dp", "tensor", None),
        P(),
        P("dp", None, "tensor"),
        P("dp", "tensor"),
        P(),
        P(),
        P(),
        P(),
        P(),
        P("dp", None, None, "tensor"),
    )
    return jax.shard_map(
        functools.partial(per_device, mesh.shape["dp"]),
        mesh=mesh,
        in_specs=placed,
        out_specs=(
            P("dp", "tensor", None),
            P("dp", "tensor", None),
            P("dp", "tensor", None),
            P(),
            P("dp", None, "tensor"),
            P("dp", "tensor"),
            P(),
            P(),
            P(),
            P(),
            P(),
            P("dp", None, None, "tensor"),
        ),
        check_vma=False,
    )
```

```python
import functools

import jax
import jax.numpy as jnp
from jax import lax
from jax.experimental import pallas as pl
from jax.experimental.pallas import tpu as pltpu
from jax.sharding import PartitionSpec as P

HEAD_DIM = 64
FFN_EXPERTS = 8
EXPERTS = 12
CAP = 256
EPS = 1e-05
THETA = 10000.0
HIGHEST = lax.Precision.HIGHEST
BF = jnp.bfloat16
F32 = jnp.float32
NEG = float("-inf")
MIB = 1 << 20
GROUP = 4
SPLIT = FFN_EXPERTS // GROUP
EXTRA = 128


def params(mib):
    return pltpu.CompilerParams(vmem_limit_bytes=mib * MIB)


def mm(a, b):
    return jnp.dot(a, b, preferred_element_type=F32)


def mm_nt(a, b):
    return lax.dot_general(a, b, (((1,), (1,)), ((), ())), preferred_element_type=F32)


def mm_tn(a, b):
    return lax.dot_general(a, b, (((0,), (0,)), ((), ())), preferred_element_type=F32)


def full_spec(shape):
    zeros = (0,) * len(shape)
    return pl.BlockSpec(shape, lambda *ids: zeros)


def swap_x(value):
    return lax.ppermute(value, "tensor", [(0, 1), (1, 0)])


def swap_dp(value, count, mask):
    return lax.ppermute(value, "dp", [(i, i ^ mask) for i in range(count)])


def after(value, *earlier):
    return lax.optimization_barrier((value, earlier))[0]


def meet(*values):
    return lax.optimization_barrier(values)


def pick(blocks, index):
    return lax.dynamic_index_in_dim(blocks, index, 0, keepdims=False)


def chain(values, swap):
    done = []
    for value in values:
        done.append(swap(after(value, done[-1]) if done else value))
    return done


def add_low(*terms):
    total = terms[0].astype(F32)
    for term in terms[1:]:
        total = total + term.astype(F32)
    return total


def halve(blocks, bits, bit, rank, count):
    place = bits.index(bit)
    high, low = 2**place, 2 ** (len(bits) - place - 1)
    pair = blocks.reshape((high, 2, low) + blocks.shape[1:])
    side = (rank >> bit) & 1
    send = lax.dynamic_index_in_dim(pair, 1 - side, 1, keepdims=False)
    keep = lax.dynamic_index_in_dim(pair, side, 1, keepdims=False)
    total = add_low(keep, swap_dp(send, count, 1 << bit)).astype(BF)
    return total.reshape((high * low,) + blocks.shape[1:])


def scatter_bits(blocks, order, rank, count):
    bits = list(range(count.bit_length() - 1))[::-1]
    for bit in order:
        blocks = halve(blocks, bits, bit, rank, count)
        bits.remove(bit)
    return blocks


def sum_all(value, count):
    bit = 1
    while bit < count:
        value = value + swap_dp(value, count, bit)
        bit *= 2
    return value + swap_x(value)


FAR = 2


def share_group(own, count):
    other = swap_x(own)
    far_own = swap_dp(own, count, FAR)
    far_other = swap_dp(other, count, FAR)
    near = [swap_dp(v, count, 1) for v in (own, other, far_own, far_other)]
    return [own, other, near[0], near[1], far_own, far_other, near[2], near[3]]


def share_far(pair, far, count):
    got = swap_dp(far, count, FAR)
    return [(swap_dp(pair, count, 1), 0), (got, 0), (swap_dp(got, count, 1), 1)]


def entry(item):
    return item[0][item[1] : item[1] + 1]


def turn(values, cosine, sine):
    lane = lax.broadcasted_iota(jnp.int32, values.shape, 1)
    other = jnp.where(lane % HEAD_DIM < HEAD_DIM // 2, pltpu.roll(values, 96, 1), pltpu.roll(values, 32, 1))
    return values * cosine + other * sine


def qkv_kernel(x_ref, gain_ref, w_ref, cos_ref, sin_ref, attn_ref, q_ref, k_ref, v_ref, out_ref):
    @pl.when(pl.program_id(0) == 0)
    def _():
        out_ref[...] = w_ref[:, 3].reshape(out_ref.shape)

    values = x_ref[...].astype(F32)
    inverse = lax.rsqrt(jnp.mean(values * values, axis=-1, keepdims=True) + EPS)
    attn = (values * inverse * gain_ref[...]).astype(BF)
    attn_ref[...] = attn
    width = q_ref.shape[1]
    for part, out in enumerate((q_ref, k_ref, v_ref)):
        weight = w_ref[:, part].reshape(values.shape[1], width)
        rows = mm(attn, weight)
        if part == 2:
            out[...] = rows.astype(BF)
            continue
        for start in range(0, width, 128):
            turned = turn(rows[:, start : start + 128], cos_ref[...], sin_ref[...]).astype(BF)
            if part == 0:
                turned = turned * BF(HEAD_DIM ** -0.5)
            out[:, start : start + 128] = turned


def project(rows, gain, weight, cosine, sine):
    length, width = rows.shape
    heads = weight.shape[-1]
    block = 256
    row_spec = lambda n: pl.BlockSpec((block, n), lambda i: (i, 0))
    return pl.pallas_call(
        qkv_kernel,
        grid=(length // block,),
        in_specs=[
            row_spec(width),
            full_spec((1, width)),
            full_spec(weight.shape),
            row_spec(128),
            row_spec(128),
        ],
        out_specs=[row_spec(width), row_spec(heads), row_spec(heads), row_spec(heads), full_spec((width, heads))],
        out_shape=[jax.ShapeDtypeStruct((length, width), BF)]
        + [jax.ShapeDtypeStruct((length, heads), BF)] * 3
        + [jax.ShapeDtypeStruct((width, heads), BF)],
        compiler_params=params(40),
        name="project",
    )(rows, gain, weight, cosine, sine)


BLOCK = 256


def head_scores(query, k_ref, bias_ref, index):
    row = lax.broadcasted_iota(jnp.int32, (BLOCK, BLOCK), 0)
    column = lax.broadcasted_iota(jnp.int32, (BLOCK, BLOCK), 1)
    parts = []
    for block in range(index + 1):
        span = pl.ds(block * BLOCK, BLOCK)
        scores = mm_nt(query, k_ref[span, :]) + bias_ref[:, span]
        if block == index:
            scores = jnp.where(column <= row, scores, NEG)
        parts.append(scores)
    return parts


def attend_kernel(q_ref, k_ref, v_ref, bias_ref, o_ref, lse_ref):
    length = q_ref.shape[0]
    lane = lax.broadcasted_iota(jnp.int32, (BLOCK, 128), 1)
    for index in range(length // BLOCK):
        rows = pl.ds(index * BLOCK, BLOCK)
        outs, totals = [], []
        for head in range(2):
            mine = (lane < HEAD_DIM) if head == 0 else (lane >= HEAD_DIM)
            query = jnp.where(mine, q_ref[rows, :], BF(0))
            parts = head_scores(query, k_ref, bias_ref, index)
            top = functools.reduce(jnp.maximum, [jnp.max(p, axis=1, keepdims=True) for p in parts])
            parts = [jnp.exp(p - top) for p in parts]
            total = functools.reduce(jnp.add, [jnp.sum(p, axis=1, keepdims=True) for p in parts])
            inverse = 1.0 / total
            out = jnp.zeros((BLOCK, 128), F32)
            for block, part in enumerate(parts):
                out = out + mm((part * inverse).astype(BF), v_ref[pl.ds(block * BLOCK, BLOCK), :])
            outs.append(out)
            totals.append(top + jnp.log(total))
        o_ref[rows, :] = jnp.where(lane < HEAD_DIM, outs[0], outs[1]).astype(BF)
        lse_ref[rows, :] = jnp.where(lane < HEAD_DIM, totals[0], totals[1])


def attend(query, key, value, bias):
    length, width = query.shape
    pair = pl.BlockSpec((length, 128), lambda p: (0, p))
    return pl.pallas_call(
        attend_kernel,
        grid=(width // 128,),
        in_specs=[pair, pair, pair, full_spec((1, length))],
        out_specs=[pair, pair],
        out_shape=[jax.ShapeDtypeStruct((length, width), BF), jax.ShapeDtypeStruct((length, width), F32)],
        compiler_params=params(40),
        name="attend",
    )(query, key, value, bias)


def attend_back_kernel(q_ref, k_ref, v_ref, g_ref, lse_ref, bias_ref, cos_ref, sin_ref, out_ref, dk_ref, dv_ref):
    length = q_ref.shape[0]
    lane = lax.broadcasted_iota(jnp.int32, (BLOCK, 128), 1)
    dk_ref[...] = jnp.zeros_like(dk_ref)
    dv_ref[...] = jnp.zeros_like(dv_ref)
    for index in range(length // BLOCK):
        rows = pl.ds(index * BLOCK, BLOCK)
        grad_query = jnp.zeros((BLOCK, 128), F32)
        for head in range(2):
            mine = (lane < HEAD_DIM) if head == 0 else (lane >= HEAD_DIM)
            query = jnp.where(mine, q_ref[rows, :], BF(0))
            grad = jnp.where(mine, g_ref[rows, :], BF(0))
            lse = lse_ref[rows, head * HEAD_DIM : head * HEAD_DIM + 1]
            probs = [jnp.exp(p - lse) for p in head_scores(query, k_ref, bias_ref, index)]
            grads = [mm_nt(grad, v_ref[pl.ds(b * BLOCK, BLOCK), :]) for b in range(index + 1)]
            delta = functools.reduce(
                jnp.add, [jnp.sum(p * g, axis=1, keepdims=True) for p, g in zip(probs, grads)]
            )
            for block in range(index + 1):
                span = pl.ds(block * BLOCK, BLOCK)
                scored = (probs[block] * (grads[block] - delta)).astype(BF)
                key = k_ref[span, :]
                grad_query = grad_query + jnp.where(mine, mm(scored, key), 0.0)
                dk_ref[span, :] += mm_tn(scored, query)
                dv_ref[span, :] += mm_tn(probs[block].astype(BF), grad)
        grad_query = grad_query * HEAD_DIM ** -0.5
        out_ref[0, rows, :] = turn(grad_query, cos_ref[rows, :], -sin_ref[rows, :]).astype(BF)
    out_ref[1] = turn(dk_ref[...], cos_ref[...], -sin_ref[...]).astype(BF)
    out_ref[2] = dv_ref[...].astype(BF)


def attend_back(query, key, value, grad, lse, bias, cosine, sine):
    length, width = query.shape
    pair = pl.BlockSpec((length, 128), lambda p: (0, p))
    return pl.pallas_call(
        attend_back_kernel,
        grid=(width // 128,),
        in_specs=[pair, pair, pair, pair, pair, full_spec((1, length)), full_spec((length, 128)), full_spec((length, 128))],
        out_specs=pl.BlockSpec((3, length, 128), lambda p: (0, 0, p)),
        out_shape=jax.ShapeDtypeStruct((3, length, width), BF),
        scratch_shapes=[pltpu.VMEM((length, 128), F32)] * 2,
        compiler_params=params(48),
        name="attend_back",
    )(query, key, value, grad, lse, bias, cosine, sine)


def slot_ids(routes):
    length = routes.shape[0]
    labels = jnp.arange(FFN_EXPERTS, dtype=jnp.int32)
    chosen = (routes[:, :, None] == labels).astype(BF)
    member = chosen[:, 0] + chosen[:, 1]
    order = jnp.arange(length, dtype=jnp.int32)
    before = (order[None, :] < order[:, None]).astype(BF)
    place = mm(before, member).astype(jnp.int32)
    ids = jnp.sum(
        jnp.where(routes[:, :, None] == labels, place[:, None, :] + labels * CAP, 0), axis=-1
    )
    return jnp.where(routes < FFN_EXPERTS, ids, -1)


def unpack_kernel(info_ref, w_ref, near_ref, pair_ref, *far_refs):
    jobs = [(near_ref, 0, c, 0, c) for c in range(SPLIT)] + [(pair_ref, 0, c, 1, c) for c in range(SPLIT)]
    jobs += [(ref, m, 0, 2 + m, c) for c, ref in enumerate(far_refs) for m in range(2)]
    for out_ref, place, slot, member, chunk in jobs:
        expert = jnp.bitwise_xor(info_ref[0], member) * SPLIT + chunk
        for part in range(3):
            rows = pl.ds(part * FFN_EXPERTS + expert, out_ref.shape[4], stride=3 * FFN_EXPERTS)
            out_ref[place, slot, 0, part] = w_ref[rows, :].astype(BF)


def unpack(info, weights, halves):
    depth, _, _, hidden = weights.shape
    flat = weights.transpose(0, 2, 1, 3).reshape(depth * 3 * FFN_EXPERTS, hidden)
    tile = 128
    each = hidden // halves // tile
    counts = [(1, SPLIT)] * 2 + [(2, 1)] * SPLIT
    return pl.pallas_call(
        unpack_kernel,
        grid_spec=pltpu.PrefetchScalarGridSpec(
            num_scalar_prefetch=1,
            grid=(hidden // tile,),
            in_specs=[pl.BlockSpec((flat.shape[0], tile), lambda c, info: (0, c))],
            out_specs=[
                pl.BlockSpec(n + (1, 3, depth, tile), lambda c, info: (0, 0, c // each, 0, 0, c % each))
                for n in counts
            ],
        ),
        out_shape=[jax.ShapeDtypeStruct(n + (halves, 3, depth, hidden // halves), BF) for n in counts],
        compiler_params=params(40),
        name="unpack",
    )(info, flat)


def pack_kernel(info_ref, *refs):
    out_ref = refs[-1]
    depth = refs[0].shape[2]
    for index, ref in enumerate(refs[:-1]):
        chunk, member = index // GROUP, index % GROUP
        expert = jnp.bitwise_xor(info_ref[0], member) * SPLIT + chunk
        for part in range(3):
            rows = pl.ds(part * FFN_EXPERTS + expert, depth, stride=3 * FFN_EXPERTS)
            out_ref[rows, :] = ref[0, part].astype(F32)


def pack(info, pieces):
    _, _, depth, hidden = pieces[0][0].shape
    tile = 128
    flat = pl.pallas_call(
        pack_kernel,
        grid_spec=pltpu.PrefetchScalarGridSpec(
            num_scalar_prefetch=1,
            grid=(hidden // tile,),
            in_specs=[
                pl.BlockSpec((1, 3, depth, tile), lambda c, info, place=place: (place, 0, 0, c))
                for _, place in pieces
            ],
            out_specs=pl.BlockSpec((depth * 3 * FFN_EXPERTS, tile), lambda c, info: (0, c)),
        ),
        out_shape=jax.ShapeDtypeStruct((depth * 3 * FFN_EXPERTS, hidden), F32),
        compiler_params=params(40),
        name="pack",
    )(info, *[p for p, _ in pieces])
    return flat.reshape(depth, 3, FFN_EXPERTS, hidden).transpose(0, 2, 1, 3)


def dispatch_kernel(with_gates, info_ref, ids_ref, *refs):
    first = (info_ref[0] * SPLIT + pl.program_id(0)) * CAP
    half_refs, outs = refs[-9:-1] if not with_gates else refs[1:9], refs[-2:] if with_gates else refs[-1:]
    half = half_refs[0].shape[0]
    for slot in range(GROUP):
        row = lax.broadcasted_iota(jnp.int32, (CAP, 2 * half), 0) + first
        one, two = row == ids_ref[slot, 0:1, :], row == ids_ref[slot, 1:2, :]
        select = jnp.where(one | two, 1.0, 0.0).astype(BF)
        rows = mm(select[:, :half], half_refs[2 * slot][...]) + mm(select[:, half:], half_refs[2 * slot + 1][...])
        outs[0][0, slot] = rows.astype(BF)
        if not with_gates:
            continue
        gates_ref = refs[0]
        weight = jnp.where(one, gates_ref[slot, 0:1, :], 0.0) + jnp.where(two, gates_ref[slot, 1:2, :], 0.0)
        sign = jnp.where(one, 1.0, 0.0) - jnp.where(two, 1.0, 0.0)
        lane = lax.broadcasted_iota(jnp.int32, (CAP, 128), 1)
        outs[1][0, slot] = jnp.where(
            lane < 64, jnp.sum(weight, axis=1, keepdims=True), jnp.sum(sign, axis=1, keepdims=True)
        )


def dispatch(info, ids, halves, gates=None):
    half, width = halves[0][0].shape[-2:]

    def half_spec(item):
        if item[1] is None:
            return full_spec((half, width))
        return pl.BlockSpec((None, half, width), lambda e, info, place=item[1]: (place, 0, 0))

    extra = [] if gates is None else [gates]
    block = lambda n: pl.BlockSpec((1, GROUP, CAP, n), lambda e, info: (e, 0, 0, 0))
    outs = [(width, BF)] + ([] if gates is None else [(128, F32)])
    return pl.pallas_call(
        functools.partial(dispatch_kernel, gates is not None),
        grid_spec=pltpu.PrefetchScalarGridSpec(
            num_scalar_prefetch=1,
            grid=(SPLIT,),
            in_specs=[full_spec(ids.shape)] + [full_spec(g.shape) for g in extra] + [half_spec(v) for v in halves],
            out_specs=[block(n) for n, _ in outs],
        ),
        out_shape=[jax.ShapeDtypeStruct((SPLIT, GROUP, CAP, n), t) for n, t in outs],
        compiler_params=params(48),
        name="dispatch",
    )(info, ids, *extra, *[v for v, _ in halves])


def split_low(value):
    high = value.astype(BF)
    rest = value - high.astype(F32)
    middle = rest.astype(BF)
    return high, middle, (rest - middle.astype(F32)).astype(BF)


def expert_kernel(pieces, last, joined, info_ref, x_ref, c_ref, meta_ref, *refs):
    refs = list(refs)
    take = lambda n: [refs.pop(0) for _ in range(n)]
    piece_refs = take(len(pieces))
    if last:
        y_in, db_in, _ = take(3)
    (out_ref,) = take(1)
    if last:
        d_refs = take(3)
        y_refs = d_refs if joined else take(3)
    else:
        y_ref, db_ref = take(2)
    xt_ref, dt_ref, grad_ref, w_ref = take(4)
    if last:
        y_ref, db_ref = take(2)
    step = pl.program_id(0)
    width = x_ref.shape[-1]
    rows = GROUP * CAP
    x = x_ref[...].reshape(rows, width)

    @pl.when(step == 0)
    def _():
        grad = (c_ref[...].reshape(rows, width).astype(F32) * meta_ref[...].reshape(rows, 128)[:, 0:1]).astype(BF)
        grad_ref[...] = grad
        xt_ref[...] = x.T
        dt_ref[...] = grad.T
        if last:
            y_ref[...] = y_in[...]
            db_ref[...] = db_in[...]
        else:
            y_ref[...] = jnp.zeros_like(y_ref)
            db_ref[...] = jnp.zeros_like(db_ref)

    columns = w_ref.shape[-1]
    for ref, mask in zip(piece_refs, pieces):
        for member in range(ref.shape[0]):
            if ref.shape[0] == 1:
                source = 0
            elif mask is None:
                source = (member & ~3) + jnp.bitwise_xor(info_ref[2] & 3, member & 3)
            else:
                source = jnp.bitwise_xor(info_ref[2], mask | member)
            w_ref[source] = ref[member, 0]
    w_gate, w_up, w_down = [w_ref[:, part].reshape(width, columns) for part in range(3)]
    grad = grad_ref[...]
    gate = mm(x, w_gate)
    up = mm(x, w_up)
    sigmoid = 1.0 / (1.0 + jnp.exp(-gate))
    silu = gate * sigmoid
    act = (silu * up).astype(BF)
    d_act = mm(grad, w_down)
    d_gate = (d_act * up * sigmoid * (1.0 + gate * (1.0 - sigmoid))).astype(BF)
    d_up = (d_act * silu).astype(BF)
    y_ref[...] += mm_nt(act, w_down)
    db_ref[...] += mm_nt(d_gate, w_gate) + mm_nt(d_up, w_up)
    shape = (out_ref.shape[0], out_ref.shape[2], columns)
    out_ref[:, 0] = mm(xt_ref[...], d_gate).astype(BF).reshape(shape)
    out_ref[:, 1] = mm(xt_ref[...], d_up).astype(BF).reshape(shape)
    out_ref[:, 2] = mm(dt_ref[...], act).astype(BF).reshape(shape)

    if last:

        @pl.when(step == pl.num_programs(0) - 1)
        def _():
            meta = meta_ref[...].reshape(rows, 128)
            y = y_ref[...]
            share = jnp.sum(c_ref[...].reshape(rows, width).astype(F32) * y, axis=1, keepdims=True) * meta[:, 64:65]
            lane = lax.broadcasted_iota(jnp.int32, (rows, EXTRA), 1)
            high, middle, low = [part.astype(F32) for part in split_low(share)]
            extra = jnp.where(lane == 0, high, jnp.where(lane == 1, middle, jnp.where(lane == 2, low, 0.0)))
            weighted = (y * meta[:, 0:1]).astype(BF)
            back = db_ref[...].astype(BF)
            extra = extra.astype(BF)
            for slot in range(GROUP):
                span = slice(slot * CAP, (slot + 1) * CAP)
                to, place = min(slot, 2), max(slot - 2, 0)
                d_refs[to][place, :, :width] = back[span]
                d_refs[to][place, :, width : width + EXTRA] = extra[span]
                if joined:
                    y_refs[to][place, :, width + EXTRA :] = weighted[span]
                else:
                    y_refs[to][place] = weighted[span]


def experts(info, rows, cotangents, meta, pieces, masks, chunk, half, lead, carried, joined):
    width = rows.shape[-1]
    part = pieces[0].shape[-1]
    tile = 256
    piece = width // lead
    count = GROUP * CAP
    once = pl.Buffered(1)
    each = part // tile
    grad_spec = pl.BlockSpec((lead, 3, piece, tile), lambda f, info: (0, 0, 0, half * each + f))
    row_spec = lambda n: pl.BlockSpec((1, GROUP, CAP, n), lambda f, info: (chunk, 0, 0, 0), pipeline_mode=once)
    whole = lambda n, m: pl.BlockSpec((n, m), lambda f, info: (0, 0))
    single = lambda n, m: pl.BlockSpec((n, m), lambda f, info: (0, 0), pipeline_mode=once)
    if carried:
        widths = [2 * width + EXTRA] if joined else [width + EXTRA, width]
        shapes = [(n, CAP, m) for m in widths for n in (1, 1, 2)]
        out_specs = [pl.BlockSpec(shape, lambda f, info: (0, 0, 0)) for shape in shapes]
        out_shape = [jax.ShapeDtypeStruct(shape, BF) for shape in shapes]
        carried_specs = [single(count, width)] * 2 + [pl.BlockSpec(memory_space=pl.ANY)]
    else:
        out_specs = [whole(count, width)] * 2
        out_shape = [jax.ShapeDtypeStruct((count, width), F32)] * 2
        carried_specs = []
    depth = pieces[0].shape[-2]
    return pl.pallas_call(
        functools.partial(expert_kernel, masks, bool(carried), joined),
        grid_spec=pltpu.PrefetchScalarGridSpec(
            num_scalar_prefetch=1,
            grid=(each,),
            in_specs=[row_spec(width), row_spec(width), row_spec(128)]
            + [
                pl.BlockSpec((p.shape[0], 1, 3, depth, tile), lambda f, info, h=half * (p.shape[1] - 1): (0, h, 0, 0, f))
                for p in pieces
            ]
            + carried_specs,
            out_specs=[grad_spec] + out_specs,
            scratch_shapes=[
                pltpu.VMEM((width, count), BF),
                pltpu.VMEM((width, count), BF),
                pltpu.VMEM((count, width), BF),
                pltpu.VMEM((width // depth, 3, depth, tile), BF),
            ]
            + [pltpu.VMEM((count, width), F32)] * (2 if carried else 0),
        ),
        out_shape=[jax.ShapeDtypeStruct((lead, 3, piece, 2 * part), BF)] + out_shape,
        input_output_aliases={4 + len(pieces) + 2: 0} if carried else {},
        compiler_params=params(60),
        name="experts",
    )(info, rows, cotangents, meta, *pieces, *carried)


def combine_kernel(starts, info_ref, ids_ref, *refs):
    row_refs, outs = refs[: SPLIT * GROUP], refs[SPLIT * GROUP :]
    block = ids_ref.shape[0]
    width = sum(ref.shape[1] for ref in outs)
    column = lax.broadcasted_iota(jnp.int32, (block, CAP), 1)
    one = jnp.broadcast_to(ids_ref[:, 0:1], (block, CAP)) - column
    two = jnp.broadcast_to(ids_ref[:, 1:2], (block, CAP)) - column
    total = jnp.zeros((block, width), F32)
    for index, rows in enumerate(row_refs):
        member, chunk = index // SPLIT, index % SPLIT
        expert = jnp.bitwise_xor(info_ref[0], member) * SPLIT + chunk
        select = jnp.where((one == expert * CAP) | (two == expert * CAP), 1.0, 0.0).astype(BF)
        total = total + mm(select, rows[0, :, starts[chunk] : starts[chunk] + width])
    first = 0
    for ref in outs:
        ref[...] = total[:, first : first + ref.shape[1]].astype(ref.dtype)
        first += ref.shape[1]


def combine(info, ids, rows, outs, starts):
    length = ids.shape[0]
    width = sum(n for n, _ in outs)
    block = 256

    def row_spec(index, item):
        columns = width if starts[index % SPLIT] == 0 else item[0].shape[2]
        return pl.BlockSpec((1, CAP, columns), lambda i, info, place=item[1]: (place, 0, 0))

    return pl.pallas_call(
        functools.partial(combine_kernel, starts),
        grid_spec=pltpu.PrefetchScalarGridSpec(
            num_scalar_prefetch=1,
            grid=(length // block,),
            in_specs=[pl.BlockSpec((block, 2), lambda i, info: (i, 0))]
            + [row_spec(index, item) for index, item in enumerate(rows)],
            out_specs=[pl.BlockSpec((block, n), lambda i, info: (i, 0)) for n, _ in outs],
        ),
        out_shape=[jax.ShapeDtypeStruct((length, n), t) for n, t in outs],
        compiler_params=params(48),
        name="combine",
    )(info, ids, *[item[0] for item in rows])


def per_device(
    count,
    inputs,
    prev_logits,
    routes,
    lengths,
    cotangent,
    attn_gain,
    w_qkv,
    w_out,
    moe_gain,
    w_router,
    w_resid,
    const_mix,
    const_vec,
    w_experts,
):
    half, width = inputs.shape[1:]
    length = routes.shape[1]
    depth = w_experts.shape[0]
    hidden = w_experts.shape[3]
    heads = w_out.shape[1]
    t_rank = lax.axis_index("tensor")
    d_rank = lax.axis_index("dp")
    bit = lambda n: (d_rank >> n) & 1
    group = d_rank % GROUP
    fast = count == 16 and depth % 16 == 0
    info = jnp.stack([group, bit(2), d_rank]).astype(jnp.int32)
    first_row = t_rank * half
    length_here = lengths[0]

    def in_order(own, other):
        return jnp.where(t_rank == 0, jnp.concatenate([own, other]), jnp.concatenate([other, own]))

    attn_shard = jnp.concatenate([w_qkv.transpose(1, 0, 2), w_out[None]]).astype(BF)
    attn_full = lax.all_gather(attn_shard, "dp", axis=0, tiled=False)
    halves = 2
    part = hidden // halves
    chunks = [(e, h) for e in range(SPLIT) for h in range(halves)]
    if fast:
        mine = unpack(info, after(w_experts, attn_shard), halves)
        masks = [None]
        pair = swap_dp(mine[1], count, 1)
        quads = []
        for e in range(SPLIT):
            got = swap_dp(mine[2 + e], count, FAR)
            passed = swap_dp(got, count, 1)
            quads.append(jnp.concatenate([mine[0][:, e], pair[:, e], got[:1, 0], passed[1:, 0]]))
        lines = [[i + GROUP * j for j in range(count // GROUP)] for i in range(GROUP)]
        weights = {}
        for e in range(SPLIT):
            full = lax.all_gather(quads[e], "dp", axis=0, tiled=True, axis_index_groups=lines)
            weights.update({(e, h): [full] for h in range(halves)})
    else:
        attn_full = attn_full.transpose(1, 0, 2, 3).reshape(1, 4, width, heads)
        expert_low = w_experts.astype(BF).reshape(depth, GROUP, SPLIT, 3, halves, part)
        expert_low = expert_low.transpose(1, 2, 4, 3, 0, 5)
        gathered = lax.all_gather(expert_low, "dp", axis=4, tiled=True)
        gathered = pick(gathered, group)
        masks = [0]
        weights = {(e, h): [gathered[e, h][None, None]] for e, h in chunks}

    own_in = inputs[0]
    other_in = swap_x(own_in)
    all_in = in_order(own_in, other_in)
    row_place = first_row + jnp.arange(half, dtype=jnp.int32)
    live = (row_place < length_here)[:, None]
    cot_own = jnp.where(live, cotangent[0], BF(0))
    def slot_order(rows):
        turned = jnp.concatenate([rows[:, half:], rows[:, :half]], axis=1)
        return jnp.where(t_rank == 0, rows, turned)

    far_routes = jnp.concatenate([routes, swap_dp(routes, count, FAR)])
    near_routes = swap_dp(far_routes, count, 1)
    all_routes = jnp.stack([far_routes[0], near_routes[0], far_routes[1], near_routes[1]])
    all_routes = slot_order(all_routes)
    routes_rel = all_routes[0]
    ids_own = slot_ids(routes_rel)
    ids_rows = jnp.stack([ids_own.T] + [slot_ids(all_routes[m]).T for m in range(1, GROUP)])
    cot_other = swap_x(after(cot_own, other_in))
    far_cot = [swap_dp(after(cot_own, mine) if fast else cot_own, count, FAR)]
    inv_freq = THETA ** (-jnp.arange(HEAD_DIM // 2, dtype=F32) / (HEAD_DIM // 2))
    angles = jnp.arange(length, dtype=F32)[:, None] * inv_freq[None, :]
    cosine = jnp.tile(jnp.cos(angles), (1, 4))
    sine = jnp.sin(angles)
    sine = jnp.tile(jnp.concatenate([-sine, sine], axis=1), (1, 2))
    bias = jnp.where(jnp.arange(length, dtype=jnp.int32) < length_here, 0.0, NEG)[None, :].astype(F32)

    all_in = after(all_in, ids_rows)
    if fast:
        all_in = after(all_in, quads[0])
    attn, query, key, value, out_own = project(all_in, attn_gain[None], attn_full, cosine, sine)
    out_other = swap_x(out_own)
    far_cot.append(swap_dp(after(cot_other, query), count, FAR))
    if fast:
        query = after(query, quads[1])
    attended, lse = attend(query, key, value, bias)
    att_own = lax.dynamic_slice_in_dim(attended, first_row, half, 0)
    att_send = lax.dynamic_slice_in_dim(attended, half - first_row, half, 0)
    att_other = swap_x(after(att_send, out_other))
    near_cot = chain(after([cot_own, cot_other, far_cot[0]], attended), lambda v: swap_dp(v, count, 1))
    att_other = after(att_other, far_cot[1], near_cot)
    near_cot.append(swap_dp(far_cot[1], count, 1))
    resid_in = own_in.astype(F32)
    resid_mid = resid_in + mm_nt(att_own, out_own) + mm_nt(att_other, out_other)

    inv_two = lax.rsqrt(jnp.mean(resid_mid * resid_mid, axis=-1, keepdims=True) + EPS)
    normed = resid_mid * inv_two * moe_gain
    moe_own = normed.astype(BF)
    moe_other = swap_x(moe_own)
    far_moe = [swap_dp(moe_own, count, FAR)]
    prev_rows = prev_logits[0]
    cot_halves = [cot_own, cot_other] + near_cot[:2] + far_cot + near_cot[2:]
    (cot_rows,) = dispatch(info, ids_rows, [(v, None) for v in after(cot_halves, moe_own)])
    small_w = jnp.concatenate([w_router, const_mix.reshape(4, width).T], axis=1)
    small = jnp.dot(normed, small_w, precision=HIGHEST)
    logits = small[:, :EXPERTS] + jnp.dot(prev_rows, w_resid, precision=HIGHEST)
    route_own = routes_rel[:half]
    labels = jnp.arange(EXPERTS, dtype=jnp.int32)
    onehot = (route_own[:, :, None] == labels).astype(F32)
    chosen = jnp.sum(onehot * logits[:, None, :], axis=-1)
    top = jnp.max(chosen, axis=-1, keepdims=True)
    gate_weight = jnp.exp(chosen - top)
    gate_weight = gate_weight / jnp.sum(gate_weight, axis=-1, keepdims=True)
    mix = small[:, EXPERTS:].reshape(half, 2, 2)
    mix = jnp.exp(mix - jnp.max(mix, axis=-1, keepdims=True))
    mix = mix / jnp.sum(mix, axis=-1, keepdims=True)
    gate_t = gate_weight.T
    gates = jnp.stack([gate_t, swap_dp(gate_t, count, FAR)])
    gates = jnp.concatenate([gates, swap_x(gates)], axis=2)
    gates = jnp.stack([gates, swap_dp(gates, count, 1)], axis=1).reshape(GROUP, 2, length)

    far_moe.append(swap_dp(after(moe_other, gates), count, FAR))
    near_moe = jnp.stack([moe_own, moe_other, after(far_moe[0], cot_rows)])
    near_moe = swap_dp(near_moe, count, 1)
    is_copy = onehot[:, :, FFN_EXPERTS + 1]
    is_const = onehot[:, :, FFN_EXPERTS + 2 :]
    w_copy = jnp.sum(gate_weight * is_copy, axis=1, keepdims=True)
    w_const = jnp.sum(gate_weight[:, :, None] * is_const, axis=1)
    on_normed = w_copy + jnp.sum(w_const * mix[:, :, 0], axis=1, keepdims=True)
    on_vec = w_const * mix[:, :, 1]
    grad_top = cot_own.astype(F32)
    dot_normed = jnp.sum(grad_top * normed, axis=1, keepdims=True)
    dot_vec = jnp.stack([jnp.sum(grad_top * const_vec[j], axis=1) for j in range(2)], axis=1)
    const_gate = mix[:, :, 0] * dot_normed + mix[:, :, 1] * dot_vec
    special = is_copy * dot_normed + jnp.sum(is_const * const_gate[:, None, :], axis=-1)
    d_mix = jnp.stack([w_const * dot_normed, w_const * dot_vec], axis=-1)
    d_mix = mix * (d_mix - jnp.sum(mix * d_mix, axis=-1, keepdims=True))
    special = special[:, 0] - special[:, 1]
    gate_product = gate_weight[:, 0] * gate_weight[:, 1]
    d_mix = d_mix.reshape(half, 4)
    far_moe[1], special, gate_product, d_mix, on_normed, on_vec = meet(
        far_moe[1], special, gate_product, d_mix, on_normed, on_vec
    )
    near_last = swap_dp(far_moe[1], count, 1)
    moe_halves = [(moe_own, None), (moe_other, None), (near_moe, 0), (near_moe, 1)]
    moe_halves += [(far_moe[0], None), (far_moe[1], None), (near_moe, 2), (near_last, None)]
    moe_rows, meta = dispatch(info, ids_rows, moe_halves, gates)
    rows_in = moe_rows
    lead = 1
    if fast:
        lead = count // GROUP
    grads = []
    for e, h in chunks:
        if h == 0:
            carried = ()
        results = experts(info, rows_in, cot_rows, meta, weights[e, h], masks, e, h, lead, carried, e == 0)
        if h == 0:
            carried = (results[1], results[2], results[0])
            continue
        if e == 0:
            joint = results[1:]
            rows_in = after(rows_in, joint[0])
        else:
            d_last, y_last = results[1:4], results[4:]
        blocks = results[0]
        if fast:
            blocks = lax.psum_scatter(blocks, "dp", scatter_dimension=0, tiled=False, axis_index_groups=lines)
        else:
            blocks = blocks.reshape(3, count, depth, hidden).transpose(1, 0, 2, 3)
            blocks = scatter_bits(blocks, range(2, count.bit_length() - 1), d_rank, count)
            blocks = blocks.transpose(1, 0, 2, 3)
        grads.append(blocks.reshape(3, GROUP, depth, hidden))
    first_rows = [(joint[0], 0)] + share_far(joint[1], joint[2], count)
    last_rows = [(d_last[0], 0)] + share_far(d_last[1], after(d_last[2], first_rows[1][0], first_rows[2][0]), count)
    d_rows = [r for pair in zip(first_rows, last_rows) for r in pair]
    d_low, share_other = combine(info, ids_own[half:], d_rows, [(width, BF), (EXTRA, F32)], (0, 0))
    d_got = swap_x(d_low)
    share_got = swap_x(jnp.sum(share_other[:, :3], axis=1))
    d_own, share_own = combine(info, after(ids_own[:half], d_low), d_rows, [(width, F32), (EXTRA, F32)], (0, 0))
    y_rest = share_far(after(y_last[1], d_own), after(y_last[2], d_own), count)
    d_tokens = d_own + d_got.astype(F32)
    share = jnp.sum(share_own[:, :3], axis=1) + share_got

    d_first = gate_product * (share + special)
    d_logits = d_first[:, None] * (onehot[:, 0] - onehot[:, 1])
    grad_prev = jnp.dot(d_logits, w_resid.T, precision=HIGHEST)
    grad_resid = jnp.dot(prev_rows.T, d_logits, precision=HIGHEST)
    d_small = jnp.concatenate([d_logits, d_mix], axis=1)
    grad_small = jnp.dot(d_small.T, normed, precision=HIGHEST)
    grad_const_vec = jnp.dot(on_vec.T, grad_top, precision=HIGHEST)
    d_normed = jnp.dot(d_small, small_w.T, precision=HIGHEST) + on_normed * grad_top + d_tokens
    grad_moe_gain = jnp.sum(d_normed * resid_mid * inv_two, axis=0)
    scaled = moe_gain * d_normed
    d_resid = (
        grad_top
        + inv_two * scaled
        - resid_mid * (inv_two * inv_two * inv_two) * jnp.mean(scaled * resid_mid, axis=-1, keepdims=True)
    )

    def final_pieces(blocks):
        blocks = [
            lax.dynamic_index_in_dim(blocks, jnp.bitwise_xor(group, m), 1, keepdims=False)[None] for m in range(GROUP)
        ]
        return [(blocks[0], 0)] + share_far(blocks[1], jnp.concatenate(blocks[2:]), count)

    d_mixed = d_resid.astype(BF)
    d_att_own = mm(d_mixed, out_own).astype(BF)
    d_att_other = swap_x(mm(d_mixed, out_other).astype(BF))
    y_rows = [r for pair in zip(first_rows, [(y_last[0], 0)] + y_rest) for r in pair]
    y_ids = after(ids_own, d_att_own)
    (y_low,) = combine(info, y_ids[half:], y_rows, [(width, BF)], (width + EXTRA, 0))
    (y_own,) = combine(info, y_ids[:half], y_rows, [(width, F32)], (width + EXTRA, 0))
    y_got = swap_x(y_low)
    first_pieces = final_pieces(after(grads[0], y_rest[2][0]))
    d_att_other = after(d_att_other, y_own, y_low, first_pieces[1][0], first_pieces[2][0])
    d_attended = in_order(d_att_own, d_att_other)
    d_mixed_all = in_order(d_mixed, swap_x(d_mixed))
    grad_out = mm_tn(d_mixed_all, attended)
    d_qkv = attend_back(query, key, value, d_attended, lse, bias, cosine, sine)
    grad_qkv = jnp.stack([mm_tn(attn, d_qkv[k]) for k in range(3)] + [grad_out])
    blocks = grad_qkv.astype(BF).reshape(4, count, depth, heads).transpose(1, 0, 2, 3)
    blocks, y_got = meet(blocks, y_got)
    bits = list(range(count.bit_length() - 1))[::-1]
    stage = halve(blocks, bits, 0, d_rank, count)
    bits.remove(0)
    d_attn = sum(mm_nt(d_qkv[k], attn_full[:, k].reshape(width, heads)) for k in range(3))
    values = all_in.astype(F32)
    inv_all = lax.rsqrt(jnp.mean(values * values, axis=-1, keepdims=True) + EPS)
    grad_attn_gain = jnp.sum(d_attn * values * inv_all, axis=0)
    d_attn_own = lax.dynamic_slice_in_dim(d_attn, first_row, half, 0)
    d_attn_other = lax.dynamic_slice_in_dim(d_attn, half - first_row, half, 0).astype(BF)
    d_attn_got = swap_x(d_attn_other)
    inv_one = lax.rsqrt(jnp.mean(resid_in * resid_in, axis=-1, keepdims=True) + EPS)
    early = jnp.concatenate(
        [
            grad_small.reshape(-1),
            grad_const_vec.reshape(-1),
            grad_moe_gain,
            jnp.pad(grad_resid.reshape(-1), (0, 112)),
            grad_attn_gain,
        ]
    )
    early = early.reshape(-1, 128)
    stage, early = meet(stage, early)
    hop = 1
    for n in bits[::-1]:
        stage = halve(stage, bits, n, d_rank, count)
        bits.remove(n)
        early = early + swap_dp(early, count, hop)
        hop *= 2
        stage, early = meet(stage, early)
        if n == 1:
            stage, grads = meet(stage, grads)
        if n == 2:
            stage, d_attn_got = meet(stage, d_attn_got)
    early = early + swap_dp(early, count, hop)
    grad_attn = stage[0].astype(F32)
    d_attn_own = d_attn_own + d_attn_got.astype(F32)
    scaled = attn_gain * d_attn_own
    grad_inputs = (
        d_resid
        + inv_one * scaled
        - resid_in * (inv_one * inv_one * inv_one) * jnp.mean(scaled * resid_in, axis=-1, keepdims=True)
    )

    block_out = resid_mid + y_own + y_got.astype(F32) + on_normed * normed
    block_out = block_out + on_vec[:, 0:1] * const_vec[0] + on_vec[:, 1:2] * const_vec[1]
    block_out = block_out.astype(BF)

    pieces = first_pieces + final_pieces(grads[1])
    if fast:
        grad_experts = pack(info, pieces)
    else:
        table = jnp.stack([entry(p).astype(F32) for p in pieces]).reshape(SPLIT, GROUP, 3, depth, hidden)
        table = jnp.take(table, jnp.bitwise_xor(jnp.arange(GROUP), group), axis=1)
        grad_experts = table.transpose(3, 1, 0, 2, 4).reshape(depth, FFN_EXPERTS, 3, hidden)

    early = (early + swap_x(early)).reshape(-1)
    grad_attn_gain = early[-width:]
    sizes = [EXPERTS * width, 4 * width, 2 * width, width]
    cuts = [sum(sizes[: i + 1]) for i in range(4)]
    grad_router = early[: cuts[0]].reshape(EXPERTS, width).T
    grad_const_mix = early[cuts[0] : cuts[1]].reshape(2, 2, width)
    grad_const_vec = early[cuts[1] : cuts[2]].reshape(2, width)
    grad_moe_gain = early[cuts[2] : cuts[3]]
    grad_resid = early[cuts[3] : cuts[3] + EXPERTS * EXPERTS].reshape(EXPERTS, EXPERTS)
    return (
        block_out[None],
        grad_inputs.astype(BF)[None],
        grad_prev[None],
        grad_attn_gain,
        grad_attn[:3].transpose(1, 0, 2),
        grad_attn[3],
        grad_moe_gain,
        grad_router,
        grad_resid,
        grad_const_mix,
        grad_const_vec,
        grad_experts,
    )


def solution(mesh):
    placed = (
        P("dp", "tensor", None),
        P("dp", "tensor", None),
        P("dp", None, None),
        P("dp"),
        P("dp", "tensor", None),
        P(),
        P("dp", None, "tensor"),
        P("dp", "tensor"),
        P(),
        P(),
        P(),
        P(),
        P(),
        P("dp", None, None, "tensor"),
    )
    return jax.shard_map(
        functools.partial(per_device, mesh.shape["dp"]),
        mesh=mesh,
        in_specs=placed,
        out_specs=(
            P("dp", "tensor", None),
            P("dp", "tensor", None),
            P("dp", "tensor", None),
            P(),
            P("dp", None, "tensor"),
            P("dp", "tensor"),
            P(),
            P(),
            P(),
            P(),
            P(),
            P("dp", None, None, "tensor"),
        ),
        check_vma=False,
    )
```

```python
import functools

import jax
import jax.numpy as jnp
from jax import lax
from jax.experimental import pallas as pl
from jax.experimental.pallas import tpu as pltpu
from jax.sharding import PartitionSpec as P

HEAD_DIM = 64
FFN_EXPERTS = 8
EXPERTS = 12
CAP = 256
EPS = 1e-05
THETA = 10000.0
HIGHEST = lax.Precision.HIGHEST
BF = jnp.bfloat16
F32 = jnp.float32
NEG = float("-inf")
MIB = 1 << 20
GROUP = 4
SPLIT = FFN_EXPERTS // GROUP
EXTRA = 128


def params(mib):
    return pltpu.CompilerParams(vmem_limit_bytes=mib * MIB)


def mm(a, b):
    return jnp.dot(a, b, preferred_element_type=F32)


def mm_nt(a, b):
    return lax.dot_general(a, b, (((1,), (1,)), ((), ())), preferred_element_type=F32)


def mm_tn(a, b):
    return lax.dot_general(a, b, (((0,), (0,)), ((), ())), preferred_element_type=F32)


def full_spec(shape):
    zeros = (0,) * len(shape)
    return pl.BlockSpec(shape, lambda *ids: zeros)


def swap_x(value):
    return lax.ppermute(value, "tensor", [(0, 1), (1, 0)])


def swap_dp(value, count, mask):
    return lax.ppermute(value, "dp", [(i, i ^ mask) for i in range(count)])


def after(value, *earlier):
    return lax.optimization_barrier((value, earlier))[0]


def meet(*values):
    return lax.optimization_barrier(values)


def pick(blocks, index):
    return lax.dynamic_index_in_dim(blocks, index, 0, keepdims=False)


def chain(values, swap):
    done = []
    for value in values:
        done.append(swap(after(value, done[-1]) if done else value))
    return done


def add_low(*terms):
    total = terms[0].astype(F32)
    for term in terms[1:]:
        total = total + term.astype(F32)
    return total


def halve(blocks, bits, bit, rank, count):
    place = bits.index(bit)
    high, low = 2**place, 2 ** (len(bits) - place - 1)
    pair = blocks.reshape((high, 2, low) + blocks.shape[1:])
    side = (rank >> bit) & 1
    send = lax.dynamic_index_in_dim(pair, 1 - side, 1, keepdims=False)
    keep = lax.dynamic_index_in_dim(pair, side, 1, keepdims=False)
    total = add_low(keep, swap_dp(send, count, 1 << bit)).astype(BF)
    return total.reshape((high * low,) + blocks.shape[1:])


def scatter_bits(blocks, order, rank, count):
    bits = list(range(count.bit_length() - 1))[::-1]
    for bit in order:
        blocks = halve(blocks, bits, bit, rank, count)
        bits.remove(bit)
    return blocks


def sum_all(value, count):
    bit = 1
    while bit < count:
        value = value + swap_dp(value, count, bit)
        bit *= 2
    return value + swap_x(value)


FAR = 2


def share_group(own, count):
    other = swap_x(own)
    far_own = swap_dp(own, count, FAR)
    far_other = swap_dp(other, count, FAR)
    near = [swap_dp(v, count, 1) for v in (own, other, far_own, far_other)]
    return [own, other, near[0], near[1], far_own, far_other, near[2], near[3]]


def share_far(pair, far, count):
    got = swap_dp(far, count, FAR)
    return [(swap_dp(pair, count, 1), 0), (got, 0), (swap_dp(got, count, 1), 1)]


def entry(item):
    return item[0][item[1] : item[1] + 1]


def turn(values, cosine, sine):
    lane = lax.broadcasted_iota(jnp.int32, values.shape, 1)
    other = jnp.where(lane % HEAD_DIM < HEAD_DIM // 2, pltpu.roll(values, 96, 1), pltpu.roll(values, 32, 1))
    return values * cosine + other * sine


def qkv_kernel(masks, info_ref, x_ref, gain_ref, w_ref, cos_ref, sin_ref, attn_ref, q_ref, k_ref, v_ref, full_ref, out_ref, other_ref, by_rank_ref):
    @pl.when(pl.program_id(0) == 0)
    def _():
        for place, mask in enumerate(masks):
            by_rank_ref[jnp.bitwise_xor(info_ref[2], mask) if len(masks) > 1 else 0] = w_ref[place]
        for part in range(3):
            full_ref[part] = by_rank_ref[:, part].reshape(full_ref.shape[1:])
        out_ref[...] = by_rank_ref[:, 3].reshape(out_ref.shape)
        other_ref[...] = by_rank_ref[:, 4].reshape(out_ref.shape)

    values = x_ref[...].astype(F32)
    inverse = lax.rsqrt(jnp.mean(values * values, axis=-1, keepdims=True) + EPS)
    attn = (values * inverse * gain_ref[...]).astype(BF)
    attn_ref[...] = attn
    width = q_ref.shape[1]
    for part, out in enumerate((q_ref, k_ref, v_ref)):
        rows = mm(attn, full_ref[part])
        if part == 2:
            out[...] = rows.astype(BF)
            continue
        for start in range(0, width, 128):
            turned = turn(rows[:, start : start + 128], cos_ref[...], sin_ref[...]).astype(BF)
            if part == 0:
                turned = turned * BF(HEAD_DIM ** -0.5)
            out[:, start : start + 128] = turned


def project(info, rows, gain, weight, masks, cosine, sine):
    length, width = rows.shape
    heads = weight.shape[-1]
    block = 256
    row_spec = lambda n: pl.BlockSpec((block, n), lambda i, info: (i, 0))
    return pl.pallas_call(
        functools.partial(qkv_kernel, masks),
        grid_spec=pltpu.PrefetchScalarGridSpec(
            num_scalar_prefetch=1,
            grid=(length // block,),
            in_specs=[
                row_spec(width),
                full_spec((1, width)),
                full_spec(weight.shape),
                row_spec(128),
                row_spec(128),
            ],
            out_specs=[row_spec(width), row_spec(heads), row_spec(heads), row_spec(heads)]
            + [full_spec((3, width, heads))] + [full_spec((width, heads))] * 2,
            scratch_shapes=[pltpu.VMEM(weight.shape, BF)],
        ),
        out_shape=[jax.ShapeDtypeStruct((length, width), BF)]
        + [jax.ShapeDtypeStruct((length, heads), BF)] * 3
        + [jax.ShapeDtypeStruct((3, width, heads), BF)]
        + [jax.ShapeDtypeStruct((width, heads), BF)] * 2,
        compiler_params=params(40),
        name="project",
    )(info, rows, gain, weight, cosine, sine)


BLOCK = 256


def head_scores(query, k_ref, bias_ref, index):
    row = lax.broadcasted_iota(jnp.int32, (BLOCK, BLOCK), 0)
    column = lax.broadcasted_iota(jnp.int32, (BLOCK, BLOCK), 1)
    parts = []
    for block in range(index + 1):
        span = pl.ds(block * BLOCK, BLOCK)
        scores = mm_nt(query, k_ref[span, :]) + bias_ref[:, span]
        if block == index:
            scores = jnp.where(column <= row, scores, NEG)
        parts.append(scores)
    return parts


def attend_kernel(q_ref, k_ref, v_ref, bias_ref, o_ref, lse_ref):
    length = q_ref.shape[0]
    lane = lax.broadcasted_iota(jnp.int32, (BLOCK, 128), 1)
    for index in range(length // BLOCK):
        rows = pl.ds(index * BLOCK, BLOCK)
        outs, totals = [], []
        for head in range(2):
            mine = (lane < HEAD_DIM) if head == 0 else (lane >= HEAD_DIM)
            query = jnp.where(mine, q_ref[rows, :], BF(0))
            parts = head_scores(query, k_ref, bias_ref, index)
            top = functools.reduce(jnp.maximum, [jnp.max(p, axis=1, keepdims=True) for p in parts])
            parts = [jnp.exp(p - top) for p in parts]
            total = functools.reduce(jnp.add, [jnp.sum(p, axis=1, keepdims=True) for p in parts])
            inverse = 1.0 / total
            out = jnp.zeros((BLOCK, 128), F32)
            for block, part in enumerate(parts):
                out = out + mm((part * inverse).astype(BF), v_ref[pl.ds(block * BLOCK, BLOCK), :])
            outs.append(out)
            totals.append(top + jnp.log(total))
        o_ref[rows, :] = jnp.where(lane < HEAD_DIM, outs[0], outs[1]).astype(BF)
        lse_ref[rows, :] = jnp.where(lane < HEAD_DIM, totals[0], totals[1])


def attend(query, key, value, bias):
    length, width = query.shape
    pair = pl.BlockSpec((length, 128), lambda p: (0, p))
    return pl.pallas_call(
        attend_kernel,
        grid=(width // 128,),
        in_specs=[pair, pair, pair, full_spec((1, length))],
        out_specs=[pair, pair],
        out_shape=[jax.ShapeDtypeStruct((length, width), BF), jax.ShapeDtypeStruct((length, width), F32)],
        compiler_params=params(40),
        name="attend",
    )(query, key, value, bias)


def attend_back_kernel(q_ref, k_ref, v_ref, g_ref, lse_ref, bias_ref, cos_ref, sin_ref, out_ref, dk_ref, dv_ref):
    length = q_ref.shape[0]
    lane = lax.broadcasted_iota(jnp.int32, (BLOCK, 128), 1)
    dk_ref[...] = jnp.zeros_like(dk_ref)
    dv_ref[...] = jnp.zeros_like(dv_ref)
    for index in range(length // BLOCK):
        rows = pl.ds(index * BLOCK, BLOCK)
        grad_query = jnp.zeros((BLOCK, 128), F32)
        for head in range(2):
            mine = (lane < HEAD_DIM) if head == 0 else (lane >= HEAD_DIM)
            query = jnp.where(mine, q_ref[rows, :], BF(0))
            grad = jnp.where(mine, g_ref[rows, :], BF(0))
            lse = lse_ref[rows, head * HEAD_DIM : head * HEAD_DIM + 1]
            probs = [jnp.exp(p - lse) for p in head_scores(query, k_ref, bias_ref, index)]
            grads = [mm_nt(grad, v_ref[pl.ds(b * BLOCK, BLOCK), :]) for b in range(index + 1)]
            delta = functools.reduce(
                jnp.add, [jnp.sum(p * g, axis=1, keepdims=True) for p, g in zip(probs, grads)]
            )
            for block in range(index + 1):
                span = pl.ds(block * BLOCK, BLOCK)
                scored = (probs[block] * (grads[block] - delta)).astype(BF)
                key = k_ref[span, :]
                grad_query = grad_query + jnp.where(mine, mm(scored, key), 0.0)
                dk_ref[span, :] += mm_tn(scored, query)
                dv_ref[span, :] += mm_tn(probs[block].astype(BF), grad)
        grad_query = grad_query * HEAD_DIM ** -0.5
        out_ref[0, rows, :] = turn(grad_query, cos_ref[rows, :], -sin_ref[rows, :]).astype(BF)
    out_ref[1] = turn(dk_ref[...], cos_ref[...], -sin_ref[...]).astype(BF)
    out_ref[2] = dv_ref[...].astype(BF)


def attend_back(query, key, value, grad, lse, bias, cosine, sine):
    length, width = query.shape
    pair = pl.BlockSpec((length, 128), lambda p: (0, p))
    return pl.pallas_call(
        attend_back_kernel,
        grid=(width // 128,),
        in_specs=[pair, pair, pair, pair, pair, full_spec((1, length)), full_spec((length, 128)), full_spec((length, 128))],
        out_specs=pl.BlockSpec((3, length, 128), lambda p: (0, 0, p)),
        out_shape=jax.ShapeDtypeStruct((3, length, width), BF),
        scratch_shapes=[pltpu.VMEM((length, 128), F32)] * 2,
        compiler_params=params(48),
        name="attend_back",
    )(query, key, value, grad, lse, bias, cosine, sine)


def slot_ids_kernel(routes_ref, rows_ref, columns_ref):
    length = routes_ref.shape[2]
    label = lax.broadcasted_iota(jnp.int32, (FFN_EXPERTS, length), 0)
    before = lax.broadcasted_iota(jnp.int32, (length, length), 0) < lax.broadcasted_iota(
        jnp.int32, (length, length), 1
    )
    before = jnp.where(before, 1.0, 0.0).astype(BF)
    for slot in range(GROUP):
        chosen = [routes_ref[slot, k : k + 1, :] == label for k in range(2)]
        member = jnp.where(chosen[0] | chosen[1], 1.0, 0.0).astype(BF)
        place = mm(member, before).astype(jnp.int32) + label * CAP
        for k in range(2):
            ids = jnp.sum(jnp.where(chosen[k], place, 0), axis=0, keepdims=True)
            routed = routes_ref[slot, k : k + 1, :] < FFN_EXPERTS
            rows_ref[slot, k : k + 1, :] = jnp.where(routed, ids, -1)
    own = jnp.concatenate([rows_ref[0], routes_ref[0]] * 2, axis=0)
    columns_ref[...] = own.T


def slot_ids(routes):
    length = routes.shape[2]
    return pl.pallas_call(
        slot_ids_kernel,
        in_specs=[full_spec(routes.shape)],
        out_specs=[full_spec(routes.shape), full_spec((length, 8))],
        grid=(1,),
        out_shape=[jax.ShapeDtypeStruct(routes.shape, jnp.int32), jax.ShapeDtypeStruct((length, 8), jnp.int32)],
        compiler_params=params(40),
        name="slot_ids",
    )(routes)


def unpack_kernel(info_ref, w_ref, near_ref, pair_ref, *far_refs):
    jobs = [(near_ref, 0, c, 0, c) for c in range(SPLIT)] + [(pair_ref, 0, c, 1, c) for c in range(SPLIT)]
    jobs += [(ref, m, 0, 2 + m, c) for c, ref in enumerate(far_refs) for m in range(2)]
    for out_ref, place, slot, member, chunk in jobs:
        expert = jnp.bitwise_xor(info_ref[0], member) * SPLIT + chunk
        for part in range(3):
            rows = pl.ds(part * FFN_EXPERTS + expert, out_ref.shape[3], stride=3 * FFN_EXPERTS)
            out_ref[place, slot, part] = w_ref[rows, :].astype(BF)


def unpack(info, weights):
    depth, _, _, hidden = weights.shape
    flat = weights.transpose(0, 2, 1, 3).reshape(depth * 3 * FFN_EXPERTS, hidden)
    tile = 128
    counts = [(1, SPLIT)] * 2 + [(2, 1)] * SPLIT
    return pl.pallas_call(
        unpack_kernel,
        grid_spec=pltpu.PrefetchScalarGridSpec(
            num_scalar_prefetch=1,
            grid=(hidden // tile,),
            in_specs=[pl.BlockSpec((flat.shape[0], tile), lambda c, info: (0, c))],
            out_specs=[pl.BlockSpec(n + (3, depth, tile), lambda c, info: (0, 0, 0, 0, c)) for n in counts],
        ),
        out_shape=[jax.ShapeDtypeStruct(n + (3, depth, hidden), BF) for n in counts],
        compiler_params=params(40),
        name="unpack",
    )(info, flat)


def pack_kernel(info_ref, *refs):
    out_ref = refs[-1]
    depth = refs[0].shape[2]
    for index, ref in enumerate(refs[:-1]):
        chunk, member = index // GROUP, index % GROUP
        expert = jnp.bitwise_xor(info_ref[0], member) * SPLIT + chunk
        for part in range(3):
            rows = pl.ds(part * FFN_EXPERTS + expert, depth, stride=3 * FFN_EXPERTS)
            out_ref[rows, :] = ref[0, part].astype(F32)


def pack(info, pieces):
    _, _, depth, hidden = pieces[0][0].shape
    tile = 128
    flat = pl.pallas_call(
        pack_kernel,
        grid_spec=pltpu.PrefetchScalarGridSpec(
            num_scalar_prefetch=1,
            grid=(hidden // tile,),
            in_specs=[
                pl.BlockSpec((1, 3, depth, tile), lambda c, info, place=place: (place, 0, 0, c))
                for _, place in pieces
            ],
            out_specs=pl.BlockSpec((depth * 3 * FFN_EXPERTS, tile), lambda c, info: (0, c)),
        ),
        out_shape=jax.ShapeDtypeStruct((depth * 3 * FFN_EXPERTS, hidden), F32),
        compiler_params=params(40),
        name="pack",
    )(info, *[p for p, _ in pieces])
    return flat.reshape(depth, 3, FFN_EXPERTS, hidden).transpose(0, 2, 1, 3)


def dispatch_kernel(with_gates, info_ref, ids_ref, *refs):
    first = (info_ref[0] * SPLIT + pl.program_id(0)) * CAP
    half_refs, outs = refs[-9:-1] if not with_gates else refs[1:9], refs[-2:] if with_gates else refs[-1:]
    half = half_refs[0].shape[0]
    for slot in range(GROUP):
        row = lax.broadcasted_iota(jnp.int32, (CAP, 2 * half), 0) + first
        one, two = row == ids_ref[slot, 0:1, :], row == ids_ref[slot, 1:2, :]
        select = jnp.where(one | two, 1.0, 0.0).astype(BF)
        rows = mm(select[:, :half], half_refs[2 * slot][...]) + mm(select[:, half:], half_refs[2 * slot + 1][...])
        outs[0][0, slot] = rows.astype(BF)
        if not with_gates:
            continue
        gates_ref = refs[0]
        weight = jnp.where(one, gates_ref[slot, 0:1, :], 0.0) + jnp.where(two, gates_ref[slot, 1:2, :], 0.0)
        sign = jnp.where(one, 1.0, 0.0) - jnp.where(two, 1.0, 0.0)
        lane = lax.broadcasted_iota(jnp.int32, (CAP, 128), 1)
        outs[1][0, slot] = jnp.where(
            lane < 64, jnp.sum(weight, axis=1, keepdims=True), jnp.sum(sign, axis=1, keepdims=True)
        )


def dispatch(info, ids, halves, gates=None):
    half, width = halves[0][0].shape[-2:]

    def half_spec(item):
        if item[1] is None:
            return full_spec((half, width))
        return pl.BlockSpec((None, half, width), lambda e, info, place=item[1]: (place, 0, 0))

    extra = [] if gates is None else [gates]
    block = lambda n: pl.BlockSpec((1, GROUP, CAP, n), lambda e, info: (e, 0, 0, 0))
    outs = [(width, BF)] + ([] if gates is None else [(128, F32)])
    return pl.pallas_call(
        functools.partial(dispatch_kernel, gates is not None),
        grid_spec=pltpu.PrefetchScalarGridSpec(
            num_scalar_prefetch=1,
            grid=(SPLIT,),
            in_specs=[full_spec(ids.shape)] + [full_spec(g.shape) for g in extra] + [half_spec(v) for v in halves],
            out_specs=[block(n) for n, _ in outs],
        ),
        out_shape=[jax.ShapeDtypeStruct((SPLIT, GROUP, CAP, n), t) for n, t in outs],
        compiler_params=params(48),
        name="dispatch",
    )(info, ids, *extra, *[v for v, _ in halves])


def split_low(value):
    high = value.astype(BF)
    rest = value - high.astype(F32)
    middle = rest.astype(BF)
    return high, middle, (rest - middle.astype(F32)).astype(BF)


def expert_kernel(info_ref, x_ref, c_ref, meta_ref, full_ref, out_ref, *refs):
    outs, (xt_ref, dt_ref, grad_ref, w_ref, y_ref, db_ref) = refs[:-6], refs[-6:]
    d_refs, y_refs = outs[:3], outs[3:]
    step = pl.program_id(0)
    width = x_ref.shape[-1]
    rows = GROUP * CAP
    x = x_ref[...].reshape(rows, width)

    @pl.when(step == 0)
    def _():
        grad = (c_ref[...].reshape(rows, width).astype(F32) * meta_ref[...].reshape(rows, 128)[:, 0:1]).astype(BF)
        grad_ref[...] = grad
        xt_ref[...] = x.T
        dt_ref[...] = grad.T
        y_ref[...] = jnp.zeros_like(y_ref)
        db_ref[...] = jnp.zeros_like(db_ref)

    columns = w_ref.shape[-1]
    for rank in range(full_ref.shape[0]):
        source = 0
        if full_ref.shape[0] > 1:
            source = (rank & ~3) + jnp.bitwise_xor(info_ref[0], rank & 3)
        w_ref[source] = full_ref[rank]
    w_gate, w_up, w_down = [w_ref[:, part].reshape(width, columns) for part in range(3)]
    grad = grad_ref[...]
    gate = mm(x, w_gate)
    up = mm(x, w_up)
    sigmoid = 1.0 / (1.0 + jnp.exp(-gate))
    silu = gate * sigmoid
    act = (silu * up).astype(BF)
    d_act = mm(grad, w_down)
    d_gate = (d_act * up * sigmoid * (1.0 + gate * (1.0 - sigmoid))).astype(BF)
    d_up = (d_act * silu).astype(BF)
    y_ref[...] += mm_nt(act, w_down)
    db_ref[...] += mm_nt(d_gate, w_gate) + mm_nt(d_up, w_up)
    shape = (out_ref.shape[0], out_ref.shape[2], columns)
    out_ref[:, 0] = mm(xt_ref[...], d_gate).astype(BF).reshape(shape)
    out_ref[:, 1] = mm(xt_ref[...], d_up).astype(BF).reshape(shape)
    out_ref[:, 2] = mm(dt_ref[...], act).astype(BF).reshape(shape)

    @pl.when(step == pl.num_programs(0) - 1)
    def _():
        meta = meta_ref[...].reshape(rows, 128)
        y = y_ref[...]
        share = jnp.sum(c_ref[...].reshape(rows, width).astype(F32) * y, axis=1, keepdims=True) * meta[:, 64:65]
        lane = lax.broadcasted_iota(jnp.int32, (rows, EXTRA), 1)
        high, middle, low = [part.astype(F32) for part in split_low(share)]
        extra = jnp.where(lane == 0, high, jnp.where(lane == 1, middle, jnp.where(lane == 2, low, 0.0))).astype(BF)
        weighted = (y * meta[:, 0:1]).astype(BF)
        back = db_ref[...].astype(BF)
        for slot in range(GROUP):
            span = slice(slot * CAP, (slot + 1) * CAP)
            to, place = min(slot, 2), max(slot - 2, 0)
            d_refs[to][place, :, :width] = back[span]
            d_refs[to][place, :, width:] = extra[span]
            y_refs[to][place] = weighted[span]


def experts(info, rows, cotangents, meta, full, chunk, lead):
    width = rows.shape[-1]
    ranks, _, depth, hidden = full.shape
    tile = 256
    piece = width // lead
    count = GROUP * CAP
    row_spec = lambda n: pl.BlockSpec(
        (1, GROUP, CAP, n), lambda f, info: (chunk, 0, 0, 0), pipeline_mode=pl.Buffered(1)
    )
    shapes = [(n, CAP, m) for m in (width + EXTRA, width) for n in (1, 1, 2)]
    return pl.pallas_call(
        expert_kernel,
        grid_spec=pltpu.PrefetchScalarGridSpec(
            num_scalar_prefetch=1,
            grid=(hidden // tile,),
            in_specs=[row_spec(width), row_spec(width), row_spec(128)]
            + [pl.BlockSpec((ranks, 3, depth, tile), lambda f, info: (0, 0, 0, f))],
            out_specs=[pl.BlockSpec((lead, 3, piece, tile), lambda f, info: (0, 0, 0, f))]
            + [pl.BlockSpec(shape, lambda f, info: (0, 0, 0)) for shape in shapes],
            scratch_shapes=[
                pltpu.VMEM((width, count), BF),
                pltpu.VMEM((width, count), BF),
                pltpu.VMEM((count, width), BF),
                pltpu.VMEM((width // depth, 3, depth, tile), BF),
                pltpu.VMEM((count, width), F32),
                pltpu.VMEM((count, width), F32),
            ],
        ),
        out_shape=[jax.ShapeDtypeStruct((lead, 3, piece, hidden), BF)]
        + [jax.ShapeDtypeStruct(shape, BF) for shape in shapes],
        compiler_params=params(60),
        name="experts",
    )(info, rows, cotangents, meta, full)


def combine_kernel(info_ref, ids_ref, *refs):
    row_refs, outs = refs[: SPLIT * GROUP], refs[SPLIT * GROUP :]
    block = ids_ref.shape[0]
    width = sum(ref.shape[1] for ref in outs)
    column = lax.broadcasted_iota(jnp.int32, (block, CAP), 1)
    one = jnp.broadcast_to(ids_ref[:, 0:1], (block, CAP)) - column
    two = jnp.broadcast_to(ids_ref[:, 1:2], (block, CAP)) - column
    total = jnp.zeros((block, width), F32)
    for index, rows in enumerate(row_refs):
        member, chunk = index // SPLIT, index % SPLIT
        expert = jnp.bitwise_xor(info_ref[0], member) * SPLIT + chunk
        select = jnp.where((one == expert * CAP) | (two == expert * CAP), 1.0, 0.0).astype(BF)
        total = total + mm(select, rows[0])
    first = 0
    for ref in outs:
        ref[...] = total[:, first : first + ref.shape[1]].astype(ref.dtype)
        first += ref.shape[1]


def combine(info, ids, rows, outs):
    length = ids.shape[0]
    width = sum(n for n, _ in outs)
    block = 256

    def row_spec(item):
        return pl.BlockSpec((1, CAP, width), lambda i, info, place=item[1]: (place, 0, 0))

    return pl.pallas_call(
        combine_kernel,
        grid_spec=pltpu.PrefetchScalarGridSpec(
            num_scalar_prefetch=1,
            grid=(length // block,),
            in_specs=[pl.BlockSpec((block, 8), lambda i, info: (i, 0))]
            + [row_spec(item) for item in rows],
            out_specs=[pl.BlockSpec((block, n), lambda i, info: (i, 0)) for n, _ in outs],
        ),
        out_shape=[jax.ShapeDtypeStruct((length, n), t) for n, t in outs],
        compiler_params=params(48),
        name="combine",
    )(info, ids, *[item[0] for item in rows])


def per_device(
    count,
    inputs,
    prev_logits,
    routes,
    lengths,
    cotangent,
    attn_gain,
    w_qkv,
    w_out,
    moe_gain,
    w_router,
    w_resid,
    const_mix,
    const_vec,
    w_experts,
):
    half, width = inputs.shape[1:]
    length = routes.shape[1]
    depth = w_experts.shape[0]
    hidden = w_experts.shape[3]
    heads = w_out.shape[1]
    t_rank = lax.axis_index("tensor")
    d_rank = lax.axis_index("dp")
    bit = lambda n: (d_rank >> n) & 1
    group = d_rank % GROUP
    fast = count == 16 and depth % 16 == 0
    info = jnp.stack([group, bit(2), d_rank]).astype(jnp.int32)
    first_row = t_rank * half
    length_here = lengths[0]

    def in_order(own, other):
        return jnp.where(t_rank == 0, jnp.concatenate([own, other]), jnp.concatenate([other, own]))

    own_in = inputs[0]
    other_in = swap_x(own_in)

    own_routes = routes.transpose(0, 2, 1)
    far_routes = jnp.concatenate([own_routes, swap_dp(own_routes, count, FAR)])

    out_low = w_out.astype(BF)[None]
    attn_shard = jnp.concatenate([w_qkv.transpose(1, 0, 2).astype(BF), out_low, swap_x(out_low)])
    lines = [[i + GROUP * j for j in range(count // GROUP)] for i in range(GROUP)]
    attn_rows, rank_masks = attn_shard[None], [0]
    weights = []

    def double(rows, masks, n):
        got = swap_dp(rows, count, 1 << n)
        return jnp.concatenate([rows, got]), masks + [mask | (1 << n) for mask in masks], got

    def expert_rows(e, got):
        passed = swap_dp(got, count, 1)
        return jnp.concatenate([mine[0][:, e], pair[:, e], got[:1, 0], passed[1:, 0]])

    if fast:
        mine = list(unpack(info, w_experts))
        pair = swap_dp(mine[1], count, 1)
        for n in (3, 2):
            attn_rows, rank_masks, _ = double(attn_rows, rank_masks, n)
        got = swap_dp(mine[2], count, FAR)
        got, attn_rows, mine[3], other_in = meet(got, attn_rows, mine[3], other_in)
        attn_rows, rank_masks, attn_got = double(attn_rows, rank_masks, 1)
        first_quad = expert_rows(0, got)
        weights.append(lax.all_gather(first_quad, "dp", axis=0, tiled=True, axis_index_groups=lines))
        attn_rows, rank_masks, _ = double(attn_rows, rank_masks, 0)
    else:
        attn_rows = lax.all_gather(attn_shard, "dp", axis=1, tiled=True)[None]
        expert_low = w_experts.astype(BF).reshape(depth, GROUP, SPLIT, 3, hidden).transpose(1, 2, 3, 0, 4)
        gathered = pick(lax.all_gather(expert_low, "dp", axis=3, tiled=True), group)
        weights = [gathered[e][None] for e in range(SPLIT)]

    near_routes = swap_dp(far_routes, count, 1)
    all_routes = jnp.stack([far_routes[0], near_routes[0], far_routes[1], near_routes[1]])
    turned = jnp.concatenate([all_routes[:, :, half:], all_routes[:, :, :half]], axis=2)
    ids_rows, ids_own = slot_ids(jnp.where(t_rank == 0, all_routes, turned))
    all_in = in_order(own_in, other_in)
    row_place = first_row + jnp.arange(half, dtype=jnp.int32)
    live = (row_place < length_here)[:, None]
    cot_own = jnp.where(live, cotangent[0], BF(0))
    cot_other = swap_x(after(cot_own, other_in))
    far_cot = [swap_dp(after(cot_own, mine) if fast else cot_own, count, FAR)]
    inv_freq = THETA ** (-jnp.arange(HEAD_DIM // 2, dtype=F32) / (HEAD_DIM // 2))
    angles = jnp.arange(length, dtype=F32)[:, None] * inv_freq[None, :]
    cosine = jnp.tile(jnp.cos(angles), (1, 4))
    sine = jnp.sin(angles)
    sine = jnp.tile(jnp.concatenate([-sine, sine], axis=1), (1, 2))
    bias = jnp.where(jnp.arange(length, dtype=jnp.int32) < length_here, 0.0, NEG)[None, :].astype(F32)

    if fast:
        all_in = after(all_in, first_quad)
    attn, query, key, value, attn_full, out_own, out_other = project(
        info, all_in, attn_gain[None], attn_rows, rank_masks, cosine, sine
    )
    far_cot.append(swap_dp(after(cot_other, query), count, FAR))
    attended, lse = attend(query, key, value, bias)
    att_own = lax.dynamic_slice_in_dim(attended, first_row, half, 0)
    att_send = lax.dynamic_slice_in_dim(attended, half - first_row, half, 0)
    att_other = swap_x(att_send)
    near_cot = chain(after([cot_own, cot_other, far_cot[0]], attended), lambda v: swap_dp(v, count, 1))
    if fast:
        rows = expert_rows(1, after(swap_dp(mine[3], count, FAR), attended))
        weights.append(lax.all_gather(rows, "dp", axis=0, tiled=True, axis_index_groups=lines))
    att_other = after(att_other, near_cot)
    near_cot.append(swap_dp(far_cot[1], count, 1))
    resid_in = own_in.astype(F32)
    resid_mid = resid_in + mm_nt(att_own, out_own) + mm_nt(att_other, out_other)

    inv_two = lax.rsqrt(jnp.mean(resid_mid * resid_mid, axis=-1, keepdims=True) + EPS)
    normed = resid_mid * inv_two * moe_gain
    moe_own = normed.astype(BF)
    moe_other = swap_x(moe_own)
    far_moe = [swap_dp(moe_own, count, FAR)]
    prev_rows = prev_logits[0]
    cot_halves = [cot_own, cot_other] + near_cot[:2] + far_cot + near_cot[2:]
    (cot_rows,) = dispatch(info, ids_rows, [(v, None) for v in after(cot_halves, moe_own)])
    small_w = jnp.concatenate([w_router, const_mix.reshape(4, width).T], axis=1)
    small = jnp.dot(normed, small_w, precision=HIGHEST)
    logits = small[:, :EXPERTS] + jnp.dot(prev_rows, w_resid, precision=HIGHEST)
    route_own = ids_own[:half, 2:4]
    labels = jnp.arange(EXPERTS, dtype=jnp.int32)
    onehot = (route_own[:, :, None] == labels).astype(F32)
    chosen = jnp.sum(onehot * logits[:, None, :], axis=-1)
    top = jnp.max(chosen, axis=-1, keepdims=True)
    gate_weight = jnp.exp(chosen - top)
    gate_weight = gate_weight / jnp.sum(gate_weight, axis=-1, keepdims=True)
    mix = small[:, EXPERTS:].reshape(half, 2, 2)
    mix = jnp.exp(mix - jnp.max(mix, axis=-1, keepdims=True))
    mix = mix / jnp.sum(mix, axis=-1, keepdims=True)
    gate_t = gate_weight.T
    gates = jnp.stack([gate_t, swap_dp(gate_t, count, FAR)])
    gates = jnp.concatenate([gates, swap_x(gates)], axis=2)
    gates = jnp.stack([gates, swap_dp(gates, count, 1)], axis=1).reshape(GROUP, 2, length)

    far_moe.append(swap_dp(after(moe_other, gates), count, FAR))
    near_moe = jnp.stack([moe_own, moe_other, after(far_moe[0], cot_rows)])
    near_moe = swap_dp(near_moe, count, 1)
    is_copy = onehot[:, :, FFN_EXPERTS + 1]
    is_const = onehot[:, :, FFN_EXPERTS + 2 :]
    w_copy = jnp.sum(gate_weight * is_copy, axis=1, keepdims=True)
    w_const = jnp.sum(gate_weight[:, :, None] * is_const, axis=1)
    on_normed = w_copy + jnp.sum(w_const * mix[:, :, 0], axis=1, keepdims=True)
    on_vec = w_const * mix[:, :, 1]
    grad_top = cot_own.astype(F32)
    dot_normed = jnp.sum(grad_top * normed, axis=1, keepdims=True)
    dot_vec = jnp.stack([jnp.sum(grad_top * const_vec[j], axis=1) for j in range(2)], axis=1)
    const_gate = mix[:, :, 0] * dot_normed + mix[:, :, 1] * dot_vec
    special = is_copy * dot_normed + jnp.sum(is_const * const_gate[:, None, :], axis=-1)
    d_mix = jnp.stack([w_const * dot_normed, w_const * dot_vec], axis=-1)
    d_mix = mix * (d_mix - jnp.sum(mix * d_mix, axis=-1, keepdims=True))
    special = special[:, 0] - special[:, 1]
    gate_product = gate_weight[:, 0] * gate_weight[:, 1]
    d_mix = d_mix.reshape(half, 4)
    far_moe[1], special, gate_product, d_mix, on_normed, on_vec = meet(
        far_moe[1], special, gate_product, d_mix, on_normed, on_vec
    )
    near_last = swap_dp(far_moe[1], count, 1)
    moe_halves = [(moe_own, None), (moe_other, None), (near_moe, 0), (near_moe, 1)]
    moe_halves += [(far_moe[0], None), (far_moe[1], None), (near_moe, 2), (near_last, None)]
    moe_rows, meta = dispatch(info, ids_rows, moe_halves, gates)
    rows_in = moe_rows
    lead = count // GROUP if fast else 1
    grads, d_sent, y_sent = [], [], []
    for e in range(SPLIT):
        blocks, *routed = experts(info, rows_in, cot_rows, meta, weights[e], e, lead)
        d_sent.append(routed[:3])
        y_sent.append(routed[3:])
        rows_in = after(rows_in, routed[0])
        if fast:
            blocks = lax.psum_scatter(blocks, "dp", scatter_dimension=0, tiled=False, axis_index_groups=lines)
        else:
            blocks = blocks.reshape(3, count, depth, hidden).transpose(1, 0, 2, 3)
            blocks = scatter_bits(blocks, range(2, count.bit_length() - 1), d_rank, count)
            blocks = blocks.transpose(1, 0, 2, 3)
        grads.append(blocks.reshape(3, GROUP, depth, hidden))
    first_rows = [(d_sent[0][0], 0)] + share_far(d_sent[0][1], d_sent[0][2], count)
    far_last = after(d_sent[1][2], first_rows[1][0], first_rows[2][0])
    last_rows = [(d_sent[1][0], 0)] + share_far(d_sent[1][1], far_last, count)
    d_rows = [r for pair in zip(first_rows, last_rows) for r in pair]
    d_low, share_other = combine(info, ids_own[half:], d_rows, [(width, BF), (EXTRA, F32)])
    d_got = swap_x(d_low)
    share_got = swap_x(jnp.sum(share_other[:, :3], axis=1))
    d_own, share_own = combine(info, after(ids_own[:half], d_low), d_rows, [(width, F32), (EXTRA, F32)])
    y_rows = [[(y[0], 0)] + share_far(after(y[1], d_own), after(y[2], d_own), count) for y in y_sent]
    y_rows = [r for pair in zip(*y_rows) for r in pair]
    d_tokens = d_own + d_got.astype(F32)
    share = jnp.sum(share_own[:, :3], axis=1) + share_got

    d_first = gate_product * (share + special)
    d_logits = d_first[:, None] * (onehot[:, 0] - onehot[:, 1])
    d_small = jnp.concatenate([d_logits, d_mix], axis=1)
    d_normed = jnp.dot(d_small, small_w.T, precision=HIGHEST) + on_normed * grad_top + d_tokens
    grad_moe_gain = jnp.sum(d_normed * resid_mid * inv_two, axis=0)
    scaled = moe_gain * d_normed
    d_resid = (
        grad_top
        + inv_two * scaled
        - resid_mid * (inv_two * inv_two * inv_two) * jnp.mean(scaled * resid_mid, axis=-1, keepdims=True)
    )

    def final_pieces(blocks):
        blocks = [
            lax.dynamic_index_in_dim(blocks, jnp.bitwise_xor(group, m), 1, keepdims=False)[None] for m in range(GROUP)
        ]
        return [(blocks[0], 0)] + share_far(blocks[1], jnp.concatenate(blocks[2:]), count)

    d_mixed = d_resid.astype(BF)
    d_att_low = mm(d_mixed, out_other).astype(BF)
    d_att_got = swap_x(d_att_low)
    d_late, on_vec_late = after((d_small, on_vec), d_att_low)
    grad_prev = jnp.dot(d_late[:, :EXPERTS], w_resid.T, precision=HIGHEST)
    grad_resid = jnp.dot(prev_rows.T, d_late[:, :EXPERTS], precision=HIGHEST)
    grad_small = jnp.dot(d_late.T, normed, precision=HIGHEST)
    grad_const_vec = jnp.dot(on_vec_late.T, grad_top, precision=HIGHEST)
    d_att_own = mm(after(d_mixed, d_att_low), out_own).astype(BF)
    attn_late = after(attn, d_att_low)
    first_pieces = final_pieces(after(grads[0], d_att_low))
    d_att_other = d_att_got
    d_attended = in_order(d_att_own, d_att_other)
    d_mixed_other = swap_x(after(d_mixed, d_att_got))
    d_qkv = attend_back(query, key, value, d_attended, lse, bias, cosine, sine)
    d_mixed_all = in_order(d_mixed, after(d_mixed_other, d_qkv))
    grad_out = mm_tn(d_mixed_all, attended)
    grad_qkv = jnp.stack([mm_tn(attn_late, d_qkv[k]) for k in range(3)] + [grad_out])
    blocks = grad_qkv.astype(BF).reshape(4, count, depth, heads).transpose(1, 0, 2, 3)
    bits = list(range(count.bit_length() - 1))[::-1]
    blocks, *arrived = meet(blocks, *[p for p, _ in first_pieces])
    first_pieces = [(p, place) for p, (_, place) in zip(arrived, first_pieces)]
    stage = halve(blocks, bits, 0, d_rank, count)
    bits.remove(0)
    d_attn = sum(mm_nt(d_qkv[k], attn_full[k]) for k in range(3))
    values = all_in.astype(F32)
    inv_all = lax.rsqrt(jnp.mean(values * values, axis=-1, keepdims=True) + EPS)
    grad_attn_gain = jnp.sum(d_attn * values * inv_all, axis=0)
    d_attn_own = lax.dynamic_slice_in_dim(d_attn, first_row, half, 0)
    d_attn_other = lax.dynamic_slice_in_dim(d_attn, half - first_row, half, 0).astype(BF)
    d_attn_got = swap_x(d_attn_other)
    y_ids = after(ids_own, d_attn_other)
    (y_low,) = combine(info, y_ids[half:], y_rows, [(width, BF)])
    y_got = swap_x(y_low)
    (y_own,) = combine(info, after(y_ids[:half], y_low), y_rows, [(width, F32)])
    inv_one = lax.rsqrt(jnp.mean(resid_in * resid_in, axis=-1, keepdims=True) + EPS)
    early = jnp.concatenate(
        [
            grad_small.reshape(-1),
            grad_const_vec.reshape(-1),
            grad_moe_gain,
            jnp.pad(grad_resid.reshape(-1), (0, 112)),
            grad_attn_gain,
        ]
    )
    early = early.reshape(-1, 128)
    last_grad = grads[1]
    stage, early = meet(stage, early)
    hops = [[0, 1], [2], [3] + list(range(4, count.bit_length() - 1))] + [[]] * count
    for n in bits[::-1]:
        stage = halve(stage, bits, n, d_rank, count)
        bits.remove(n)
        for hop in hops.pop(0):
            early = early + swap_dp(early, count, 1 << hop)
        stage, early = meet(stage, early)
        if n == 2:
            stage, d_attn_got, last_grad = meet(stage, d_attn_got, last_grad)
        if n == 3:
            stage, y_got = meet(stage, y_got)
    early = early + swap_x(early)
    grad_attn = stage[0].astype(F32)
    d_attn_own = d_attn_own + d_attn_got.astype(F32)
    scaled = attn_gain * d_attn_own
    grad_inputs = (
        d_resid
        + inv_one * scaled
        - resid_in * (inv_one * inv_one * inv_one) * jnp.mean(scaled * resid_in, axis=-1, keepdims=True)
    )

    block_out = resid_mid + y_own + y_got.astype(F32) + on_normed * normed
    block_out = block_out + on_vec[:, 0:1] * const_vec[0] + on_vec[:, 1:2] * const_vec[1]
    block_out = block_out.astype(BF)

    pieces = first_pieces + final_pieces(last_grad)
    if fast:
        grad_experts = pack(info, pieces)
    else:
        table = jnp.stack([entry(p).astype(F32) for p in pieces]).reshape(SPLIT, GROUP, 3, depth, hidden)
        table = jnp.take(table, jnp.bitwise_xor(jnp.arange(GROUP), group), axis=1)
        grad_experts = table.transpose(3, 1, 0, 2, 4).reshape(depth, FFN_EXPERTS, 3, hidden)

    early = early.reshape(-1)
    grad_attn_gain = early[-width:]
    sizes = [EXPERTS * width, 4 * width, 2 * width, width]
    cuts = [sum(sizes[: i + 1]) for i in range(4)]
    grad_router = early[: cuts[0]].reshape(EXPERTS, width).T
    grad_const_mix = early[cuts[0] : cuts[1]].reshape(2, 2, width)
    grad_const_vec = early[cuts[1] : cuts[2]].reshape(2, width)
    grad_moe_gain = early[cuts[2] : cuts[3]]
    grad_resid = early[cuts[3] : cuts[3] + EXPERTS * EXPERTS].reshape(EXPERTS, EXPERTS)
    return (
        block_out[None],
        grad_inputs.astype(BF)[None],
        grad_prev[None],
        grad_attn_gain,
        grad_attn[:3].transpose(1, 0, 2),
        grad_attn[3],
        grad_moe_gain,
        grad_router,
        grad_resid,
        grad_const_mix,
        grad_const_vec,
        grad_experts,
    )


def solution(mesh):
    placed = (
        P("dp", "tensor", None),
        P("dp", "tensor", None),
        P("dp", None, None),
        P("dp"),
        P("dp", "tensor", None),
        P(),
        P("dp", None, "tensor"),
        P("dp", "tensor"),
        P(),
        P(),
        P(),
        P(),
        P(),
        P("dp", None, None, "tensor"),
    )
    return jax.shard_map(
        functools.partial(per_device, mesh.shape["dp"]),
        mesh=mesh,
        in_specs=placed,
        out_specs=(
            P("dp", "tensor", None),
            P("dp", "tensor", None),
            P("dp", "tensor", None),
            P(),
            P("dp", None, "tensor"),
            P("dp", "tensor"),
            P(),
            P(),
            P(),
            P(),
            P(),
            P("dp", None, None, "tensor"),
        ),
        check_vma=False,
    )
```

```python
import functools

import jax
import jax.numpy as jnp
from jax import lax
from jax.experimental import pallas as pl
from jax.experimental.pallas import tpu as pltpu
from jax.sharding import PartitionSpec as P

HEAD_DIM = 64
FFN_EXPERTS = 8
EXPERTS = 12
CAP = 256
EPS = 1e-05
THETA = 10000.0
HIGHEST = lax.Precision.HIGHEST
BF = jnp.bfloat16
F32 = jnp.float32
NEG = float("-inf")
MIB = 1 << 20
GROUP = 4
SPLIT = FFN_EXPERTS // GROUP
EXTRA = 128


def params(mib):
    return pltpu.CompilerParams(vmem_limit_bytes=mib * MIB)


def mm(a, b):
    return jnp.dot(a, b, preferred_element_type=F32)


def mm_nt(a, b):
    return lax.dot_general(a, b, (((1,), (1,)), ((), ())), preferred_element_type=F32)


def mm_tn(a, b):
    return lax.dot_general(a, b, (((0,), (0,)), ((), ())), preferred_element_type=F32)


def full_spec(shape):
    zeros = (0,) * len(shape)
    return pl.BlockSpec(shape, lambda *ids: zeros)


def swap_x(value):
    return lax.ppermute(value, "tensor", [(0, 1), (1, 0)])


def swap_dp(value, count, mask):
    return lax.ppermute(value, "dp", [(i, i ^ mask) for i in range(count)])


def after(value, *earlier):
    return lax.optimization_barrier((value, earlier))[0]


def meet(*values):
    return lax.optimization_barrier(values)


def pick(blocks, index):
    return lax.dynamic_index_in_dim(blocks, index, 0, keepdims=False)


def chain(values, swap):
    done = []
    for value in values:
        done.append(swap(after(value, done[-1]) if done else value))
    return done


def add_low(*terms):
    total = terms[0].astype(F32)
    for term in terms[1:]:
        total = total + term.astype(F32)
    return total


def halve(blocks, bits, bit, rank, count):
    place = bits.index(bit)
    high, low = 2**place, 2 ** (len(bits) - place - 1)
    pair = blocks.reshape((high, 2, low) + blocks.shape[1:])
    side = (rank >> bit) & 1
    send = lax.dynamic_index_in_dim(pair, 1 - side, 1, keepdims=False)
    keep = lax.dynamic_index_in_dim(pair, side, 1, keepdims=False)
    total = add_low(keep, swap_dp(send, count, 1 << bit)).astype(BF)
    return total.reshape((high * low,) + blocks.shape[1:])


def scatter_bits(blocks, order, rank, count):
    bits = list(range(count.bit_length() - 1))[::-1]
    for bit in order:
        blocks = halve(blocks, bits, bit, rank, count)
        bits.remove(bit)
    return blocks


def sum_all(value, count):
    bit = 1
    while bit < count:
        value = value + swap_dp(value, count, bit)
        bit *= 2
    return value + swap_x(value)


FAR = 2


def share_group(own, count):
    other = swap_x(own)
    far_own = swap_dp(own, count, FAR)
    far_other = swap_dp(other, count, FAR)
    near = [swap_dp(v, count, 1) for v in (own, other, far_own, far_other)]
    return [own, other, near[0], near[1], far_own, far_other, near[2], near[3]]


def share_all(parts, count):
    return [(swap_dp(part, count, mask), 0) for mask, part in enumerate(parts, 1)]


def share_far(pair, far, count):
    got = swap_dp(far, count, FAR)
    return [(swap_dp(pair, count, 1), 0), (got, 0), (swap_dp(got, count, 1), 1)]


def entry(item):
    return item[0][item[1] : item[1] + 1]


def turn(values, cosine, sine):
    lane = lax.broadcasted_iota(jnp.int32, values.shape, 1)
    other = jnp.where(lane % HEAD_DIM < HEAD_DIM // 2, pltpu.roll(values, 96, 1), pltpu.roll(values, 32, 1))
    return values * cosine + other * sine


def qkv_kernel(masks, info_ref, x_ref, gain_ref, w_ref, cos_ref, sin_ref, attn_ref, q_ref, k_ref, v_ref, full_ref, out_ref, other_ref, by_rank_ref):
    @pl.when(pl.program_id(0) == 0)
    def _():
        for place, mask in enumerate(masks):
            by_rank_ref[jnp.bitwise_xor(info_ref[2], mask) if len(masks) > 1 else 0] = w_ref[place]
        for part in range(3):
            full_ref[part] = by_rank_ref[:, part].reshape(full_ref.shape[1:])
        out_ref[...] = by_rank_ref[:, 3].reshape(out_ref.shape)
        other_ref[...] = by_rank_ref[:, 4].reshape(out_ref.shape)

    values = x_ref[...].astype(F32)
    inverse = lax.rsqrt(jnp.mean(values * values, axis=-1, keepdims=True) + EPS)
    attn = (values * inverse * gain_ref[...]).astype(BF)
    attn_ref[...] = attn
    width = q_ref.shape[1]
    for part, out in enumerate((q_ref, k_ref, v_ref)):
        rows = mm(attn, full_ref[part])
        if part == 2:
            out[...] = rows.astype(BF)
            continue
        for start in range(0, width, 128):
            turned = turn(rows[:, start : start + 128], cos_ref[...], sin_ref[...]).astype(BF)
            if part == 0:
                turned = turned * BF(HEAD_DIM ** -0.5)
            out[:, start : start + 128] = turned


def project(info, rows, gain, weight, masks, cosine, sine):
    length, width = rows.shape
    heads = weight.shape[-1]
    block = 256
    row_spec = lambda n: pl.BlockSpec((block, n), lambda i, info: (i, 0))
    return pl.pallas_call(
        functools.partial(qkv_kernel, masks),
        grid_spec=pltpu.PrefetchScalarGridSpec(
            num_scalar_prefetch=1,
            grid=(length // block,),
            in_specs=[
                row_spec(width),
                full_spec((1, width)),
                full_spec(weight.shape),
                row_spec(128),
                row_spec(128),
            ],
            out_specs=[row_spec(width), row_spec(heads), row_spec(heads), row_spec(heads)]
            + [full_spec((3, width, heads))] + [full_spec((width, heads))] * 2,
            scratch_shapes=[pltpu.VMEM(weight.shape, BF)],
        ),
        out_shape=[jax.ShapeDtypeStruct((length, width), BF)]
        + [jax.ShapeDtypeStruct((length, heads), BF)] * 3
        + [jax.ShapeDtypeStruct((3, width, heads), BF)]
        + [jax.ShapeDtypeStruct((width, heads), BF)] * 2,
        compiler_params=params(40),
        name="project",
    )(info, rows, gain, weight, cosine, sine)


BLOCK = 256


def head_scores(query, k_ref, bias_ref, index):
    row = lax.broadcasted_iota(jnp.int32, (BLOCK, BLOCK), 0)
    column = lax.broadcasted_iota(jnp.int32, (BLOCK, BLOCK), 1)
    parts = []
    for block in range(index + 1):
        span = pl.ds(block * BLOCK, BLOCK)
        scores = mm_nt(query, k_ref[span, :]) + bias_ref[:, span]
        if block == index:
            scores = jnp.where(column <= row, scores, NEG)
        parts.append(scores)
    return parts


def attend_kernel(q_ref, k_ref, v_ref, bias_ref, o_ref, lse_ref):
    length = q_ref.shape[0]
    lane = lax.broadcasted_iota(jnp.int32, (BLOCK, 128), 1)
    for index in range(length // BLOCK):
        rows = pl.ds(index * BLOCK, BLOCK)
        outs, totals = [], []
        for head in range(2):
            mine = (lane < HEAD_DIM) if head == 0 else (lane >= HEAD_DIM)
            query = jnp.where(mine, q_ref[rows, :], BF(0))
            parts = head_scores(query, k_ref, bias_ref, index)
            top = functools.reduce(jnp.maximum, [jnp.max(p, axis=1, keepdims=True) for p in parts])
            parts = [jnp.exp(p - top) for p in parts]
            total = functools.reduce(jnp.add, [jnp.sum(p, axis=1, keepdims=True) for p in parts])
            inverse = 1.0 / total
            out = jnp.zeros((BLOCK, 128), F32)
            for block, part in enumerate(parts):
                out = out + mm((part * inverse).astype(BF), v_ref[pl.ds(block * BLOCK, BLOCK), :])
            outs.append(out)
            totals.append(top + jnp.log(total))
        o_ref[rows, :] = jnp.where(lane < HEAD_DIM, outs[0], outs[1]).astype(BF)
        lse_ref[rows, :] = jnp.where(lane < HEAD_DIM, totals[0], totals[1])


def attend(query, key, value, bias):
    length, width = query.shape
    pair = pl.BlockSpec((length, 128), lambda p: (0, p))
    return pl.pallas_call(
        attend_kernel,
        grid=(width // 128,),
        in_specs=[pair, pair, pair, full_spec((1, length))],
        out_specs=[pair, pair],
        out_shape=[jax.ShapeDtypeStruct((length, width), BF), jax.ShapeDtypeStruct((length, width), F32)],
        compiler_params=params(40),
        name="attend",
    )(query, key, value, bias)


def attend_back_kernel(q_ref, k_ref, v_ref, g_ref, lse_ref, bias_ref, cos_ref, sin_ref, out_ref, dk_ref, dv_ref):
    length = q_ref.shape[0]
    lane = lax.broadcasted_iota(jnp.int32, (BLOCK, 128), 1)
    dk_ref[...] = jnp.zeros_like(dk_ref)
    dv_ref[...] = jnp.zeros_like(dv_ref)
    for index in range(length // BLOCK):
        rows = pl.ds(index * BLOCK, BLOCK)
        grad_query = jnp.zeros((BLOCK, 128), F32)
        for head in range(2):
            mine = (lane < HEAD_DIM) if head == 0 else (lane >= HEAD_DIM)
            query = jnp.where(mine, q_ref[rows, :], BF(0))
            grad = jnp.where(mine, g_ref[rows, :], BF(0))
            lse = lse_ref[rows, head * HEAD_DIM : head * HEAD_DIM + 1]
            probs = [jnp.exp(p - lse) for p in head_scores(query, k_ref, bias_ref, index)]
            grads = [mm_nt(grad, v_ref[pl.ds(b * BLOCK, BLOCK), :]) for b in range(index + 1)]
            delta = functools.reduce(
                jnp.add, [jnp.sum(p * g, axis=1, keepdims=True) for p, g in zip(probs, grads)]
            )
            for block in range(index + 1):
                span = pl.ds(block * BLOCK, BLOCK)
                scored = (probs[block] * (grads[block] - delta)).astype(BF)
                key = k_ref[span, :]
                grad_query = grad_query + jnp.where(mine, mm(scored, key), 0.0)
                dk_ref[span, :] += mm_tn(scored, query)
                dv_ref[span, :] += mm_tn(probs[block].astype(BF), grad)
        grad_query = grad_query * HEAD_DIM ** -0.5
        out_ref[0, rows, :] = turn(grad_query, cos_ref[rows, :], -sin_ref[rows, :]).astype(BF)
    out_ref[1] = turn(dk_ref[...], cos_ref[...], -sin_ref[...]).astype(BF)
    out_ref[2] = dv_ref[...].astype(BF)


def attend_back(query, key, value, grad, lse, bias, cosine, sine):
    length, width = query.shape
    pair = pl.BlockSpec((length, 128), lambda p: (0, p))
    return pl.pallas_call(
        attend_back_kernel,
        grid=(width // 128,),
        in_specs=[pair, pair, pair, pair, pair, full_spec((1, length)), full_spec((length, 128)), full_spec((length, 128))],
        out_specs=pl.BlockSpec((3, length, 128), lambda p: (0, 0, p)),
        out_shape=jax.ShapeDtypeStruct((3, length, width), BF),
        scratch_shapes=[pltpu.VMEM((length, 128), F32)] * 2,
        compiler_params=params(48),
        name="attend_back",
    )(query, key, value, grad, lse, bias, cosine, sine)


def slot_ids_kernel(routes_ref, rows_ref, columns_ref):
    length = routes_ref.shape[2]
    label = lax.broadcasted_iota(jnp.int32, (FFN_EXPERTS, length), 0)
    before = lax.broadcasted_iota(jnp.int32, (length, length), 0) < lax.broadcasted_iota(
        jnp.int32, (length, length), 1
    )
    before = jnp.where(before, 1.0, 0.0).astype(BF)
    for slot in range(GROUP):
        chosen = [routes_ref[slot, k : k + 1, :] == label for k in range(2)]
        member = jnp.where(chosen[0] | chosen[1], 1.0, 0.0).astype(BF)
        place = mm(member, before).astype(jnp.int32) + label * CAP
        for k in range(2):
            ids = jnp.sum(jnp.where(chosen[k], place, 0), axis=0, keepdims=True)
            routed = routes_ref[slot, k : k + 1, :] < FFN_EXPERTS
            rows_ref[slot, k : k + 1, :] = jnp.where(routed, ids, -1)
    own = jnp.concatenate([rows_ref[0], routes_ref[0]] * 2, axis=0)
    columns_ref[...] = own.T


def slot_ids(routes):
    length = routes.shape[2]
    return pl.pallas_call(
        slot_ids_kernel,
        in_specs=[full_spec(routes.shape)],
        out_specs=[full_spec(routes.shape), full_spec((length, 8))],
        grid=(1,),
        out_shape=[jax.ShapeDtypeStruct(routes.shape, jnp.int32), jax.ShapeDtypeStruct((length, 8), jnp.int32)],
        compiler_params=params(40),
        name="slot_ids",
    )(routes)


def unpack_kernel(info_ref, w_ref, near_ref, pair_ref, *far_refs):
    jobs = [(near_ref, 0, c, 0, c) for c in range(SPLIT)] + [(pair_ref, 0, c, 1, c) for c in range(SPLIT)]
    jobs += [(ref, m, 0, 2 + m, c) for c, ref in enumerate(far_refs) for m in range(2)]
    for out_ref, place, slot, member, chunk in jobs:
        expert = jnp.bitwise_xor(info_ref[0], member) * SPLIT + chunk
        for part in range(3):
            rows = pl.ds(part * FFN_EXPERTS + expert, out_ref.shape[3], stride=3 * FFN_EXPERTS)
            out_ref[place, slot, part] = w_ref[rows, :].astype(BF)


def unpack(info, weights):
    depth, _, _, hidden = weights.shape
    flat = weights.transpose(0, 2, 1, 3).reshape(depth * 3 * FFN_EXPERTS, hidden)
    tile = 128
    counts = [(1, SPLIT)] * 2 + [(2, 1)] * SPLIT
    return pl.pallas_call(
        unpack_kernel,
        grid_spec=pltpu.PrefetchScalarGridSpec(
            num_scalar_prefetch=1,
            grid=(hidden // tile,),
            in_specs=[pl.BlockSpec((flat.shape[0], tile), lambda c, info: (0, c))],
            out_specs=[pl.BlockSpec(n + (3, depth, tile), lambda c, info: (0, 0, 0, 0, c)) for n in counts],
        ),
        out_shape=[jax.ShapeDtypeStruct(n + (3, depth, hidden), BF) for n in counts],
        compiler_params=params(40),
        name="unpack",
    )(info, flat)


def pack_kernel(info_ref, *refs):
    out_ref = refs[-1]
    depth = refs[0].shape[2]
    for index, ref in enumerate(refs[:-1]):
        chunk, member = index // GROUP, index % GROUP
        expert = jnp.bitwise_xor(info_ref[0], member) * SPLIT + chunk
        for part in range(3):
            rows = pl.ds(part * FFN_EXPERTS + expert, depth, stride=3 * FFN_EXPERTS)
            out_ref[rows, :] = ref[0, part].astype(F32)


def pack(info, pieces):
    _, _, depth, hidden = pieces[0][0].shape
    tile = 128
    flat = pl.pallas_call(
        pack_kernel,
        grid_spec=pltpu.PrefetchScalarGridSpec(
            num_scalar_prefetch=1,
            grid=(hidden // tile,),
            in_specs=[
                pl.BlockSpec((1, 3, depth, tile), lambda c, info, place=place: (place, 0, 0, c))
                for _, place in pieces
            ],
            out_specs=pl.BlockSpec((depth * 3 * FFN_EXPERTS, tile), lambda c, info: (0, c)),
        ),
        out_shape=jax.ShapeDtypeStruct((depth * 3 * FFN_EXPERTS, hidden), F32),
        compiler_params=params(40),
        name="pack",
    )(info, *[p for p, _ in pieces])
    return flat.reshape(depth, 3, FFN_EXPERTS, hidden).transpose(0, 2, 1, 3)


def dispatch_kernel(with_gates, info_ref, ids_ref, *refs):
    first = (info_ref[0] * SPLIT + pl.program_id(0)) * CAP
    half_refs, outs = refs[-9:-1] if not with_gates else refs[1:9], refs[-2:] if with_gates else refs[-1:]
    half = half_refs[0].shape[0]
    for slot in range(GROUP):
        row = lax.broadcasted_iota(jnp.int32, (CAP, 2 * half), 0) + first
        one, two = row == ids_ref[slot, 0:1, :], row == ids_ref[slot, 1:2, :]
        select = jnp.where(one | two, 1.0, 0.0).astype(BF)
        rows = mm(select[:, :half], half_refs[2 * slot][...]) + mm(select[:, half:], half_refs[2 * slot + 1][...])
        outs[0][0, slot] = rows.astype(BF)
        if not with_gates:
            continue
        gates_ref = refs[0]
        weight = jnp.where(one, gates_ref[slot, 0:1, :], 0.0) + jnp.where(two, gates_ref[slot, 1:2, :], 0.0)
        sign = jnp.where(one, 1.0, 0.0) - jnp.where(two, 1.0, 0.0)
        lane = lax.broadcasted_iota(jnp.int32, (CAP, 128), 1)
        outs[1][0, slot] = jnp.where(
            lane < 64, jnp.sum(weight, axis=1, keepdims=True), jnp.sum(sign, axis=1, keepdims=True)
        )


def dispatch(info, ids, halves, gates=None):
    half, width = halves[0][0].shape[-2:]

    def half_spec(item):
        if item[1] is None:
            return full_spec((half, width))
        return pl.BlockSpec((None, half, width), lambda e, info, place=item[1]: (place, 0, 0))

    extra = [] if gates is None else [gates]
    block = lambda n: pl.BlockSpec((1, GROUP, CAP, n), lambda e, info: (e, 0, 0, 0))
    outs = [(width, BF)] + ([] if gates is None else [(128, F32)])
    return pl.pallas_call(
        functools.partial(dispatch_kernel, gates is not None),
        grid_spec=pltpu.PrefetchScalarGridSpec(
            num_scalar_prefetch=1,
            grid=(SPLIT,),
            in_specs=[full_spec(ids.shape)] + [full_spec(g.shape) for g in extra] + [half_spec(v) for v in halves],
            out_specs=[block(n) for n, _ in outs],
        ),
        out_shape=[jax.ShapeDtypeStruct((SPLIT, GROUP, CAP, n), t) for n, t in outs],
        compiler_params=params(48),
        name="dispatch",
    )(info, ids, *extra, *[v for v, _ in halves])


def split_low(value):
    high = value.astype(BF)
    rest = value - high.astype(F32)
    middle = rest.astype(BF)
    return high, middle, (rest - middle.astype(F32)).astype(BF)


def expert_kernel(info_ref, x_ref, c_ref, meta_ref, full_ref, out_ref, *refs):
    outs, (xt_ref, dt_ref, grad_ref, w_ref, y_ref, db_ref) = refs[:-6], refs[-6:]
    d_refs, y_refs = outs[:GROUP], outs[GROUP:]
    step = pl.program_id(0)
    width = x_ref.shape[-1]
    rows = GROUP * CAP
    x = x_ref[...].reshape(rows, width)

    @pl.when(step == 0)
    def _():
        grad = (c_ref[...].reshape(rows, width).astype(F32) * meta_ref[...].reshape(rows, 128)[:, 0:1]).astype(BF)
        grad_ref[...] = grad
        xt_ref[...] = x.T
        dt_ref[...] = grad.T
        y_ref[...] = jnp.zeros_like(y_ref)
        db_ref[...] = jnp.zeros_like(db_ref)

    columns = w_ref.shape[-1]
    for rank in range(full_ref.shape[0]):
        source = 0
        if full_ref.shape[0] > 1:
            source = (rank & ~3) + jnp.bitwise_xor(info_ref[0], rank & 3)
        w_ref[source] = full_ref[rank]
    w_gate, w_up, w_down = [w_ref[:, part].reshape(width, columns) for part in range(3)]
    grad = grad_ref[...]
    gate = mm(x, w_gate)
    up = mm(x, w_up)
    sigmoid = 1.0 / (1.0 + jnp.exp(-gate))
    silu = gate * sigmoid
    act = (silu * up).astype(BF)
    d_act = mm(grad, w_down)
    d_gate = (d_act * up * sigmoid * (1.0 + gate * (1.0 - sigmoid))).astype(BF)
    d_up = (d_act * silu).astype(BF)
    y_ref[...] += mm_nt(act, w_down)
    db_ref[...] += mm_nt(d_gate, w_gate) + mm_nt(d_up, w_up)
    shape = (out_ref.shape[0], out_ref.shape[2], columns)
    out_ref[:, 0] = mm(xt_ref[...], d_gate).astype(BF).reshape(shape)
    out_ref[:, 1] = mm(xt_ref[...], d_up).astype(BF).reshape(shape)
    out_ref[:, 2] = mm(dt_ref[...], act).astype(BF).reshape(shape)

    @pl.when(step == pl.num_programs(0) - 1)
    def _():
        meta = meta_ref[...].reshape(rows, 128)
        y = y_ref[...]
        share = jnp.sum(c_ref[...].reshape(rows, width).astype(F32) * y, axis=1, keepdims=True) * meta[:, 64:65]
        lane = lax.broadcasted_iota(jnp.int32, (rows, EXTRA), 1)
        high, middle, low = [part.astype(F32) for part in split_low(share)]
        extra = jnp.where(lane == 0, high, jnp.where(lane == 1, middle, jnp.where(lane == 2, low, 0.0))).astype(BF)
        weighted = (y * meta[:, 0:1]).astype(BF)
        back = db_ref[...].astype(BF)
        for slot in range(GROUP):
            span = slice(slot * CAP, (slot + 1) * CAP)
            d_refs[slot][0, :, :width] = back[span]
            d_refs[slot][0, :, width:] = extra[span]
            y_refs[min(slot, 2)][max(slot - 2, 0)] = weighted[span]


def experts(info, rows, cotangents, meta, full, chunk, lead):
    width = rows.shape[-1]
    ranks, _, depth, hidden = full.shape
    tile = 256
    piece = width // lead
    count = GROUP * CAP
    row_spec = lambda n: pl.BlockSpec(
        (1, GROUP, CAP, n), lambda f, info: (chunk, 0, 0, 0), pipeline_mode=pl.Buffered(1)
    )
    shapes = [(1, CAP, width + EXTRA)] * GROUP + [(n, CAP, width) for n in (1, 1, 2)]
    return pl.pallas_call(
        expert_kernel,
        grid_spec=pltpu.PrefetchScalarGridSpec(
            num_scalar_prefetch=1,
            grid=(hidden // tile,),
            in_specs=[row_spec(width), row_spec(width), row_spec(128)]
            + [pl.BlockSpec((ranks, 3, depth, tile), lambda f, info: (0, 0, 0, f))],
            out_specs=[pl.BlockSpec((lead, 3, piece, tile), lambda f, info: (0, 0, 0, f))]
            + [pl.BlockSpec(shape, lambda f, info: (0, 0, 0)) for shape in shapes],
            scratch_shapes=[
                pltpu.VMEM((width, count), BF),
                pltpu.VMEM((width, count), BF),
                pltpu.VMEM((count, width), BF),
                pltpu.VMEM((width // depth, 3, depth, tile), BF),
                pltpu.VMEM((count, width), F32),
                pltpu.VMEM((count, width), F32),
            ],
        ),
        out_shape=[jax.ShapeDtypeStruct((lead, 3, piece, hidden), BF)]
        + [jax.ShapeDtypeStruct(shape, BF) for shape in shapes],
        compiler_params=params(60),
        name="experts",
    )(info, rows, cotangents, meta, full)


def combine_kernel(info_ref, ids_ref, *refs):
    row_refs, outs = refs[: SPLIT * GROUP], refs[SPLIT * GROUP :]
    block = ids_ref.shape[0]
    width = sum(ref.shape[1] for ref in outs)
    column = lax.broadcasted_iota(jnp.int32, (block, CAP), 1)
    one = jnp.broadcast_to(ids_ref[:, 0:1], (block, CAP)) - column
    two = jnp.broadcast_to(ids_ref[:, 1:2], (block, CAP)) - column
    total = jnp.zeros((block, width), F32)
    for index, rows in enumerate(row_refs):
        member, chunk = index // SPLIT, index % SPLIT
        expert = jnp.bitwise_xor(info_ref[0], member) * SPLIT + chunk
        select = jnp.where((one == expert * CAP) | (two == expert * CAP), 1.0, 0.0).astype(BF)
        total = total + mm(select, rows[0])
    first = 0
    for ref in outs:
        ref[...] = total[:, first : first + ref.shape[1]].astype(ref.dtype)
        first += ref.shape[1]


def combine(info, ids, rows, outs):
    length = ids.shape[0]
    width = sum(n for n, _ in outs)
    block = 256

    def row_spec(item):
        return pl.BlockSpec((1, CAP, width), lambda i, info, place=item[1]: (place, 0, 0))

    return pl.pallas_call(
        combine_kernel,
        grid_spec=pltpu.PrefetchScalarGridSpec(
            num_scalar_prefetch=1,
            grid=(length // block,),
            in_specs=[pl.BlockSpec((block, 8), lambda i, info: (i, 0))]
            + [row_spec(item) for item in rows],
            out_specs=[pl.BlockSpec((block, n), lambda i, info: (i, 0)) for n, _ in outs],
        ),
        out_shape=[jax.ShapeDtypeStruct((length, n), t) for n, t in outs],
        compiler_params=params(48),
        name="combine",
    )(info, ids, *[item[0] for item in rows])


def per_device(
    count,
    inputs,
    prev_logits,
    routes,
    lengths,
    cotangent,
    attn_gain,
    w_qkv,
    w_out,
    moe_gain,
    w_router,
    w_resid,
    const_mix,
    const_vec,
    w_experts,
):
    half, width = inputs.shape[1:]
    length = routes.shape[1]
    depth = w_experts.shape[0]
    hidden = w_experts.shape[3]
    heads = w_out.shape[1]
    t_rank = lax.axis_index("tensor")
    d_rank = lax.axis_index("dp")
    bit = lambda n: (d_rank >> n) & 1
    group = d_rank % GROUP
    fast = count == 16 and depth % 16 == 0
    info = jnp.stack([group, bit(2), d_rank]).astype(jnp.int32)
    first_row = t_rank * half
    length_here = lengths[0]

    def in_order(own, other):
        return jnp.where(t_rank == 0, jnp.concatenate([own, other]), jnp.concatenate([other, own]))

    own_in = inputs[0]
    other_in = swap_x(own_in)

    own_routes = routes.transpose(0, 2, 1)
    far_routes = jnp.concatenate([own_routes, swap_dp(own_routes, count, FAR)])

    out_low = w_out.astype(BF)[None]
    attn_shard = jnp.concatenate([w_qkv.transpose(1, 0, 2).astype(BF), out_low, swap_x(out_low)])
    lines = [[i + GROUP * j for j in range(count // GROUP)] for i in range(GROUP)]
    attn_rows, rank_masks = attn_shard[None], [0]
    weights = []

    def double(rows, masks, n):
        got = swap_dp(rows, count, 1 << n)
        return jnp.concatenate([rows, got]), masks + [mask | (1 << n) for mask in masks], got

    def expert_rows(e, got):
        passed = swap_dp(got, count, 1)
        return jnp.concatenate([mine[0][:, e], pair[:, e], got[:1, 0], passed[1:, 0]])

    if fast:
        mine = list(unpack(info, w_experts))
        pair = swap_dp(mine[1], count, 1)
        for n in (3, 2):
            attn_rows, rank_masks, _ = double(attn_rows, rank_masks, n)
        got = swap_dp(mine[2], count, FAR)
        got, attn_rows, mine[3], other_in = meet(got, attn_rows, mine[3], other_in)
        attn_rows, rank_masks, attn_got = double(attn_rows, rank_masks, 1)
        first_quad = expert_rows(0, got)
        weights.append(lax.all_gather(first_quad, "dp", axis=0, tiled=True, axis_index_groups=lines))
        attn_rows, rank_masks, _ = double(attn_rows, rank_masks, 0)
    else:
        attn_rows = lax.all_gather(attn_shard, "dp", axis=1, tiled=True)[None]
        expert_low = w_experts.astype(BF).reshape(depth, GROUP, SPLIT, 3, hidden).transpose(1, 2, 3, 0, 4)
        gathered = pick(lax.all_gather(expert_low, "dp", axis=3, tiled=True), group)
        weights = [gathered[e][None] for e in range(SPLIT)]

    near_routes = swap_dp(far_routes, count, 1)
    all_routes = jnp.stack([far_routes[0], near_routes[0], far_routes[1], near_routes[1]])
    turned = jnp.concatenate([all_routes[:, :, half:], all_routes[:, :, :half]], axis=2)
    ids_rows, ids_own = slot_ids(jnp.where(t_rank == 0, all_routes, turned))
    all_in = in_order(own_in, other_in)
    row_place = first_row + jnp.arange(half, dtype=jnp.int32)
    live = (row_place < length_here)[:, None]
    cot_own = jnp.where(live, cotangent[0], BF(0))
    cot_other = swap_x(after(cot_own, other_in))
    far_cot = [swap_dp(after(cot_own, mine) if fast else cot_own, count, FAR)]
    inv_freq = THETA ** (-jnp.arange(HEAD_DIM // 2, dtype=F32) / (HEAD_DIM // 2))
    angles = jnp.arange(length, dtype=F32)[:, None] * inv_freq[None, :]
    cosine = jnp.tile(jnp.cos(angles), (1, 4))
    sine = jnp.sin(angles)
    sine = jnp.tile(jnp.concatenate([-sine, sine], axis=1), (1, 2))
    bias = jnp.where(jnp.arange(length, dtype=jnp.int32) < length_here, 0.0, NEG)[None, :].astype(F32)

    if fast:
        all_in = after(all_in, first_quad)
    attn, query, key, value, attn_full, out_own, out_other = project(
        info, all_in, attn_gain[None], attn_rows, rank_masks, cosine, sine
    )
    far_cot.append(swap_dp(after(cot_other, query), count, FAR))
    attended, lse = attend(query, key, value, bias)
    att_own = lax.dynamic_slice_in_dim(attended, first_row, half, 0)
    att_send = lax.dynamic_slice_in_dim(attended, half - first_row, half, 0)
    att_other = swap_x(att_send)
    near_cot = chain(after([cot_own, cot_other, far_cot[0]], attended), lambda v: swap_dp(v, count, 1))
    if fast:
        rows = expert_rows(1, after(swap_dp(mine[3], count, FAR), attended))
        weights.append(lax.all_gather(rows, "dp", axis=0, tiled=True, axis_index_groups=lines))
    att_other = after(att_other, near_cot)
    near_cot.append(swap_dp(far_cot[1], count, 1))
    resid_in = own_in.astype(F32)
    resid_mid = resid_in + mm_nt(att_own, out_own) + mm_nt(att_other, out_other)

    inv_two = lax.rsqrt(jnp.mean(resid_mid * resid_mid, axis=-1, keepdims=True) + EPS)
    normed = resid_mid * inv_two * moe_gain
    moe_own = normed.astype(BF)
    moe_other = swap_x(moe_own)
    far_moe = [swap_dp(moe_own, count, FAR)]
    prev_rows = prev_logits[0]
    cot_halves = [cot_own, cot_other] + near_cot[:2] + far_cot + near_cot[2:]
    (cot_rows,) = dispatch(info, ids_rows, [(v, None) for v in after(cot_halves, moe_own)])
    small_w = jnp.concatenate([w_router, const_mix.reshape(4, width).T], axis=1)
    small = jnp.dot(normed, small_w, precision=HIGHEST)
    logits = small[:, :EXPERTS] + jnp.dot(prev_rows, w_resid, precision=HIGHEST)
    route_own = ids_own[:half, 2:4]
    labels = jnp.arange(EXPERTS, dtype=jnp.int32)
    onehot = (route_own[:, :, None] == labels).astype(F32)
    chosen = jnp.sum(onehot * logits[:, None, :], axis=-1)
    top = jnp.max(chosen, axis=-1, keepdims=True)
    gate_weight = jnp.exp(chosen - top)
    gate_weight = gate_weight / jnp.sum(gate_weight, axis=-1, keepdims=True)
    mix = small[:, EXPERTS:].reshape(half, 2, 2)
    mix = jnp.exp(mix - jnp.max(mix, axis=-1, keepdims=True))
    mix = mix / jnp.sum(mix, axis=-1, keepdims=True)
    gate_t = gate_weight.T
    gates = jnp.stack([gate_t, swap_dp(gate_t, count, FAR)])
    gates = jnp.concatenate([gates, swap_x(gates)], axis=2)
    gates = jnp.stack([gates, swap_dp(gates, count, 1)], axis=1).reshape(GROUP, 2, length)

    far_moe.append(swap_dp(after(moe_other, gates), count, FAR))
    near_moe = jnp.stack([moe_own, moe_other, after(far_moe[0], cot_rows)])
    near_moe = swap_dp(near_moe, count, 1)
    is_copy = onehot[:, :, FFN_EXPERTS + 1]
    is_const = onehot[:, :, FFN_EXPERTS + 2 :]
    w_copy = jnp.sum(gate_weight * is_copy, axis=1, keepdims=True)
    w_const = jnp.sum(gate_weight[:, :, None] * is_const, axis=1)
    on_normed = w_copy + jnp.sum(w_const * mix[:, :, 0], axis=1, keepdims=True)
    on_vec = w_const * mix[:, :, 1]
    grad_top = cot_own.astype(F32)
    dot_normed = jnp.sum(grad_top * normed, axis=1, keepdims=True)
    dot_vec = jnp.stack([jnp.sum(grad_top * const_vec[j], axis=1) for j in range(2)], axis=1)
    const_gate = mix[:, :, 0] * dot_normed + mix[:, :, 1] * dot_vec
    special = is_copy * dot_normed + jnp.sum(is_const * const_gate[:, None, :], axis=-1)
    d_mix = jnp.stack([w_const * dot_normed, w_const * dot_vec], axis=-1)
    d_mix = mix * (d_mix - jnp.sum(mix * d_mix, axis=-1, keepdims=True))
    special = special[:, 0] - special[:, 1]
    gate_product = gate_weight[:, 0] * gate_weight[:, 1]
    d_mix = d_mix.reshape(half, 4)
    far_moe[1], special, gate_product, d_mix, on_normed, on_vec = meet(
        far_moe[1], special, gate_product, d_mix, on_normed, on_vec
    )
    near_last = swap_dp(far_moe[1], count, 1)
    moe_halves = [(moe_own, None), (moe_other, None), (near_moe, 0), (near_moe, 1)]
    moe_halves += [(far_moe[0], None), (far_moe[1], None), (near_moe, 2), (near_last, None)]
    moe_rows, meta = dispatch(info, ids_rows, moe_halves, gates)
    rows_in = moe_rows
    lead = count // GROUP if fast else 1
    grads, d_sent, y_sent = [], [], []
    for e in range(SPLIT):
        blocks, *routed = experts(info, rows_in, cot_rows, meta, weights[e], e, lead)
        d_sent.append(routed[:GROUP])
        y_sent.append(routed[GROUP:])
        rows_in = after(rows_in, routed[0])
        if fast:
            blocks = lax.psum_scatter(blocks, "dp", scatter_dimension=0, tiled=False, axis_index_groups=lines)
        else:
            blocks = blocks.reshape(3, count, depth, hidden).transpose(1, 0, 2, 3)
            blocks = scatter_bits(blocks, range(2, count.bit_length() - 1), d_rank, count)
            blocks = blocks.transpose(1, 0, 2, 3)
        grads.append(blocks.reshape(3, GROUP, depth, hidden))
    first_rows = [(d_sent[0][0], 0)] + share_all(d_sent[0][1:], count)
    last_sent = after(d_sent[1][1:], [r for r, _ in first_rows[1:]])
    last_rows = [(d_sent[1][0], 0)] + share_all(last_sent, count)
    d_rows = [r for pair in zip(first_rows, last_rows) for r in pair]
    d_low, share_other = combine(info, ids_own[half:], d_rows, [(width, BF), (EXTRA, F32)])
    d_got = swap_x(d_low)
    share_got = swap_x(jnp.sum(share_other[:, :3], axis=1))
    d_own, share_own = combine(info, after(ids_own[:half], d_low), d_rows, [(width, F32), (EXTRA, F32)])
    y_rows = [[(y[0], 0)] + share_far(after(y[1], d_own), after(y[2], d_own), count) for y in y_sent]
    y_rows = [r for pair in zip(*y_rows) for r in pair]
    d_tokens = d_own + d_got.astype(F32)
    share = jnp.sum(share_own[:, :3], axis=1) + share_got

    d_first = gate_product * (share + special)
    d_logits = d_first[:, None] * (onehot[:, 0] - onehot[:, 1])
    d_small = jnp.concatenate([d_logits, d_mix], axis=1)
    d_normed = jnp.dot(d_small, small_w.T, precision=HIGHEST) + on_normed * grad_top + d_tokens
    grad_moe_gain = jnp.sum(d_normed * resid_mid * inv_two, axis=0)
    scaled = moe_gain * d_normed
    d_resid = (
        grad_top
        + inv_two * scaled
        - resid_mid * (inv_two * inv_two * inv_two) * jnp.mean(scaled * resid_mid, axis=-1, keepdims=True)
    )

    def final_pieces(blocks):
        blocks = [
            lax.dynamic_index_in_dim(blocks, jnp.bitwise_xor(group, m), 1, keepdims=False)[None] for m in range(GROUP)
        ]
        return [(blocks[0], 0)] + share_far(blocks[1], jnp.concatenate(blocks[2:]), count)

    d_mixed = d_resid.astype(BF)
    d_att_low = mm(d_mixed, out_other).astype(BF)
    d_att_got = swap_x(d_att_low)
    d_late, on_vec_late = after((d_small, on_vec), d_att_low)
    grad_prev = jnp.dot(d_late[:, :EXPERTS], w_resid.T, precision=HIGHEST)
    grad_resid = jnp.dot(prev_rows.T, d_late[:, :EXPERTS], precision=HIGHEST)
    grad_small = jnp.dot(d_late.T, normed, precision=HIGHEST)
    grad_const_vec = jnp.dot(on_vec_late.T, grad_top, precision=HIGHEST)
    d_att_own = mm(after(d_mixed, d_att_low), out_own).astype(BF)
    attn_late = after(attn, d_att_low)
    first_pieces = final_pieces(after(grads[0], d_att_low))
    d_att_other = d_att_got
    d_attended = in_order(d_att_own, d_att_other)
    d_mixed_other = swap_x(after(d_mixed, d_att_got))
    d_qkv = attend_back(query, key, value, d_attended, lse, bias, cosine, sine)
    d_mixed_all = in_order(d_mixed, after(d_mixed_other, d_qkv))
    grad_out = mm_tn(d_mixed_all, attended)
    grad_qkv = jnp.stack([mm_tn(attn_late, d_qkv[k]) for k in range(3)] + [grad_out])
    blocks = grad_qkv.astype(BF).reshape(4, count, depth, heads).transpose(1, 0, 2, 3)
    bits = list(range(count.bit_length() - 1))[::-1]
    blocks, *arrived = meet(blocks, *[p for p, _ in first_pieces])
    first_pieces = [(p, place) for p, (_, place) in zip(arrived, first_pieces)]
    stage = halve(blocks, bits, 0, d_rank, count)
    bits.remove(0)
    d_attn = sum(mm_nt(d_qkv[k], attn_full[k]) for k in range(3))
    values = all_in.astype(F32)
    inv_all = lax.rsqrt(jnp.mean(values * values, axis=-1, keepdims=True) + EPS)
    grad_attn_gain = jnp.sum(d_attn * values * inv_all, axis=0)
    d_attn_own = lax.dynamic_slice_in_dim(d_attn, first_row, half, 0)
    d_attn_other = lax.dynamic_slice_in_dim(d_attn, half - first_row, half, 0).astype(BF)
    d_attn_got = swap_x(d_attn_other)
    y_ids = after(ids_own, d_attn_other)
    (y_low,) = combine(info, y_ids[half:], y_rows, [(width, BF)])
    y_got = swap_x(y_low)
    (y_own,) = combine(info, after(y_ids[:half], y_low), y_rows, [(width, F32)])
    inv_one = lax.rsqrt(jnp.mean(resid_in * resid_in, axis=-1, keepdims=True) + EPS)
    early = jnp.concatenate(
        [
            grad_small.reshape(-1),
            grad_const_vec.reshape(-1),
            grad_moe_gain,
            jnp.pad(grad_resid.reshape(-1), (0, 112)),
            grad_attn_gain,
        ]
    )
    early = early.reshape(-1, 128)
    last_grad = grads[1]
    stage, early = meet(stage, early)
    hops = [[0, 1, 2], [3], list(range(4, count.bit_length() - 1))] + [[]] * count
    for n in bits[::-1]:
        stage = halve(stage, bits, n, d_rank, count)
        bits.remove(n)
        for hop in hops.pop(0):
            early = early + swap_dp(early, count, 1 << hop)
        stage, early = meet(stage, early)
        if n == 2:
            stage, d_attn_got, last_grad = meet(stage, d_attn_got, last_grad)
        if n == 3:
            stage, y_got = meet(stage, y_got)
    early = early + swap_x(early)
    grad_attn = stage[0].astype(F32)
    d_attn_own = d_attn_own + d_attn_got.astype(F32)
    scaled = attn_gain * d_attn_own
    grad_inputs = (
        d_resid
        + inv_one * scaled
        - resid_in * (inv_one * inv_one * inv_one) * jnp.mean(scaled * resid_in, axis=-1, keepdims=True)
    )

    block_out = resid_mid + y_own + y_got.astype(F32) + on_normed * normed
    block_out = block_out + on_vec[:, 0:1] * const_vec[0] + on_vec[:, 1:2] * const_vec[1]
    block_out = block_out.astype(BF)

    pieces = first_pieces + final_pieces(last_grad)
    if fast:
        grad_experts = pack(info, pieces)
    else:
        table = jnp.stack([entry(p).astype(F32) for p in pieces]).reshape(SPLIT, GROUP, 3, depth, hidden)
        table = jnp.take(table, jnp.bitwise_xor(jnp.arange(GROUP), group), axis=1)
        grad_experts = table.transpose(3, 1, 0, 2, 4).reshape(depth, FFN_EXPERTS, 3, hidden)

    early = early.reshape(-1)
    grad_attn_gain = early[-width:]
    sizes = [EXPERTS * width, 4 * width, 2 * width, width]
    cuts = [sum(sizes[: i + 1]) for i in range(4)]
    grad_router = early[: cuts[0]].reshape(EXPERTS, width).T
    grad_const_mix = early[cuts[0] : cuts[1]].reshape(2, 2, width)
    grad_const_vec = early[cuts[1] : cuts[2]].reshape(2, width)
    grad_moe_gain = early[cuts[2] : cuts[3]]
    grad_resid = early[cuts[3] : cuts[3] + EXPERTS * EXPERTS].reshape(EXPERTS, EXPERTS)
    return (
        block_out[None],
        grad_inputs.astype(BF)[None],
        grad_prev[None],
        grad_attn_gain,
        grad_attn[:3].transpose(1, 0, 2),
        grad_attn[3],
        grad_moe_gain,
        grad_router,
        grad_resid,
        grad_const_mix,
        grad_const_vec,
        grad_experts,
    )


def solution(mesh):
    placed = (
        P("dp", "tensor", None),
        P("dp", "tensor", None),
        P("dp", None, None),
        P("dp"),
        P("dp", "tensor", None),
        P(),
        P("dp", None, "tensor"),
        P("dp", "tensor"),
        P(),
        P(),
        P(),
        P(),
        P(),
        P("dp", None, None, "tensor"),
    )
    return jax.shard_map(
        functools.partial(per_device, mesh.shape["dp"]),
        mesh=mesh,
        in_specs=placed,
        out_specs=(
            P("dp", "tensor", None),
            P("dp", "tensor", None),
            P("dp", "tensor", None),
            P(),
            P("dp", None, "tensor"),
            P("dp", "tensor"),
            P(),
            P(),
            P(),
            P(),
            P(),
            P("dp", None, None, "tensor"),
        ),
        check_vma=False,
    )
```

```python
import functools

import jax
import jax.numpy as jnp
from jax import lax
from jax.experimental import pallas as pl
from jax.experimental.pallas import tpu as pltpu
from jax.sharding import PartitionSpec as P

HEAD_DIM = 64
FFN_EXPERTS = 8
EXPERTS = 12
CAP = 256
EPS = 1e-05
THETA = 10000.0
HIGHEST = lax.Precision.HIGHEST
BF = jnp.bfloat16
F32 = jnp.float32
NEG = float("-inf")
MIB = 1 << 20
GROUP = 4
SPLIT = FFN_EXPERTS // GROUP
EXTRA = 128


def params(mib):
    return pltpu.CompilerParams(vmem_limit_bytes=mib * MIB)


def mm(a, b):
    return jnp.dot(a, b, preferred_element_type=F32)


def mm_nt(a, b):
    return lax.dot_general(a, b, (((1,), (1,)), ((), ())), preferred_element_type=F32)


def mm_tn(a, b):
    return lax.dot_general(a, b, (((0,), (0,)), ((), ())), preferred_element_type=F32)


def full_spec(shape):
    zeros = (0,) * len(shape)
    return pl.BlockSpec(shape, lambda *ids: zeros)


def swap_x(value):
    return lax.ppermute(value, "tensor", [(0, 1), (1, 0)])


def swap_dp(value, count, mask):
    return lax.ppermute(value, "dp", [(i, i ^ mask) for i in range(count)])


def after(value, *earlier):
    return lax.optimization_barrier((value, earlier))[0]


def meet(*values):
    return lax.optimization_barrier(values)


def pick(blocks, index):
    return lax.dynamic_index_in_dim(blocks, index, 0, keepdims=False)


def chain(values, swap):
    done = []
    for value in values:
        done.append(swap(after(value, done[-1]) if done else value))
    return done


def add_low(*terms):
    total = terms[0].astype(F32)
    for term in terms[1:]:
        total = total + term.astype(F32)
    return total


def halve(blocks, bits, bit, rank, count):
    place = bits.index(bit)
    high, low = 2**place, 2 ** (len(bits) - place - 1)
    pair = blocks.reshape((high, 2, low) + blocks.shape[1:])
    side = (rank >> bit) & 1
    send = lax.dynamic_index_in_dim(pair, 1 - side, 1, keepdims=False)
    keep = lax.dynamic_index_in_dim(pair, side, 1, keepdims=False)
    total = add_low(keep, swap_dp(send, count, 1 << bit)).astype(BF)
    return total.reshape((high * low,) + blocks.shape[1:])


def scatter_bits(blocks, order, rank, count):
    bits = list(range(count.bit_length() - 1))[::-1]
    for bit in order:
        blocks = halve(blocks, bits, bit, rank, count)
        bits.remove(bit)
    return blocks


def sum_all(value, count):
    bit = 1
    while bit < count:
        value = value + swap_dp(value, count, bit)
        bit *= 2
    return value + swap_x(value)


FAR = 2


def share_group(own, count):
    other = swap_x(own)
    far_own = swap_dp(own, count, FAR)
    far_other = swap_dp(other, count, FAR)
    near = [swap_dp(v, count, 1) for v in (own, other, far_own, far_other)]
    return [own, other, near[0], near[1], far_own, far_other, near[2], near[3]]


def share_all(parts, count):
    return [(swap_dp(part, count, mask), 0) for mask, part in enumerate(parts, 1)]


def share_far(pair, far, count):
    got = swap_dp(far, count, FAR)
    return [(swap_dp(pair, count, 1), 0), (got, 0), (swap_dp(got, count, 1), 1)]


def entry(item):
    return item[0][item[1] : item[1] + 1]


def turn(values, cosine, sine):
    lane = lax.broadcasted_iota(jnp.int32, values.shape, 1)
    other = jnp.where(lane % HEAD_DIM < HEAD_DIM // 2, pltpu.roll(values, 96, 1), pltpu.roll(values, 32, 1))
    return values * cosine + other * sine


def qkv_kernel(masks, info_ref, x_ref, gain_ref, w_ref, cos_ref, sin_ref, attn_ref, q_ref, k_ref, v_ref, full_ref, out_ref, other_ref, by_rank_ref):
    @pl.when(pl.program_id(0) == 0)
    def _():
        for place, mask in enumerate(masks):
            by_rank_ref[jnp.bitwise_xor(info_ref[2], mask) if len(masks) > 1 else 0] = w_ref[place]
        for part in range(3):
            full_ref[part] = by_rank_ref[:, part].reshape(full_ref.shape[1:])
        out_ref[...] = by_rank_ref[:, 3].reshape(out_ref.shape)
        other_ref[...] = by_rank_ref[:, 4].reshape(out_ref.shape)

    values = x_ref[...].astype(F32)
    inverse = lax.rsqrt(jnp.mean(values * values, axis=-1, keepdims=True) + EPS)
    attn = (values * inverse * gain_ref[...]).astype(BF)
    attn_ref[...] = attn
    width = q_ref.shape[1]
    for part, out in enumerate((q_ref, k_ref, v_ref)):
        rows = mm(attn, full_ref[part])
        if part == 2:
            out[...] = rows.astype(BF)
            continue
        for start in range(0, width, 128):
            turned = turn(rows[:, start : start + 128], cos_ref[...], sin_ref[...]).astype(BF)
            if part == 0:
                turned = turned * BF(HEAD_DIM ** -0.5)
            out[:, start : start + 128] = turned


def project(info, rows, gain, weight, masks, cosine, sine):
    length, width = rows.shape
    heads = weight.shape[-1]
    block = 256
    row_spec = lambda n: pl.BlockSpec((block, n), lambda i, info: (i, 0))
    return pl.pallas_call(
        functools.partial(qkv_kernel, masks),
        grid_spec=pltpu.PrefetchScalarGridSpec(
            num_scalar_prefetch=1,
            grid=(length // block,),
            in_specs=[
                row_spec(width),
                full_spec((1, width)),
                full_spec(weight.shape),
                row_spec(128),
                row_spec(128),
            ],
            out_specs=[row_spec(width), row_spec(heads), row_spec(heads), row_spec(heads)]
            + [full_spec((3, width, heads))] + [full_spec((width, heads))] * 2,
            scratch_shapes=[pltpu.VMEM(weight.shape, BF)],
        ),
        out_shape=[jax.ShapeDtypeStruct((length, width), BF)]
        + [jax.ShapeDtypeStruct((length, heads), BF)] * 3
        + [jax.ShapeDtypeStruct((3, width, heads), BF)]
        + [jax.ShapeDtypeStruct((width, heads), BF)] * 2,
        compiler_params=params(40),
        name="project",
    )(info, rows, gain, weight, cosine, sine)


BLOCK = 256


def head_scores(query, k_ref, bias_ref, index):
    row = lax.broadcasted_iota(jnp.int32, (BLOCK, BLOCK), 0)
    column = lax.broadcasted_iota(jnp.int32, (BLOCK, BLOCK), 1)
    parts = []
    for block in range(index + 1):
        span = pl.ds(block * BLOCK, BLOCK)
        scores = mm_nt(query, k_ref[span, :]) + bias_ref[:, span]
        if block == index:
            scores = jnp.where(column <= row, scores, NEG)
        parts.append(scores)
    return parts


def attend_kernel(q_ref, k_ref, v_ref, bias_ref, o_ref, lse_ref):
    length = q_ref.shape[0]
    lane = lax.broadcasted_iota(jnp.int32, (BLOCK, 128), 1)
    for index in range(length // BLOCK):
        rows = pl.ds(index * BLOCK, BLOCK)
        outs, totals = [], []
        for head in range(2):
            mine = (lane < HEAD_DIM) if head == 0 else (lane >= HEAD_DIM)
            query = jnp.where(mine, q_ref[rows, :], BF(0))
            parts = head_scores(query, k_ref, bias_ref, index)
            top = functools.reduce(jnp.maximum, [jnp.max(p, axis=1, keepdims=True) for p in parts])
            parts = [jnp.exp(p - top) for p in parts]
            total = functools.reduce(jnp.add, [jnp.sum(p, axis=1, keepdims=True) for p in parts])
            inverse = 1.0 / total
            out = jnp.zeros((BLOCK, 128), F32)
            for block, part in enumerate(parts):
                out = out + mm((part * inverse).astype(BF), v_ref[pl.ds(block * BLOCK, BLOCK), :])
            outs.append(out)
            totals.append(top + jnp.log(total))
        o_ref[rows, :] = jnp.where(lane < HEAD_DIM, outs[0], outs[1]).astype(BF)
        lse_ref[rows, :] = jnp.where(lane < HEAD_DIM, totals[0], totals[1])


def attend(query, key, value, bias):
    length, width = query.shape
    pair = pl.BlockSpec((length, 128), lambda p: (0, p))
    return pl.pallas_call(
        attend_kernel,
        grid=(width // 128,),
        in_specs=[pair, pair, pair, full_spec((1, length))],
        out_specs=[pair, pair],
        out_shape=[jax.ShapeDtypeStruct((length, width), BF), jax.ShapeDtypeStruct((length, width), F32)],
        compiler_params=params(40),
        name="attend",
    )(query, key, value, bias)


def attend_back_kernel(q_ref, k_ref, v_ref, g_ref, lse_ref, bias_ref, cos_ref, sin_ref, out_ref, dk_ref, dv_ref):
    length = q_ref.shape[0]
    lane = lax.broadcasted_iota(jnp.int32, (BLOCK, 128), 1)
    dk_ref[...] = jnp.zeros_like(dk_ref)
    dv_ref[...] = jnp.zeros_like(dv_ref)
    for index in range(length // BLOCK):
        rows = pl.ds(index * BLOCK, BLOCK)
        grad_query = jnp.zeros((BLOCK, 128), F32)
        for head in range(2):
            mine = (lane < HEAD_DIM) if head == 0 else (lane >= HEAD_DIM)
            query = jnp.where(mine, q_ref[rows, :], BF(0))
            grad = jnp.where(mine, g_ref[rows, :], BF(0))
            lse = lse_ref[rows, head * HEAD_DIM : head * HEAD_DIM + 1]
            probs = [jnp.exp(p - lse) for p in head_scores(query, k_ref, bias_ref, index)]
            grads = [mm_nt(grad, v_ref[pl.ds(b * BLOCK, BLOCK), :]) for b in range(index + 1)]
            delta = functools.reduce(
                jnp.add, [jnp.sum(p * g, axis=1, keepdims=True) for p, g in zip(probs, grads)]
            )
            for block in range(index + 1):
                span = pl.ds(block * BLOCK, BLOCK)
                scored = (probs[block] * (grads[block] - delta)).astype(BF)
                key = k_ref[span, :]
                grad_query = grad_query + jnp.where(mine, mm(scored, key), 0.0)
                dk_ref[span, :] += mm_tn(scored, query)
                dv_ref[span, :] += mm_tn(probs[block].astype(BF), grad)
        grad_query = grad_query * HEAD_DIM ** -0.5
        out_ref[0, rows, :] = turn(grad_query, cos_ref[rows, :], -sin_ref[rows, :]).astype(BF)
    out_ref[1] = turn(dk_ref[...], cos_ref[...], -sin_ref[...]).astype(BF)
    out_ref[2] = dv_ref[...].astype(BF)


def attend_back(query, key, value, grad, lse, bias, cosine, sine):
    length, width = query.shape
    pair = pl.BlockSpec((length, 128), lambda p: (0, p))
    return pl.pallas_call(
        attend_back_kernel,
        grid=(width // 128,),
        in_specs=[pair, pair, pair, pair, pair, full_spec((1, length)), full_spec((length, 128)), full_spec((length, 128))],
        out_specs=pl.BlockSpec((3, length, 128), lambda p: (0, 0, p)),
        out_shape=jax.ShapeDtypeStruct((3, length, width), BF),
        scratch_shapes=[pltpu.VMEM((length, 128), F32)] * 2,
        compiler_params=params(48),
        name="attend_back",
    )(query, key, value, grad, lse, bias, cosine, sine)


def slot_ids_kernel(routes_ref, rows_ref, columns_ref):
    length = routes_ref.shape[2]
    label = lax.broadcasted_iota(jnp.int32, (FFN_EXPERTS, length), 0)
    before = lax.broadcasted_iota(jnp.int32, (length, length), 0) < lax.broadcasted_iota(
        jnp.int32, (length, length), 1
    )
    before = jnp.where(before, 1.0, 0.0).astype(BF)
    for slot in range(GROUP):
        chosen = [routes_ref[slot, k : k + 1, :] == label for k in range(2)]
        member = jnp.where(chosen[0] | chosen[1], 1.0, 0.0).astype(BF)
        place = mm(member, before).astype(jnp.int32) + label * CAP
        for k in range(2):
            ids = jnp.sum(jnp.where(chosen[k], place, 0), axis=0, keepdims=True)
            routed = routes_ref[slot, k : k + 1, :] < FFN_EXPERTS
            rows_ref[slot, k : k + 1, :] = jnp.where(routed, ids, -1)
    own = jnp.concatenate([rows_ref[0], routes_ref[0]] * 2, axis=0)
    columns_ref[...] = own.T


def slot_ids(routes):
    length = routes.shape[2]
    return pl.pallas_call(
        slot_ids_kernel,
        in_specs=[full_spec(routes.shape)],
        out_specs=[full_spec(routes.shape), full_spec((length, 8))],
        grid=(1,),
        out_shape=[jax.ShapeDtypeStruct(routes.shape, jnp.int32), jax.ShapeDtypeStruct((length, 8), jnp.int32)],
        compiler_params=params(40),
        name="slot_ids",
    )(routes)


def unpack_kernel(info_ref, w_ref, near_ref, pair_ref, *far_refs):
    jobs = [(near_ref, 0, c, 0, c) for c in range(SPLIT)] + [(pair_ref, 0, c, 1, c) for c in range(SPLIT)]
    jobs += [(ref, m, 0, 2 + m, c) for c, ref in enumerate(far_refs) for m in range(2)]
    for out_ref, place, slot, member, chunk in jobs:
        expert = jnp.bitwise_xor(info_ref[0], member) * SPLIT + chunk
        for part in range(3):
            rows = pl.ds(part * FFN_EXPERTS + expert, out_ref.shape[3], stride=3 * FFN_EXPERTS)
            out_ref[place, slot, part] = w_ref[rows, :].astype(BF)


def unpack(info, weights):
    depth, _, _, hidden = weights.shape
    flat = weights.transpose(0, 2, 1, 3).reshape(depth * 3 * FFN_EXPERTS, hidden)
    tile = 128
    counts = [(1, SPLIT)] * 2 + [(2, 1)] * SPLIT
    return pl.pallas_call(
        unpack_kernel,
        grid_spec=pltpu.PrefetchScalarGridSpec(
            num_scalar_prefetch=1,
            grid=(hidden // tile,),
            in_specs=[pl.BlockSpec((flat.shape[0], tile), lambda c, info: (0, c))],
            out_specs=[pl.BlockSpec(n + (3, depth, tile), lambda c, info: (0, 0, 0, 0, c)) for n in counts],
        ),
        out_shape=[jax.ShapeDtypeStruct(n + (3, depth, hidden), BF) for n in counts],
        compiler_params=params(40),
        name="unpack",
    )(info, flat)


def pack_kernel(info_ref, *refs):
    out_ref = refs[-1]
    depth = refs[0].shape[2]
    for index, ref in enumerate(refs[:-1]):
        chunk, member = index // GROUP, index % GROUP
        expert = jnp.bitwise_xor(info_ref[0], member) * SPLIT + chunk
        for part in range(3):
            rows = pl.ds(part * FFN_EXPERTS + expert, depth, stride=3 * FFN_EXPERTS)
            out_ref[rows, :] = ref[0, part].astype(F32)


def pack(info, pieces):
    _, _, depth, hidden = pieces[0][0].shape
    tile = 128
    flat = pl.pallas_call(
        pack_kernel,
        grid_spec=pltpu.PrefetchScalarGridSpec(
            num_scalar_prefetch=1,
            grid=(hidden // tile,),
            in_specs=[
                pl.BlockSpec((1, 3, depth, tile), lambda c, info, place=place: (place, 0, 0, c))
                for _, place in pieces
            ],
            out_specs=pl.BlockSpec((depth * 3 * FFN_EXPERTS, tile), lambda c, info: (0, c)),
        ),
        out_shape=jax.ShapeDtypeStruct((depth * 3 * FFN_EXPERTS, hidden), F32),
        compiler_params=params(40),
        name="pack",
    )(info, *[p for p, _ in pieces])
    return flat.reshape(depth, 3, FFN_EXPERTS, hidden).transpose(0, 2, 1, 3)


def dispatch_kernel(with_gates, info_ref, ids_ref, *refs):
    first = (info_ref[0] * SPLIT + pl.program_id(0)) * CAP
    half_refs, outs = refs[-9:-1] if not with_gates else refs[1:9], refs[-2:] if with_gates else refs[-1:]
    half = half_refs[0].shape[0]
    for slot in range(GROUP):
        row = lax.broadcasted_iota(jnp.int32, (CAP, 2 * half), 0) + first
        one, two = row == ids_ref[slot, 0:1, :], row == ids_ref[slot, 1:2, :]
        select = jnp.where(one | two, 1.0, 0.0).astype(BF)
        rows = mm(select[:, :half], half_refs[2 * slot][...]) + mm(select[:, half:], half_refs[2 * slot + 1][...])
        outs[0][0, slot] = rows.astype(BF)
        if not with_gates:
            continue
        gates_ref = refs[0]
        weight = jnp.where(one, gates_ref[slot, 0:1, :], 0.0) + jnp.where(two, gates_ref[slot, 1:2, :], 0.0)
        sign = jnp.where(one, 1.0, 0.0) - jnp.where(two, 1.0, 0.0)
        lane = lax.broadcasted_iota(jnp.int32, (CAP, 128), 1)
        outs[1][0, slot] = jnp.where(
            lane < 64, jnp.sum(weight, axis=1, keepdims=True), jnp.sum(sign, axis=1, keepdims=True)
        )


def dispatch(info, ids, halves, gates=None):
    half, width = halves[0][0].shape[-2:]

    def half_spec(item):
        if item[1] is None:
            return full_spec((half, width))
        return pl.BlockSpec((None, half, width), lambda e, info, place=item[1]: (place, 0, 0))

    extra = [] if gates is None else [gates]
    block = lambda n: pl.BlockSpec((1, GROUP, CAP, n), lambda e, info: (e, 0, 0, 0))
    outs = [(width, BF)] + ([] if gates is None else [(128, F32)])
    return pl.pallas_call(
        functools.partial(dispatch_kernel, gates is not None),
        grid_spec=pltpu.PrefetchScalarGridSpec(
            num_scalar_prefetch=1,
            grid=(SPLIT,),
            in_specs=[full_spec(ids.shape)] + [full_spec(g.shape) for g in extra] + [half_spec(v) for v in halves],
            out_specs=[block(n) for n, _ in outs],
        ),
        out_shape=[jax.ShapeDtypeStruct((SPLIT, GROUP, CAP, n), t) for n, t in outs],
        compiler_params=params(48),
        name="dispatch",
    )(info, ids, *extra, *[v for v, _ in halves])


def split_low(value):
    high = value.astype(BF)
    rest = value - high.astype(F32)
    middle = rest.astype(BF)
    return high, middle, (rest - middle.astype(F32)).astype(BF)


def expert_kernel(info_ref, x_ref, c_ref, meta_ref, full_ref, out_ref, *refs):
    outs, (xt_ref, dt_ref, grad_ref, w_ref, y_ref, db_ref) = refs[:-6], refs[-6:]
    d_refs, y_refs = outs[:GROUP], outs[GROUP:]
    step = pl.program_id(0)
    width = x_ref.shape[-1]
    rows = GROUP * CAP
    x = x_ref[...].reshape(rows, width)

    @pl.when(step == 0)
    def _():
        grad = (c_ref[...].reshape(rows, width).astype(F32) * meta_ref[...].reshape(rows, 128)[:, 0:1]).astype(BF)
        grad_ref[...] = grad
        xt_ref[...] = x.T
        dt_ref[...] = grad.T
        y_ref[...] = jnp.zeros_like(y_ref)
        db_ref[...] = jnp.zeros_like(db_ref)

    columns = w_ref.shape[-1]
    for rank in range(full_ref.shape[0]):
        source = 0
        if full_ref.shape[0] > 1:
            source = (rank & ~3) + jnp.bitwise_xor(info_ref[0], rank & 3)
        w_ref[source] = full_ref[rank]
    w_gate, w_up, w_down = [w_ref[:, part].reshape(width, columns) for part in range(3)]
    grad = grad_ref[...]
    gate = mm(x, w_gate)
    up = mm(x, w_up)
    sigmoid = 1.0 / (1.0 + jnp.exp(-gate))
    silu = gate * sigmoid
    act = (silu * up).astype(BF)
    d_act = mm(grad, w_down)
    d_gate = (d_act * up * sigmoid * (1.0 + gate * (1.0 - sigmoid))).astype(BF)
    d_up = (d_act * silu).astype(BF)
    y_ref[...] += mm_nt(act, w_down)
    db_ref[...] += mm_nt(d_gate, w_gate) + mm_nt(d_up, w_up)
    shape = (out_ref.shape[0], out_ref.shape[2], columns)
    out_ref[:, 0] = mm(xt_ref[...], d_gate).astype(BF).reshape(shape)
    out_ref[:, 1] = mm(xt_ref[...], d_up).astype(BF).reshape(shape)
    out_ref[:, 2] = mm(dt_ref[...], act).astype(BF).reshape(shape)

    @pl.when(step == pl.num_programs(0) - 1)
    def _():
        meta = meta_ref[...].reshape(rows, 128)
        y = y_ref[...]
        share = jnp.sum(c_ref[...].reshape(rows, width).astype(F32) * y, axis=1, keepdims=True) * meta[:, 64:65]
        lane = lax.broadcasted_iota(jnp.int32, (rows, EXTRA), 1)
        high, middle, low = [part.astype(F32) for part in split_low(share)]
        extra = jnp.where(lane == 0, high, jnp.where(lane == 1, middle, jnp.where(lane == 2, low, 0.0))).astype(BF)
        weighted = (y * meta[:, 0:1]).astype(BF)
        back = db_ref[...].astype(BF)
        for slot in range(GROUP):
            span = slice(slot * CAP, (slot + 1) * CAP)
            d_refs[slot][0, :, :width] = back[span]
            d_refs[slot][0, :, width:] = extra[span]
            y_refs[min(slot, 2)][max(slot - 2, 0)] = weighted[span]


def experts(info, rows, cotangents, meta, full, chunk, lead):
    width = rows.shape[-1]
    ranks, _, depth, hidden = full.shape
    tile = 256
    piece = width // lead
    count = GROUP * CAP
    row_spec = lambda n: pl.BlockSpec(
        (1, GROUP, CAP, n), lambda f, info: (chunk, 0, 0, 0), pipeline_mode=pl.Buffered(1)
    )
    shapes = [(1, CAP, width + EXTRA)] * GROUP + [(n, CAP, width) for n in (1, 1, 2)]
    return pl.pallas_call(
        expert_kernel,
        grid_spec=pltpu.PrefetchScalarGridSpec(
            num_scalar_prefetch=1,
            grid=(hidden // tile,),
            in_specs=[row_spec(width), row_spec(width), row_spec(128)]
            + [pl.BlockSpec((ranks, 3, depth, tile), lambda f, info: (0, 0, 0, f))],
            out_specs=[pl.BlockSpec((lead, 3, piece, tile), lambda f, info: (0, 0, 0, f))]
            + [pl.BlockSpec(shape, lambda f, info: (0, 0, 0)) for shape in shapes],
            scratch_shapes=[
                pltpu.VMEM((width, count), BF),
                pltpu.VMEM((width, count), BF),
                pltpu.VMEM((count, width), BF),
                pltpu.VMEM((width // depth, 3, depth, tile), BF),
                pltpu.VMEM((count, width), F32),
                pltpu.VMEM((count, width), F32),
            ],
        ),
        out_shape=[jax.ShapeDtypeStruct((lead, 3, piece, hidden), BF)]
        + [jax.ShapeDtypeStruct(shape, BF) for shape in shapes],
        compiler_params=params(60),
        name="experts",
    )(info, rows, cotangents, meta, full)


def combine_kernel(info_ref, ids_ref, *refs):
    row_refs, outs = refs[: SPLIT * GROUP], refs[SPLIT * GROUP :]
    block = ids_ref.shape[0]
    width = sum(ref.shape[1] for ref in outs)
    column = lax.broadcasted_iota(jnp.int32, (block, CAP), 1)
    one = jnp.broadcast_to(ids_ref[:, 0:1], (block, CAP)) - column
    two = jnp.broadcast_to(ids_ref[:, 1:2], (block, CAP)) - column
    total = jnp.zeros((block, width), F32)
    for index, rows in enumerate(row_refs):
        member, chunk = index // SPLIT, index % SPLIT
        expert = jnp.bitwise_xor(info_ref[0], member) * SPLIT + chunk
        select = jnp.where((one == expert * CAP) | (two == expert * CAP), 1.0, 0.0).astype(BF)
        total = total + mm(select, rows[0])
    first = 0
    for ref in outs:
        ref[...] = total[:, first : first + ref.shape[1]].astype(ref.dtype)
        first += ref.shape[1]


def combine(info, ids, rows, outs):
    length = ids.shape[0]
    width = sum(n for n, _ in outs)
    block = 256

    def row_spec(item):
        return pl.BlockSpec((1, CAP, width), lambda i, info, place=item[1]: (place, 0, 0))

    return pl.pallas_call(
        combine_kernel,
        grid_spec=pltpu.PrefetchScalarGridSpec(
            num_scalar_prefetch=1,
            grid=(length // block,),
            in_specs=[pl.BlockSpec((block, 8), lambda i, info: (i, 0))]
            + [row_spec(item) for item in rows],
            out_specs=[pl.BlockSpec((block, n), lambda i, info: (i, 0)) for n, _ in outs],
        ),
        out_shape=[jax.ShapeDtypeStruct((length, n), t) for n, t in outs],
        compiler_params=params(48),
        name="combine",
    )(info, ids, *[item[0] for item in rows])


def per_device(
    count,
    inputs,
    prev_logits,
    routes,
    lengths,
    cotangent,
    attn_gain,
    w_qkv,
    w_out,
    moe_gain,
    w_router,
    w_resid,
    const_mix,
    const_vec,
    w_experts,
):
    half, width = inputs.shape[1:]
    length = routes.shape[1]
    depth = w_experts.shape[0]
    hidden = w_experts.shape[3]
    heads = w_out.shape[1]
    t_rank = lax.axis_index("tensor")
    d_rank = lax.axis_index("dp")
    bit = lambda n: (d_rank >> n) & 1
    group = d_rank % GROUP
    fast = count == 16 and depth % 16 == 0
    info = jnp.stack([group, bit(2), d_rank]).astype(jnp.int32)
    first_row = t_rank * half
    length_here = lengths[0]

    def in_order(own, other):
        return jnp.where(t_rank == 0, jnp.concatenate([own, other]), jnp.concatenate([other, own]))

    own_in = inputs[0]
    other_in = swap_x(own_in)

    own_routes = routes.transpose(0, 2, 1)
    far_routes = jnp.concatenate([own_routes, swap_dp(own_routes, count, FAR)])

    out_low = w_out.astype(BF)[None]
    attn_shard = jnp.concatenate([w_qkv.transpose(1, 0, 2).astype(BF), out_low, swap_x(out_low)])
    lines = [[i + GROUP * j for j in range(count // GROUP)] for i in range(GROUP)]
    attn_rows, rank_masks = attn_shard[None], [0]
    weights = []

    def double(rows, masks, n):
        got = swap_dp(rows, count, 1 << n)
        return jnp.concatenate([rows, got]), masks + [mask | (1 << n) for mask in masks], got

    def expert_rows(e, got):
        passed = swap_dp(got, count, 1)
        return jnp.concatenate([mine[0][:, e], pair[:, e], got[:1, 0], passed[1:, 0]])

    if fast:
        mine = list(unpack(info, w_experts))
        pair = swap_dp(mine[1], count, 1)
        for n in (3, 2):
            attn_rows, rank_masks, _ = double(attn_rows, rank_masks, n)
        got = swap_dp(mine[2], count, FAR)
        got, attn_rows, mine[3], other_in = meet(got, attn_rows, mine[3], other_in)
        attn_rows, rank_masks, attn_got = double(attn_rows, rank_masks, 1)
        first_quad = expert_rows(0, got)
        weights.append(lax.all_gather(first_quad, "dp", axis=0, tiled=True, axis_index_groups=lines))
        attn_rows, rank_masks, _ = double(attn_rows, rank_masks, 0)
    else:
        attn_rows = lax.all_gather(attn_shard, "dp", axis=1, tiled=True)[None]
        expert_low = w_experts.astype(BF).reshape(depth, GROUP, SPLIT, 3, hidden).transpose(1, 2, 3, 0, 4)
        gathered = pick(lax.all_gather(expert_low, "dp", axis=3, tiled=True), group)
        weights = [gathered[e][None] for e in range(SPLIT)]

    near_routes = swap_dp(far_routes, count, 1)
    all_routes = jnp.stack([far_routes[0], near_routes[0], far_routes[1], near_routes[1]])
    turned = jnp.concatenate([all_routes[:, :, half:], all_routes[:, :, :half]], axis=2)
    ids_rows, ids_own = slot_ids(jnp.where(t_rank == 0, all_routes, turned))
    all_in = in_order(own_in, other_in)
    row_place = first_row + jnp.arange(half, dtype=jnp.int32)
    live = (row_place < length_here)[:, None]
    cot_own = jnp.where(live, cotangent[0], BF(0))
    cot_other = swap_x(after(cot_own, other_in))
    far_cot = [swap_dp(after(cot_own, mine) if fast else cot_own, count, FAR)]
    inv_freq = THETA ** (-jnp.arange(HEAD_DIM // 2, dtype=F32) / (HEAD_DIM // 2))
    angles = jnp.arange(length, dtype=F32)[:, None] * inv_freq[None, :]
    cosine = jnp.tile(jnp.cos(angles), (1, 4))
    sine = jnp.sin(angles)
    sine = jnp.tile(jnp.concatenate([-sine, sine], axis=1), (1, 2))
    bias = jnp.where(jnp.arange(length, dtype=jnp.int32) < length_here, 0.0, NEG)[None, :].astype(F32)

    if fast:
        all_in = after(all_in, first_quad)
    attn, query, key, value, attn_full, out_own, out_other = project(
        info, all_in, attn_gain[None], attn_rows, rank_masks, cosine, sine
    )
    far_cot.append(swap_dp(after(cot_other, query), count, FAR))
    attended, lse = attend(query, key, value, bias)
    att_own = lax.dynamic_slice_in_dim(attended, first_row, half, 0)
    att_send = lax.dynamic_slice_in_dim(attended, half - first_row, half, 0)
    att_other = swap_x(att_send)
    near_cot = chain(after([cot_own, cot_other, far_cot[0]], attended), lambda v: swap_dp(v, count, 1))
    if fast:
        rows = expert_rows(1, after(swap_dp(mine[3], count, FAR), attended))
        weights.append(lax.all_gather(rows, "dp", axis=0, tiled=True, axis_index_groups=lines))
    att_other = after(att_other, near_cot)
    near_cot.append(swap_dp(far_cot[1], count, 1))
    resid_in = own_in.astype(F32)
    resid_mid = resid_in + mm_nt(att_own, out_own) + mm_nt(att_other, out_other)

    inv_two = lax.rsqrt(jnp.mean(resid_mid * resid_mid, axis=-1, keepdims=True) + EPS)
    normed = resid_mid * inv_two * moe_gain
    moe_own = normed.astype(BF)
    moe_other = swap_x(moe_own)
    far_moe = [swap_dp(moe_own, count, FAR)]
    prev_rows = prev_logits[0]
    cot_halves = [cot_own, cot_other] + near_cot[:2] + far_cot + near_cot[2:]
    (cot_rows,) = dispatch(info, ids_rows, [(v, None) for v in after(cot_halves, moe_own)])
    small_w = jnp.concatenate([w_router, const_mix.reshape(4, width).T], axis=1)
    small = jnp.dot(normed, small_w, precision=HIGHEST)
    logits = small[:, :EXPERTS] + jnp.dot(prev_rows, w_resid, precision=HIGHEST)
    route_own = ids_own[:half, 2:4]
    labels = jnp.arange(EXPERTS, dtype=jnp.int32)
    onehot = (route_own[:, :, None] == labels).astype(F32)
    chosen = jnp.sum(onehot * logits[:, None, :], axis=-1)
    top = jnp.max(chosen, axis=-1, keepdims=True)
    gate_weight = jnp.exp(chosen - top)
    gate_weight = gate_weight / jnp.sum(gate_weight, axis=-1, keepdims=True)
    mix = small[:, EXPERTS:].reshape(half, 2, 2)
    mix = jnp.exp(mix - jnp.max(mix, axis=-1, keepdims=True))
    mix = mix / jnp.sum(mix, axis=-1, keepdims=True)
    gate_t = gate_weight.T
    gates = jnp.stack([gate_t, swap_dp(gate_t, count, FAR)])
    gates = jnp.concatenate([gates, swap_x(gates)], axis=2)
    gates = jnp.stack([gates, swap_dp(gates, count, 1)], axis=1).reshape(GROUP, 2, length)

    far_moe.append(swap_dp(after(moe_other, gates), count, FAR))
    near_moe = jnp.stack([moe_own, moe_other, after(far_moe[0], cot_rows)])
    near_moe = swap_dp(near_moe, count, 1)
    is_copy = onehot[:, :, FFN_EXPERTS + 1]
    is_const = onehot[:, :, FFN_EXPERTS + 2 :]
    w_copy = jnp.sum(gate_weight * is_copy, axis=1, keepdims=True)
    w_const = jnp.sum(gate_weight[:, :, None] * is_const, axis=1)
    on_normed = w_copy + jnp.sum(w_const * mix[:, :, 0], axis=1, keepdims=True)
    on_vec = w_const * mix[:, :, 1]
    grad_top = cot_own.astype(F32)
    dot_normed = jnp.sum(grad_top * normed, axis=1, keepdims=True)
    dot_vec = jnp.stack([jnp.sum(grad_top * const_vec[j], axis=1) for j in range(2)], axis=1)
    const_gate = mix[:, :, 0] * dot_normed + mix[:, :, 1] * dot_vec
    special = is_copy * dot_normed + jnp.sum(is_const * const_gate[:, None, :], axis=-1)
    d_mix = jnp.stack([w_const * dot_normed, w_const * dot_vec], axis=-1)
    d_mix = mix * (d_mix - jnp.sum(mix * d_mix, axis=-1, keepdims=True))
    special = special[:, 0] - special[:, 1]
    gate_product = gate_weight[:, 0] * gate_weight[:, 1]
    d_mix = d_mix.reshape(half, 4)
    far_moe[1], special, gate_product, d_mix, on_normed, on_vec = meet(
        far_moe[1], special, gate_product, d_mix, on_normed, on_vec
    )
    near_last = swap_dp(far_moe[1], count, 1)
    moe_halves = [(moe_own, None), (moe_other, None), (near_moe, 0), (near_moe, 1)]
    moe_halves += [(far_moe[0], None), (far_moe[1], None), (near_moe, 2), (near_last, None)]
    moe_rows, meta = dispatch(info, ids_rows, moe_halves, gates)
    rows_in = moe_rows
    lead = count // GROUP if fast else 1
    grads, d_sent, y_sent = [], [], []
    for e in range(SPLIT):
        blocks, *routed = experts(info, rows_in, cot_rows, meta, weights[e], e, lead)
        d_sent.append(routed[:GROUP])
        y_sent.append(routed[GROUP:])
        rows_in = after(rows_in, routed[0])
        if fast:
            blocks = lax.psum_scatter(blocks, "dp", scatter_dimension=0, tiled=False, axis_index_groups=lines)
        else:
            blocks = blocks.reshape(3, count, depth, hidden).transpose(1, 0, 2, 3)
            blocks = scatter_bits(blocks, range(2, count.bit_length() - 1), d_rank, count)
            blocks = blocks.transpose(1, 0, 2, 3)
        grads.append(blocks.reshape(3, GROUP, depth, hidden))
    first_rows = [(d_sent[0][0], 0)] + share_all(d_sent[0][1:], count)
    last_sent = after(d_sent[1][1:], [r for r, _ in first_rows[1:]])
    last_rows = [(d_sent[1][0], 0)] + share_all(last_sent, count)
    d_rows = [r for pair in zip(first_rows, last_rows) for r in pair]
    d_low, share_other = combine(info, ids_own[half:], d_rows, [(width, BF), (EXTRA, F32)])
    d_got = swap_x(d_low)
    share_got = swap_x(jnp.sum(share_other[:, :3], axis=1))
    d_own, share_own = combine(info, after(ids_own[:half], d_low), d_rows, [(width, F32), (EXTRA, F32)])
    y_rows = [[(y[0], 0)] + share_far(after(y[1], d_own), after(y[2], d_own), count) for y in y_sent]
    y_rows = [r for pair in zip(*y_rows) for r in pair]
    d_tokens = d_own + d_got.astype(F32)
    share = jnp.sum(share_own[:, :3], axis=1) + share_got

    d_first = gate_product * (share + special)
    d_logits = d_first[:, None] * (onehot[:, 0] - onehot[:, 1])
    d_small = jnp.concatenate([d_logits, d_mix], axis=1)
    d_normed = jnp.dot(d_small, small_w.T, precision=HIGHEST) + on_normed * grad_top + d_tokens
    grad_moe_gain = jnp.sum(d_normed * resid_mid * inv_two, axis=0)
    scaled = moe_gain * d_normed
    d_resid = (
        grad_top
        + inv_two * scaled
        - resid_mid * (inv_two * inv_two * inv_two) * jnp.mean(scaled * resid_mid, axis=-1, keepdims=True)
    )

    def final_pieces(blocks):
        blocks = [
            lax.dynamic_index_in_dim(blocks, jnp.bitwise_xor(group, m), 1, keepdims=False)[None] for m in range(GROUP)
        ]
        return [(blocks[0], 0)] + share_far(blocks[1], jnp.concatenate(blocks[2:]), count)

    d_mixed = d_resid.astype(BF)
    d_att_low = mm(d_mixed, out_other).astype(BF)
    d_att_got = swap_x(d_att_low)
    d_late, on_vec_late = after((d_small, on_vec), d_att_low)
    grad_prev = jnp.dot(d_late[:, :EXPERTS], w_resid.T, precision=HIGHEST)
    grad_resid = jnp.dot(prev_rows.T, d_late[:, :EXPERTS], precision=HIGHEST)
    grad_small = jnp.dot(d_late.T, normed, precision=HIGHEST)
    grad_const_vec = jnp.dot(on_vec_late.T, grad_top, precision=HIGHEST)
    d_att_own = mm(after(d_mixed, d_att_low), out_own).astype(BF)
    attn_late = after(attn, d_att_low)
    first_pieces = final_pieces(after(grads[0], d_att_low))
    d_att_other = d_att_got
    d_attended = in_order(d_att_own, d_att_other)
    d_mixed_other = swap_x(after(d_mixed, d_att_got))
    d_qkv = attend_back(query, key, value, d_attended, lse, bias, cosine, sine)
    d_mixed_all = in_order(d_mixed, after(d_mixed_other, d_qkv))
    grad_out = mm_tn(d_mixed_all, attended)
    grad_qkv = jnp.stack([mm_tn(attn_late, d_qkv[k]) for k in range(3)] + [grad_out])
    blocks = grad_qkv.astype(BF).reshape(4, count, depth, heads).transpose(1, 0, 2, 3)
    bits = list(range(count.bit_length() - 1))[::-1]
    blocks, *arrived = meet(blocks, *[p for p, _ in first_pieces])
    first_pieces = [(p, place) for p, (_, place) in zip(arrived, first_pieces)]
    stage = halve(blocks, bits, 0, d_rank, count)
    bits.remove(0)
    d_attn = sum(mm_nt(d_qkv[k], attn_full[k]) for k in range(3))
    values = all_in.astype(F32)
    inv_all = lax.rsqrt(jnp.mean(values * values, axis=-1, keepdims=True) + EPS)
    grad_attn_gain = jnp.sum(d_attn * values * inv_all, axis=0)
    d_attn_own = lax.dynamic_slice_in_dim(d_attn, first_row, half, 0)
    d_attn_other = lax.dynamic_slice_in_dim(d_attn, half - first_row, half, 0).astype(BF)
    d_attn_got = swap_x(d_attn_other)
    y_ids = after(ids_own, d_attn_other)
    (y_low,) = combine(info, y_ids[half:], y_rows, [(width, BF)])
    y_got = swap_x(y_low)
    (y_own,) = combine(info, after(y_ids[:half], y_low), y_rows, [(width, F32)])
    inv_one = lax.rsqrt(jnp.mean(resid_in * resid_in, axis=-1, keepdims=True) + EPS)
    early = jnp.concatenate(
        [
            grad_small.reshape(-1),
            grad_const_vec.reshape(-1),
            grad_moe_gain,
            jnp.pad(grad_resid.reshape(-1), (0, 112)),
            grad_attn_gain,
        ]
    )
    early = early.reshape(-1, 128)
    last_grad = grads[1]
    stage, early = meet(stage, early)
    hops = [[0, 1, 2], [3], list(range(4, count.bit_length() - 1))] + [[]] * count
    for n in bits[::-1]:
        stage = halve(stage, bits, n, d_rank, count)
        bits.remove(n)
        for hop in hops.pop(0):
            early = early + swap_dp(early, count, 1 << hop)
        stage, early = meet(stage, early)
        if n == 2:
            stage, d_attn_got, last_grad = meet(stage, d_attn_got, last_grad)
        if n == 3:
            stage, y_got = meet(stage, y_got)
    early = early + swap_x(early)
    grad_attn = stage[0].astype(F32)
    d_attn_own = d_attn_own + d_attn_got.astype(F32)
    scaled = attn_gain * d_attn_own
    grad_inputs = (
        d_resid
        + inv_one * scaled
        - resid_in * (inv_one * inv_one * inv_one) * jnp.mean(scaled * resid_in, axis=-1, keepdims=True)
    )


    pieces = first_pieces + final_pieces(last_grad)
    y_got = after(y_got, pieces[GROUP + 2][0])
    block_out = resid_mid + y_own + y_got.astype(F32) + on_normed * normed
    block_out = block_out + on_vec[:, 0:1] * const_vec[0] + on_vec[:, 1:2] * const_vec[1]
    block_out = block_out.astype(BF)
    if fast:
        grad_experts = pack(info, pieces)
    else:
        table = jnp.stack([entry(p).astype(F32) for p in pieces]).reshape(SPLIT, GROUP, 3, depth, hidden)
        table = jnp.take(table, jnp.bitwise_xor(jnp.arange(GROUP), group), axis=1)
        grad_experts = table.transpose(3, 1, 0, 2, 4).reshape(depth, FFN_EXPERTS, 3, hidden)

    early = early.reshape(-1)
    grad_attn_gain = early[-width:]
    sizes = [EXPERTS * width, 4 * width, 2 * width, width]
    cuts = [sum(sizes[: i + 1]) for i in range(4)]
    grad_router = early[: cuts[0]].reshape(EXPERTS, width).T
    grad_const_mix = early[cuts[0] : cuts[1]].reshape(2, 2, width)
    grad_const_vec = early[cuts[1] : cuts[2]].reshape(2, width)
    grad_moe_gain = early[cuts[2] : cuts[3]]
    grad_resid = early[cuts[3] : cuts[3] + EXPERTS * EXPERTS].reshape(EXPERTS, EXPERTS)
    return (
        block_out[None],
        grad_inputs.astype(BF)[None],
        grad_prev[None],
        grad_attn_gain,
        grad_attn[:3].transpose(1, 0, 2),
        grad_attn[3],
        grad_moe_gain,
        grad_router,
        grad_resid,
        grad_const_mix,
        grad_const_vec,
        grad_experts,
    )


def solution(mesh):
    placed = (
        P("dp", "tensor", None),
        P("dp", "tensor", None),
        P("dp", None, None),
        P("dp"),
        P("dp", "tensor", None),
        P(),
        P("dp", None, "tensor"),
        P("dp", "tensor"),
        P(),
        P(),
        P(),
        P(),
        P(),
        P("dp", None, None, "tensor"),
    )
    return jax.shard_map(
        functools.partial(per_device, mesh.shape["dp"]),
        mesh=mesh,
        in_specs=placed,
        out_specs=(
            P("dp", "tensor", None),
            P("dp", "tensor", None),
            P("dp", "tensor", None),
            P(),
            P("dp", None, "tensor"),
            P("dp", "tensor"),
            P(),
            P(),
            P(),
            P(),
            P(),
            P("dp", None, None, "tensor"),
        ),
        check_vma=False,
    )
```
